32 devices in a mesh: chan: 16 (over z, y, x), cyl: 2 (over core).
Axes of the slice: x: 2, y: 2, z: 4, core: 2. Of those that a mesh axis runs over, the one named last changes fastest.
Arguments:
- volts: bfloat16 [1024, 4, 2, 64, 512], P('chan', 'cyl'), may hold values from -6 to 6
- gain_exponents: int32 [1024, 4], P('chan', 'cyl'), may hold values from -1 to 1
Outputs:
- intensity: float32 [4, 256, 2, 16384], P('cyl', 'chan')
The draws below stay inside these ranges and needn't reach their ends.
All inputs are finite; a program needn't handle non-finite values.
Results may differ from the reference program's by a relative error of at most 0.0042.
Values may be sent and summed in bfloat16 or wider, within the bound.
A program may use at most 256 MiB of HBM per device.

```python
import math
import jax
import jax.numpy as jnp
from jax import lax

F = 1024
CYLS = 4
FEEDS = 256
POLS = 2
UP = 16
TIME = 64
FRAMES = 2
SUMS = 2
N_CYL = 2


def touch_ends(array, rng, smallest, high):
    shape = array.shape
    place = [jax.random.randint(jax.random.fold_in(rng, axis), (), 0, shape[axis]) for axis in range(len(shape))]
    array = array.at[tuple(place)].set(smallest)
    longest = shape.index(max(shape))
    place[longest] = (place[longest] + 1) % shape[longest]
    return array.at[tuple(place)].set(high)


def steps_of(own_key, extent, shards, low, largest):
    def one(axis_at, shards_of):
        heights = jax.random.uniform(jax.random.fold_in(jax.random.fold_in(own_key, 6), axis_at), (shards_of,), jnp.float32, low / len(shards), largest / len(shards))
        return jnp.repeat(jnp.exp(heights), extent[axis_at] // shards_of).reshape((-1,) + (1,) * (len(extent) - axis_at - 1))

    gain = one(*shards[0])
    for cut in shards[1:]:
        gain = gain * one(*cut)
    return gain


def centred(rng, shape, deviation, reach, cuts=(), kind=jnp.bfloat16):
    drawn = deviation * jax.random.normal(rng, shape, jnp.float32)
    if cuts:
        drawn = drawn * steps_of(rng, shape, cuts, -0.22, 0.18)
    return jnp.clip(drawn, -reach, reach).astype(kind)


def setup_inputs(seed: int = 0) -> dict:
    key_list = jax.random.split(jax.random.key(seed), 3)
    return {
        "volts": centred(key_list[0], (F, CYLS, POLS, TIME, 2 * FEEDS), 1.0, 6.0, ((0, 16), (1, 2))),
        "gain_exponents": touch_ends(jax.random.randint(key_list[1], (F, CYLS), -1, 2), jax.random.fold_in(key_list[1], 1), -1, 1).astype(jnp.int32),
    }


def ns_table(feeds):
    index = jnp.arange(feeds, dtype=jnp.int32)
    product = index[:, None] * (index[None, :] - feeds // 2) % feeds
    theta = product.astype(jnp.float32) * (2.0 * math.pi / feeds)
    cosine = jnp.cos(theta) / math.sqrt(feeds)
    sine = jnp.sin(theta) / math.sqrt(feeds)
    upper = jnp.stack([cosine, -sine], axis=-1).reshape(feeds, 2 * feeds)
    lower = jnp.stack([sine, cosine], axis=-1).reshape(feeds, 2 * feeds)
    return jnp.concatenate([upper, lower], axis=0).astype(jnp.bfloat16)

def up_table(up):
    index = jnp.arange(up, dtype=jnp.int32)
    product = index[:, None] * index[None, :] % up
    theta = product.astype(jnp.float32) * (2.0 * math.pi / up)
    cosine = jnp.cos(theta) / math.sqrt(up)
    sine = jnp.sin(theta) / math.sqrt(up)
    first = jnp.stack([cosine, -sine], axis=1)
    second = jnp.stack([sine, cosine], axis=1)
    return jnp.stack([first, second], axis=0).astype(jnp.bfloat16)

def ew_weights(beam_index, cyl_index, cyls):
    phase = 2.0 * math.pi * cyl_index[None, :].astype(jnp.float32) * (beam_index[:, None].astype(jnp.float32) - (cyls - 1) / 2.0) / cyls
    return (jnp.cos(phase) / 2.0, -jnp.sin(phase) / 2.0)

def combine(real_part, imag_part, w_real, w_imag):
    high = lax.Precision.HIGHEST
    pr = jnp.einsum('ec,ngcpt->ngept', w_real, real_part, precision=high) - jnp.einsum('ec,ngcpt->ngept', w_imag, imag_part, precision=high)
    pi = jnp.einsum('ec,ngcpt->ngept', w_real, imag_part, precision=high) + jnp.einsum('ec,ngcpt->ngept', w_imag, real_part, precision=high)
    return jnp.stack([pr, pi], axis=1)

def reference(volts, gain_exponents):
    group = 8 if F % 8 == 0 else 1
    table = ns_table(FEEDS).astype(jnp.float32)
    upper_table = up_table(UP).astype(jnp.float32)
    per_group = CYLS // N_CYL
    beam_index = jnp.arange(CYLS, dtype=jnp.int32)

    def one_block(pieces):
        block, exps = pieces
        ns_beams = lax.dot_general(table, block.astype(jnp.float32), (((0,), (4,)), ((), ())), precision=lax.Precision.HIGHEST)
        ns_beams = ns_beams.reshape(FEEDS, 2, group, CYLS, POLS, TIME)
        beams = None
        for part in range(N_CYL):
            cyl_index = part * per_group + jnp.arange(per_group, dtype=jnp.int32)
            w_real, w_imag = ew_weights(beam_index, cyl_index, CYLS)
            lo = part * per_group
            piece = combine(ns_beams[:, 0, :, lo:lo + per_group], ns_beams[:, 1, :, lo:lo + per_group], w_real, w_imag)
            piece = piece.astype(jnp.bfloat16).astype(jnp.float32)
            beams = piece if beams is None else beams + piece
        gains = jnp.exp2(exps.astype(jnp.float32))
        coded = (beams * gains[None, None, :, :, None, None]).astype(jnp.bfloat16)
        blocks = TIME // UP
        shaped = coded.astype(jnp.float32).reshape(FEEDS, 2, group, CYLS, POLS, blocks, UP)
        spectra = jnp.einsum('nrgepbk,rksm->ngepbsm', shaped, upper_table, precision=lax.Precision.HIGHEST)
        power = lax.optimization_barrier(jnp.sum(spectra * spectra, axis=(3, 5)))
        power = power.reshape(FEEDS, group, CYLS, FRAMES, SUMS, UP).sum(axis=4) / (POLS * SUMS)
        return jnp.transpose(power, (2, 0, 3, 1, 4)).reshape(CYLS, FEEDS, FRAMES, group * UP)
    shaped_volts = volts.reshape(F // group, group, CYLS, POLS, TIME, 2 * FEEDS)
    shaped_exps = gain_exponents.reshape(F // group, group, CYLS)
    result = lax.map(one_block, (shaped_volts, shaped_exps))
    result = jnp.transpose(result, (1, 2, 3, 0, 4))
    return result.reshape(CYLS, FEEDS, FRAMES, F * UP)
```

```python
import functools
import math

import jax
import jax.numpy as jnp
import ml_dtypes
import numpy as np
from jax import lax
from jax.experimental import pallas as pl
from jax.experimental.pallas import tpu as pltpu
from jax.sharding import PartitionSpec as P

UP = 16
FRAMES = 2


def ns_rows(feeds):
    index = np.arange(feeds)
    theta = (index[None, :] * (index[:, None] - feeds // 2) % feeds) * (2.0 * math.pi / feeds)
    cosine = np.cos(theta) / math.sqrt(feeds)
    sine = np.sin(theta) / math.sqrt(feeds)
    table = np.concatenate(
        [np.concatenate([cosine, sine], axis=1), np.concatenate([-sine, cosine], axis=1)], axis=0
    )
    return table.astype(ml_dtypes.bfloat16)


def fine_rows(cyls, n_cyl, up):
    index = np.arange(up)
    theta = (index[:, None] * index[None, :] % up) * (2.0 * math.pi / up)
    rounded = lambda x: (x / math.sqrt(up)).astype(ml_dtypes.bfloat16).astype(np.float64)
    fine = rounded(np.cos(theta)) - 1j * rounded(np.sin(theta))
    cyl = np.arange(cyls)
    phase = 2.0 * math.pi * cyl[None, :] * (cyl[:, None] - (cyls - 1) / 2.0) / cyls
    weight = np.exp(-1j * phase) / 2.0
    both = np.einsum("ec,km->emck", weight, fine)
    parts = np.stack(
        [np.stack([both.real, -both.imag], axis=3), np.stack([both.imag, both.real], axis=3)], axis=0
    )
    per = cyls // n_cyl
    tables = []
    for rank in range(n_cyl):
        order = [((rank - d) % n_cyl) * per + c for d in range(n_cyl) for c in range(per)]
        tables.append(parts[:, :, :, order].reshape(2 * cyls * up, cyls * 2 * up))
    return np.stack(tables).astype(ml_dtypes.bfloat16)


def beam_kernel(
    cyls, n_cyl, volts_ref, fine_ref, ns_ref, gain_ref, out_ref,
    mid_ref, held_ref, own_sem, send_sem, recv_sem,
):
    step = pl.program_id(0)
    steps = pl.num_programs(0)
    _, _, group, per, pols, times, inputs = held_ref.shape
    feeds = inputs // 2
    blocks = times // UP
    sums = blocks // FRAMES
    rank = lax.axis_index("cyl")

    def own_copy(g):
        rows = pl.ds((rank * steps + g) * group, group)
        return pltpu.make_async_copy(volts_ref.at[rows], held_ref.at[0, g], own_sem.at[g])

    def far_copy(d, g):
        to = lax.rem(rank + d, n_cyl)
        rows = pl.ds((to * steps + g) * group, group)
        return pltpu.make_async_remote_copy(
            src_ref=volts_ref.at[rows],
            dst_ref=held_ref.at[d, g],
            send_sem=send_sem.at[d, g],
            recv_sem=recv_sem.at[d, g],
            device_id={"cyl": to},
            device_id_type=pl.DeviceIdType.MESH,
        )

    @pl.when(step == 0)
    def _():
        own_copy(0).start()
        barrier = pltpu.get_barrier_semaphore()
        for d in range(1, n_cyl):
            pl.semaphore_signal(
                barrier, inc=1, device_id={"cyl": lax.rem(rank + d, n_cyl)},
                device_id_type=pl.DeviceIdType.MESH,
            )
        pl.semaphore_wait(barrier, n_cyl - 1)

        def start(g, carry):
            for d in range(1, n_cyl):
                far_copy(d, g).start()

            @pl.when(g > 0)
            def _():
                own_copy(g).start()

            return carry

        lax.fori_loop(0, steps, start, 0)

    own_copy(step).wait()
    for d in range(1, n_cyl):
        far_copy(d, step).wait()
    volt_refs = [held_ref.at[d, step] for d in range(n_cyl)]
    fine = fine_ref[rank]

    def one_chan(ch, carry):
        for p in range(pols):
            for j in range(blocks):
                rows = jnp.concatenate(
                    [
                        ref[ch, c, p, j * UP : (j + 1) * UP, r * feeds : (r + 1) * feeds]
                        for ref in volt_refs
                        for c in range(per)
                        for r in range(2)
                    ],
                    axis=0,
                )
                got = jnp.dot(fine, rows, preferred_element_type=jnp.float32).astype(jnp.bfloat16)
                for s in range(2):
                    for e in range(cyls):
                        at = (s * cyls + e) * UP
                        mid_ref[p * blocks + j, e, ch, :, s * feeds : (s + 1) * feeds] = got[at : at + UP]
        return carry

    lax.fori_loop(0, group, one_chan, 0)
    wide = group * UP
    pair = 2 if cyls % 2 == 0 else 1
    ns = ns_ref[...]
    for q in range(FRAMES):
        for e in range(0, cyls, pair):
            total = None
            for p in range(pols):
                for j in range(q * sums, (q + 1) * sums):
                    block = mid_ref[p * blocks + j, e : e + pair].reshape(pair * wide, inputs)
                    spectra = lax.dot_general(
                        ns, block, (((1,), (1,)), ((), ())), preferred_element_type=jnp.float32
                    )
                    squared = spectra * spectra
                    power = squared[:feeds] + squared[feeds:]
                    total = power if total is None else total + power
            for i in range(pair):
                scaled = total[:, i * wide : (i + 1) * wide] * gain_ref[0, e + i : e + i + 1, :]
                out_ref[0, e + i, q] = scaled.astype(jnp.bfloat16)


def spread_kernel(in_ref, out_ref):
    sources, _, frames, steps, near, wide = in_ref.shape

    def one(source, carry):
        at = pl.multiple_of(source * (steps * wide), 128)
        for g in range(steps):
            rows = [in_ref[source, 0, q, g].astype(jnp.float32) for q in range(frames)]
            out_ref[0, :, :, pl.ds(at + g * wide, wide)] = jnp.stack(rows, axis=1)
        return carry

    lax.fori_loop(0, sources, one, 0)


def spread(power):
    sources, per, frames, steps, near, wide = power.shape
    lanes = sources * steps * wide
    return pl.pallas_call(
        spread_kernel,
        out_shape=jax.ShapeDtypeStruct((per, near, frames, lanes), jnp.float32),
        grid=(per,),
        in_specs=[pl.BlockSpec((sources, 1, frames, steps, near, wide), lambda e: (0, e, 0, 0, 0, 0))],
        out_specs=pl.BlockSpec((1, near, frames, lanes), lambda e: (e, 0, 0, 0)),
        compiler_params=pltpu.CompilerParams(dimension_semantics=("arbitrary",)),
        name="spread",
    )(power)


def half_rows(feeds):
    half = feeds // 2
    table = np.asarray(ns_rows(feeds)).reshape(2, half, 2, 2, feeds)[..., :half]
    return np.transpose(table, (2, 0, 1, 3, 4)).reshape(2, feeds, feeds)


def fused_kernel(
    n_chan, n_cyl, volts_ref, gains_ref, fine_hbm, ns_hbm, out_ref,
    held_ref, mid_ref, send_ref, recv_ref, exps_ref, scale_ref, fine_ref, ns_ref,
    own_sem, volt_send_sem, volt_recv_sem, exp_sem, exp_send_sem, exp_recv_sem, table_sem,
    send_sem, recv_sem,
):
    chip = lax.axis_index("chan")
    rank = lax.axis_index("cyl")
    me = chip * n_cyl + rank
    devices = n_chan * n_cyl
    _, stages, group, per, pols, times, inputs = held_ref.shape
    pieces = volt_recv_sem.shape[2]
    piece = group // pieces
    blocks = times // UP
    feeds = inputs // 2
    half = feeds // 2
    cyls = per * n_cyl
    steps = stages // FRAMES
    own = steps * group
    wide = group * UP
    near = feeds // n_chan

    def volt_rows(to, s, first, count):
        at = to * own + (s // FRAMES) * group + first
        time = pl.multiple_of((s % FRAMES) * times, times)
        return volts_ref.at[pl.ds(at, count), :, :, pl.ds(time, times), :]

    def own_copy(s):
        return pltpu.make_async_copy(volt_rows(rank, s, 0, group), held_ref.at[rank, s], own_sem.at[s])

    def far_copy(d, s, i):
        to = lax.rem(rank + d, n_cyl)
        return pltpu.make_async_remote_copy(
            src_ref=volt_rows(to, s, i * piece, piece),
            dst_ref=held_ref.at[rank, s, pl.ds(i * piece, piece)],
            send_sem=volt_send_sem.at[d],
            recv_sem=volt_recv_sem.at[d, s, i],
            device_id={"cyl": to},
            device_id_type=pl.DeviceIdType.MESH,
        )

    def far_arrived(d, s, i):
        source = lax.rem(rank + n_cyl - d, n_cyl)
        there = held_ref.at[source, s, pl.ds(i * piece, piece)]
        return pltpu.make_async_copy(there, there, volt_recv_sem.at[d, s, i])

    def exp_copy(d):
        return pltpu.make_async_remote_copy(
            src_ref=gains_ref,
            dst_ref=exps_ref.at[rank],
            send_sem=exp_send_sem.at[d],
            recv_sem=exp_recv_sem.at[d],
            device_id={"cyl": lax.rem(rank + d, n_cyl)},
            device_id_type=pl.DeviceIdType.MESH,
        )

    fine_copy = pltpu.make_async_copy(fine_hbm, fine_ref, table_sem.at[0])
    ns_copy = pltpu.make_async_copy(ns_hbm, ns_ref, table_sem.at[1])
    own_exps = pltpu.make_async_copy(gains_ref, exps_ref.at[rank], exp_sem)

    barrier = pltpu.get_barrier_semaphore()

    def greet(i, carry):
        to = lax.rem(me + i, devices)
        pl.semaphore_signal(
            barrier, inc=1, device_id={"chan": to // n_cyl, "cyl": lax.rem(to, n_cyl)},
            device_id_type=pl.DeviceIdType.MESH,
        )
        return carry

    lax.fori_loop(1, devices, greet, 0)
    fine_copy.start()
    own_exps.start()
    own_copy(0).start()
    ns_copy.start()

    def start_own(s, carry):
        own_copy(s).start()
        return carry

    lax.fori_loop(1, stages, start_own, 0)
    pl.semaphore_wait(barrier, devices - 1)
    for d in range(1, n_cyl):
        exp_copy(d).start()

    def start_far(n, carry):
        for d in range(1, n_cyl):
            far_copy(d, n // pieces, n % pieces).start()
        return carry

    lax.fori_loop(0, stages * pieces, start_far, 0)
    fine_copy.wait()
    own_exps.wait()
    ns_copy.wait()
    for d in range(1, n_cyl):
        exp_copy(d).wait()
    chans = exps_ref.shape[2]
    lane = lax.broadcasted_iota(jnp.int32, (chans, own * UP), 1) // UP + rank * own
    pick = (lane == lax.broadcasted_iota(jnp.int32, (chans, own * UP), 0)).astype(jnp.float32)
    exps = jnp.concatenate([exps_ref[i] for i in range(n_cyl)], axis=0).astype(jnp.float32)
    spread_exps = jnp.dot(exps, pick, preferred_element_type=jnp.float32)
    scale = jnp.exp2(2.0 * spread_exps) / (pols * blocks)
    for g in range(steps):
        scale_ref[g] = scale[:, g * wide : (g + 1) * wide]

    def one_stage(s, carry):
        own_copy(s).wait()
        fine = fine_ref[...]

        def one_piece(i, inner):
            for d in range(1, n_cyl):
                far_arrived(d, s, i).wait()
            for c0 in range(piece):
                ch = i * piece + c0
                for p in range(pols):
                    for j in range(blocks):
                        rows = jnp.concatenate(
                            [
                                held_ref[o, s, ch, c, p, j * UP : (j + 1) * UP, r * feeds : (r + 1) * feeds]
                                for o in range(n_cyl)
                                for c in range(per)
                                for r in range(2)
                            ],
                            axis=0,
                        )
                        got = jnp.dot(fine, rows, preferred_element_type=jnp.float32)
                        low, high = got[:, :half], got[:, half:]
                        both = ((low + high).astype(jnp.bfloat16), (low - high).astype(jnp.bfloat16))
                        for odd in range(2):
                            for r in range(2):
                                for e in range(cyls):
                                    at = (r * cyls + e) * UP
                                    mid_ref[p * blocks + j, odd, e, ch, :, r * half : (r + 1) * half] = (
                                        both[odd][at : at + UP]
                                    )
            return inner

        lax.fori_loop(0, pieces, one_piece, 0)
        for owner in range(n_cyl):
            parts = []
            for odd in range(2):
                ns = ns_ref[odd]
                total = None
                for b in range(pols * blocks):
                    block = mid_ref[b, odd, owner * per : (owner + 1) * per].reshape(per * wide, feeds)
                    spectra = lax.dot_general(
                        ns, block, (((1,), (1,)), ((), ())), preferred_element_type=jnp.float32
                    )
                    squared = spectra * spectra
                    power = squared[:half] + squared[half:]
                    total = power if total is None else total + power
                parts.append(total)
            for e in range(per):
                factor = scale_ref[s // FRAMES, owner * per + e : owner * per + e + 1, :]
                scaled = [
                    (part[:, e * wide : (e + 1) * wide] * factor).reshape(n_chan, near // 2, wide)
                    for part in parts
                ]
                send_ref[s, owner, :, e] = jnp.concatenate(scaled, axis=1).astype(jnp.bfloat16)

            def send(i, inner):
                to = lax.rem(chip + n_chan // 2 + i, n_chan)
                here = jnp.logical_and(to == chip, rank == owner)

                @pl.when(here)
                def _():
                    pltpu.make_async_copy(
                        send_ref.at[s, owner, to], recv_ref.at[s, me], recv_sem.at[s]
                    ).start()

                @pl.when(jnp.logical_not(here))
                def _():
                    pltpu.make_async_remote_copy(
                        src_ref=send_ref.at[s, owner, to],
                        dst_ref=recv_ref.at[s, me],
                        send_sem=send_sem,
                        recv_sem=recv_sem.at[s],
                        device_id={"chan": to, "cyl": owner},
                        device_id_type=pl.DeviceIdType.MESH,
                    ).start()

                return inner

            lax.fori_loop(0, n_chan, send, 0)
        return carry

    lax.fori_loop(0, stages, one_stage, 0)

    depth = devices * stages

    def spread_stage(s, carry):
        pltpu.make_async_copy(recv_ref.at[s], recv_ref.at[s], recv_sem.at[s]).wait()

        def one(source, inner):
            row = (source * steps + s // FRAMES) * FRAMES + s % FRAMES
            for e in range(per):
                tile = recv_ref[s, source, e].astype(jnp.float32)
                for odd in range(2):
                    at = (e * near + odd) * depth + row
                    out_ref[pl.ds(at, near // 2, 2 * depth), :] = tile[odd * (near // 2) : (odd + 1) * (near // 2)]
            return inner

        lax.fori_loop(0, devices, one, 0)
        return carry

    lax.fori_loop(0, stages, spread_stage, 0)
    sent = recv_ref.at[:, : devices - 1]
    pltpu.make_async_copy(sent, sent, send_sem).wait()
    for d in range(1, n_cyl):
        pltpu.make_async_copy(held_ref.at[0], held_ref.at[0], volt_send_sem.at[d]).wait()


def fused(n_chan, n_cyl, volts, gain_exponents):
    chans, per, pols, times, inputs = volts.shape
    feeds = inputs // 2
    cyls = per * n_cyl
    own = chans // n_cyl
    group = 128 // UP
    steps = own // group
    stages = steps * FRAMES
    span = times // FRAMES
    blocks = span // UP
    near = feeds // n_chan
    devices = n_chan * n_cyl
    wide = group * UP
    pieces = 4
    fine = jnp.asarray(fine_rows(cyls, 1, UP)[0])
    ns = jnp.asarray(half_rows(feeds))
    dma = pltpu.SemaphoreType.DMA
    out = pl.pallas_call(
        functools.partial(fused_kernel, n_chan, n_cyl),
        out_shape=jax.ShapeDtypeStruct((per * near * devices * stages, wide), jnp.float32),
        in_specs=[pl.BlockSpec(memory_space=pl.ANY)] * 4,
        out_specs=pl.BlockSpec(memory_space=pltpu.VMEM),
        scratch_shapes=[
            pltpu.VMEM((n_cyl, stages, group, per, pols, span, inputs), jnp.bfloat16),
            pltpu.VMEM((pols * blocks, 2, cyls, group, UP, feeds), jnp.bfloat16),
            pltpu.VMEM((stages, n_cyl, n_chan, per, near, wide), jnp.bfloat16),
            pltpu.VMEM((stages, devices, per, near, wide), jnp.bfloat16),
            pltpu.VMEM((n_cyl, per, chans), jnp.int32),
            pltpu.VMEM((steps, cyls, wide), jnp.float32),
            pltpu.VMEM(fine.shape, jnp.bfloat16),
            pltpu.VMEM(ns.shape, jnp.bfloat16),
            dma((stages,)),
            dma((n_cyl,)),
            dma((n_cyl, stages, pieces)),
            dma,
            dma((n_cyl,)),
            dma((n_cyl,)),
            dma((2,)),
            dma,
            dma((stages,)),
        ],
        compiler_params=pltpu.CompilerParams(
            collective_id=0, has_side_effects=True, vmem_limit_bytes=48 * 1024 * 1024
        ),
        name="fused",
    )(volts, gain_exponents.T, fine, ns)
    out = out.reshape(per, near, devices * steps, FRAMES, wide)
    return jnp.transpose(out, (0, 1, 3, 2, 4)).reshape(per, near, FRAMES, -1)


def fits(n_chan, n_cyl, volts):
    chans, per, pols, times, inputs = volts.shape
    own = chans // n_cyl
    feeds = inputs // 2
    return (
        own % (128 // UP) == 0
        and feeds % (16 * n_chan) == 0
        and feeds % 256 == 0
        and times % (FRAMES * UP) == 0
    )


def local(n_chan, n_cyl, volts, gain_exponents):
    chans, per, pols, times, inputs = volts.shape
    feeds = inputs // 2
    cyls = per * n_cyl
    own = chans // n_cyl
    group = math.gcd(8, own)
    steps = own // group
    wide = group * UP
    blocks = times // UP
    rank = lax.axis_index("cyl")
    gains = [lax.dynamic_slice_in_dim(gain_exponents, rank * own, own, 0)]
    for d in range(1, n_cyl):
        ring = [(k, (k + d) % n_cyl) for k in range(n_cyl)]
        to = (rank + d) % n_cyl
        gains.append(
            lax.ppermute(lax.dynamic_slice_in_dim(gain_exponents, to * own, own, 0), "cyl", ring)
        )
    stacked = jnp.stack(gains)
    order = (rank - jnp.arange(n_cyl, dtype=jnp.int32)) % n_cyl
    exps = jnp.take(stacked, order, axis=0)
    exps = jnp.transpose(exps, (0, 2, 1)).reshape(cyls, steps, group)
    scale = jnp.exp2(2.0 * exps.astype(jnp.float32)) / (pols * (blocks // FRAMES))
    scale = jnp.transpose(jnp.repeat(scale, UP, axis=2), (1, 0, 2))

    fine = jnp.asarray(fine_rows(cyls, n_cyl, UP))
    ns = jnp.asarray(ns_rows(feeds))
    power = pl.pallas_call(
        functools.partial(beam_kernel, cyls, n_cyl),
        out_shape=jax.ShapeDtypeStruct((steps, cyls, FRAMES, feeds, wide), jnp.bfloat16),
        grid=(steps,),
        in_specs=[
            pl.BlockSpec(memory_space=pl.ANY),
            pl.BlockSpec(fine.shape, lambda g: (0, 0, 0)),
            pl.BlockSpec(ns.shape, lambda g: (0, 0)),
            pl.BlockSpec((1, cyls, wide), lambda g: (g, 0, 0)),
        ],
        out_specs=pl.BlockSpec((1, cyls, FRAMES, feeds, wide), lambda g: (g, 0, 0, 0, 0)),
        scratch_shapes=[
            pltpu.VMEM((pols * blocks, cyls, group, UP, inputs), jnp.bfloat16),
            pltpu.VMEM((n_cyl, steps, group, per, pols, times, inputs), jnp.bfloat16),
            pltpu.SemaphoreType.DMA((steps,)),
            pltpu.SemaphoreType.DMA((n_cyl, steps)),
            pltpu.SemaphoreType.DMA((n_cyl, steps)),
        ],
        compiler_params=pltpu.CompilerParams(
            dimension_semantics=("arbitrary",), collective_id=0, has_side_effects=True
        ),
        name="beams",
    )(volts, fine, ns, scale)

    near = feeds // n_chan
    power = power.reshape(steps, n_cyl, per, FRAMES, n_chan, near, wide)
    power = jnp.transpose(power, (4, 1, 2, 3, 0, 5, 6))
    power = power.reshape(n_chan * n_cyl, per, FRAMES, steps, near, wide)
    power = lax.all_to_all(power, ("chan", "cyl"), split_axis=0, concat_axis=0, tiled=True)
    if (steps * wide) % 128 == 0:
        return spread(power)
    power = jnp.transpose(power, (1, 4, 2, 0, 3, 5))
    return power.reshape(per, near, FRAMES, -1).astype(jnp.float32)


def either(n_chan, n_cyl, volts, gain_exponents):
    if fits(n_chan, n_cyl, volts):
        return fused(n_chan, n_cyl, volts, gain_exponents)
    return local(n_chan, n_cyl, volts, gain_exponents)


def solution(mesh):
    return jax.shard_map(
        functools.partial(either, mesh.shape["chan"], mesh.shape["cyl"]),
        mesh=mesh,
        in_specs=(P("chan", "cyl", None, None, None), P("chan", "cyl")),
        out_specs=P("cyl", "chan", None, None),
        check_vma=False,
    )
```

```python
import functools
import math

import jax
import jax.numpy as jnp
import ml_dtypes
import numpy as np
from jax import lax
from jax.experimental import pallas as pl
from jax.experimental.pallas import tpu as pltpu
from jax.sharding import PartitionSpec as P

UP = 16
FRAMES = 2


def ns_rows(feeds):
    index = np.arange(feeds)
    theta = (index[None, :] * (index[:, None] - feeds // 2) % feeds) * (2.0 * math.pi / feeds)
    cosine = np.cos(theta) / math.sqrt(feeds)
    sine = np.sin(theta) / math.sqrt(feeds)
    table = np.concatenate(
        [np.concatenate([cosine, sine], axis=1), np.concatenate([-sine, cosine], axis=1)], axis=0
    )
    return table.astype(ml_dtypes.bfloat16)


def fine_rows(cyls, n_cyl, up):
    index = np.arange(up)
    theta = (index[:, None] * index[None, :] % up) * (2.0 * math.pi / up)
    rounded = lambda x: (x / math.sqrt(up)).astype(ml_dtypes.bfloat16).astype(np.float64)
    fine = rounded(np.cos(theta)) - 1j * rounded(np.sin(theta))
    cyl = np.arange(cyls)
    phase = 2.0 * math.pi * cyl[None, :] * (cyl[:, None] - (cyls - 1) / 2.0) / cyls
    weight = np.exp(-1j * phase) / 2.0
    both = np.einsum("ec,km->emck", weight, fine)
    parts = np.stack(
        [np.stack([both.real, -both.imag], axis=3), np.stack([both.imag, both.real], axis=3)], axis=0
    )
    per = cyls // n_cyl
    tables = []
    for rank in range(n_cyl):
        order = [((rank - d) % n_cyl) * per + c for d in range(n_cyl) for c in range(per)]
        tables.append(parts[:, :, :, order].reshape(2 * cyls * up, cyls * 2 * up))
    return np.stack(tables).astype(ml_dtypes.bfloat16)


def beam_kernel(
    cyls, n_cyl, volts_ref, fine_ref, ns_ref, gain_ref, out_ref,
    mid_ref, held_ref, own_sem, send_sem, recv_sem,
):
    step = pl.program_id(0)
    steps = pl.num_programs(0)
    _, _, group, per, pols, times, inputs = held_ref.shape
    feeds = inputs // 2
    blocks = times // UP
    sums = blocks // FRAMES
    rank = lax.axis_index("cyl")

    def own_copy(g):
        rows = pl.ds((rank * steps + g) * group, group)
        return pltpu.make_async_copy(volts_ref.at[rows], held_ref.at[0, g], own_sem.at[g])

    def far_copy(d, g):
        to = lax.rem(rank + d, n_cyl)
        rows = pl.ds((to * steps + g) * group, group)
        return pltpu.make_async_remote_copy(
            src_ref=volts_ref.at[rows],
            dst_ref=held_ref.at[d, g],
            send_sem=send_sem.at[d, g],
            recv_sem=recv_sem.at[d, g],
            device_id={"cyl": to},
            device_id_type=pl.DeviceIdType.MESH,
        )

    @pl.when(step == 0)
    def _():
        own_copy(0).start()
        barrier = pltpu.get_barrier_semaphore()
        for d in range(1, n_cyl):
            pl.semaphore_signal(
                barrier, inc=1, device_id={"cyl": lax.rem(rank + d, n_cyl)},
                device_id_type=pl.DeviceIdType.MESH,
            )
        pl.semaphore_wait(barrier, n_cyl - 1)

        def start(g, carry):
            for d in range(1, n_cyl):
                far_copy(d, g).start()

            @pl.when(g > 0)
            def _():
                own_copy(g).start()

            return carry

        lax.fori_loop(0, steps, start, 0)

    own_copy(step).wait()
    for d in range(1, n_cyl):
        far_copy(d, step).wait()
    volt_refs = [held_ref.at[d, step] for d in range(n_cyl)]
    fine = fine_ref[rank]

    def one_chan(ch, carry):
        for p in range(pols):
            for j in range(blocks):
                rows = jnp.concatenate(
                    [
                        ref[ch, c, p, j * UP : (j + 1) * UP, r * feeds : (r + 1) * feeds]
                        for ref in volt_refs
                        for c in range(per)
                        for r in range(2)
                    ],
                    axis=0,
                )
                got = jnp.dot(fine, rows, preferred_element_type=jnp.float32).astype(jnp.bfloat16)
                for s in range(2):
                    for e in range(cyls):
                        at = (s * cyls + e) * UP
                        mid_ref[p * blocks + j, e, ch, :, s * feeds : (s + 1) * feeds] = got[at : at + UP]
        return carry

    lax.fori_loop(0, group, one_chan, 0)
    wide = group * UP
    pair = 2 if cyls % 2 == 0 else 1
    ns = ns_ref[...]
    for q in range(FRAMES):
        for e in range(0, cyls, pair):
            total = None
            for p in range(pols):
                for j in range(q * sums, (q + 1) * sums):
                    block = mid_ref[p * blocks + j, e : e + pair].reshape(pair * wide, inputs)
                    spectra = lax.dot_general(
                        ns, block, (((1,), (1,)), ((), ())), preferred_element_type=jnp.float32
                    )
                    squared = spectra * spectra
                    power = squared[:feeds] + squared[feeds:]
                    total = power if total is None else total + power
            for i in range(pair):
                scaled = total[:, i * wide : (i + 1) * wide] * gain_ref[0, e + i : e + i + 1, :]
                out_ref[0, e + i, q] = scaled.astype(jnp.bfloat16)


def spread_kernel(in_ref, out_ref):
    sources, _, frames, steps, near, wide = in_ref.shape

    def one(source, carry):
        at = pl.multiple_of(source * (steps * wide), 128)
        for g in range(steps):
            rows = [in_ref[source, 0, q, g].astype(jnp.float32) for q in range(frames)]
            out_ref[0, :, :, pl.ds(at + g * wide, wide)] = jnp.stack(rows, axis=1)
        return carry

    lax.fori_loop(0, sources, one, 0)


def spread(power):
    sources, per, frames, steps, near, wide = power.shape
    lanes = sources * steps * wide
    return pl.pallas_call(
        spread_kernel,
        out_shape=jax.ShapeDtypeStruct((per, near, frames, lanes), jnp.float32),
        grid=(per,),
        in_specs=[pl.BlockSpec((sources, 1, frames, steps, near, wide), lambda e: (0, e, 0, 0, 0, 0))],
        out_specs=pl.BlockSpec((1, near, frames, lanes), lambda e: (e, 0, 0, 0)),
        compiler_params=pltpu.CompilerParams(dimension_semantics=("arbitrary",)),
        name="spread",
    )(power)


def half_rows(feeds):
    half = feeds // 2
    table = np.asarray(ns_rows(feeds)).reshape(2, half, 2, 2, feeds)[..., :half]
    return np.transpose(table, (2, 0, 1, 3, 4)).reshape(2, feeds, feeds)


def fused_kernel(
    n_chan, n_cyl, volts_ref, gains_ref, fine_hbm, ns_hbm, out_ref,
    held_ref, mid_ref, send_ref, recv_ref, exps_ref, scale_ref, fine_ref, ns_ref,
    own_sem, volt_send_sem, volt_recv_sem, exp_sem, exp_send_sem, exp_recv_sem, table_sem,
    send_sem, recv_sem, pair_sem, go_sem,
):
    chip = lax.axis_index("chan")
    rank = lax.axis_index("cyl")
    me = chip * n_cyl + rank
    devices = n_chan * n_cyl
    _, stages, group, per, pols, times, inputs = held_ref.shape
    pieces = volt_recv_sem.shape[2]
    piece = group // pieces
    blocks = times // UP
    feeds = inputs // 2
    half = feeds // 2
    cyls = per * n_cyl
    steps = stages // FRAMES
    own = steps * group
    wide = group * UP
    near = feeds // n_chan

    def volt_rows(to, s, first, count):
        at = to * own + (s // FRAMES) * group + first
        time = pl.multiple_of((s % FRAMES) * times, times)
        return volts_ref.at[pl.ds(at, count), :, :, pl.ds(time, times), :]

    def own_copy(s):
        return pltpu.make_async_copy(volt_rows(rank, s, 0, group), held_ref.at[rank, s], own_sem.at[s])

    def far_copy(d, s, i):
        to = lax.rem(rank + d, n_cyl)
        return pltpu.make_async_remote_copy(
            src_ref=volt_rows(to, s, i * piece, piece),
            dst_ref=held_ref.at[rank, s, pl.ds(i * piece, piece)],
            send_sem=volt_send_sem.at[d],
            recv_sem=volt_recv_sem.at[d, s, i],
            device_id={"cyl": to},
            device_id_type=pl.DeviceIdType.MESH,
        )

    def far_arrived(d, s, i):
        source = lax.rem(rank + n_cyl - d, n_cyl)
        there = held_ref.at[source, s, pl.ds(i * piece, piece)]
        return pltpu.make_async_copy(there, there, volt_recv_sem.at[d, s, i])

    def exp_copy(d):
        return pltpu.make_async_remote_copy(
            src_ref=gains_ref,
            dst_ref=exps_ref.at[rank],
            send_sem=exp_send_sem.at[d],
            recv_sem=exp_recv_sem.at[d],
            device_id={"cyl": lax.rem(rank + d, n_cyl)},
            device_id_type=pl.DeviceIdType.MESH,
        )

    fine_copy = pltpu.make_async_copy(fine_hbm, fine_ref, table_sem.at[0])
    ns_copy = pltpu.make_async_copy(ns_hbm, ns_ref, table_sem.at[1])
    own_exps = pltpu.make_async_copy(gains_ref, exps_ref.at[rank], exp_sem)

    barrier = pltpu.get_barrier_semaphore()
    mesh_id = pl.DeviceIdType.MESH

    @pl.when(rank == 0)
    def _():
        pl.semaphore_signal(barrier, inc=1, device_id={"cyl": 1}, device_id_type=mesh_id)

    own_copy(0).start()
    fine_copy.start()
    own_exps.start()
    ns_copy.start()

    @pl.when(rank == 1)
    def _():
        pl.semaphore_wait(barrier, 1)
        pl.semaphore_signal(pair_sem, inc=1, device_id={"cyl": 0}, device_id_type=mesh_id)

    @pl.when(rank == 0)
    def _():
        pl.semaphore_wait(pair_sem, 1)

        def greet(i, carry):
            to = lax.rem(chip + i, n_chan)
            pl.semaphore_signal(barrier, inc=1, device_id={"chan": to}, device_id_type=mesh_id)
            return carry

        lax.fori_loop(1, n_chan, greet, 0)

    def all_here():
        @pl.when(rank == 0)
        def _():
            pl.semaphore_wait(barrier, n_chan - 1)
            pl.semaphore_signal(go_sem, inc=1, device_id={"cyl": 1}, device_id_type=mesh_id)

        @pl.when(rank == 1)
        def _():
            pl.semaphore_wait(go_sem, 1)

    def start_own(s, carry):
        own_copy(s).start()
        return carry

    def start_far(n, carry):
        for d in range(1, n_cyl):
            far_copy(d, n // pieces, n % pieces).start()
        return carry

    lax.fori_loop(0, pieces, start_far, 0)
    for d in range(1, n_cyl):
        exp_copy(d).start()
    lax.fori_loop(1, stages, start_own, 0)
    lax.fori_loop(pieces, stages * pieces, start_far, 0)
    fine_copy.wait()
    own_exps.wait()
    ns_copy.wait()
    for d in range(1, n_cyl):
        exp_copy(d).wait()
    chans = exps_ref.shape[2]
    lane = lax.broadcasted_iota(jnp.int32, (chans, own * UP), 1) // UP + rank * own
    pick = (lane == lax.broadcasted_iota(jnp.int32, (chans, own * UP), 0)).astype(jnp.float32)
    exps = jnp.concatenate([exps_ref[i] for i in range(n_cyl)], axis=0).astype(jnp.float32)
    spread_exps = jnp.dot(exps, pick, preferred_element_type=jnp.float32)
    scale = jnp.exp2(2.0 * spread_exps) / (pols * blocks)
    for g in range(steps):
        scale_ref[g] = scale[:, g * wide : (g + 1) * wide]

    def one_stage(s, carry):
        own_copy(s).wait()
        fine = fine_ref[...]

        def one_piece(i, inner):
            for d in range(1, n_cyl):
                far_arrived(d, s, i).wait()
            for c0 in range(piece):
                ch = i * piece + c0
                for p in range(pols):
                    for j in range(blocks):
                        rows = jnp.concatenate(
                            [
                                held_ref[o, s, ch, c, p, j * UP : (j + 1) * UP, r * feeds : (r + 1) * feeds]
                                for o in range(n_cyl)
                                for c in range(per)
                                for r in range(2)
                            ],
                            axis=0,
                        )
                        got = jnp.dot(fine, rows, preferred_element_type=jnp.float32)
                        low, high = got[:, :half], got[:, half:]
                        both = ((low + high).astype(jnp.bfloat16), (low - high).astype(jnp.bfloat16))
                        for odd in range(2):
                            for r in range(2):
                                for e in range(cyls):
                                    at = (r * cyls + e) * UP
                                    mid_ref[p * blocks + j, odd, e, ch, :, r * half : (r + 1) * half] = (
                                        both[odd][at : at + UP]
                                    )
            return inner

        lax.fori_loop(0, pieces, one_piece, 0)
        for owner in range(n_cyl):
            parts = []
            for odd in range(2):
                ns = ns_ref[odd]
                total = None
                for b in range(pols * blocks):
                    block = mid_ref[b, odd, owner * per : (owner + 1) * per].reshape(per * wide, feeds)
                    spectra = lax.dot_general(
                        ns, block, (((1,), (1,)), ((), ())), preferred_element_type=jnp.float32
                    )
                    squared = spectra * spectra
                    power = squared[:half] + squared[half:]
                    total = power if total is None else total + power
                parts.append(total)
            for e in range(per):
                factor = scale_ref[s // FRAMES, owner * per + e : owner * per + e + 1, :]
                scaled = [
                    (part[:, e * wide : (e + 1) * wide] * factor).reshape(n_chan, near // 2, wide)
                    for part in parts
                ]
                send_ref[s, owner, :, e] = jnp.concatenate(scaled, axis=1).astype(jnp.bfloat16)

            if owner == 0:
                pl.when(s == 0)(all_here)

            def send(i, inner):
                side = lax.rem(chip // (n_chan // 2) + 1 + i // (n_chan // 2), 2)
                to = side * (n_chan // 2) + lax.rem(chip + 1 + i, n_chan // 2)
                here = jnp.logical_and(to == chip, rank == owner)

                @pl.when(here)
                def _():
                    pltpu.make_async_copy(
                        send_ref.at[s, owner, to], recv_ref.at[s, me], recv_sem.at[s]
                    ).start()

                @pl.when(jnp.logical_not(here))
                def _():
                    pltpu.make_async_remote_copy(
                        src_ref=send_ref.at[s, owner, to],
                        dst_ref=recv_ref.at[s, me],
                        send_sem=send_sem,
                        recv_sem=recv_sem.at[s],
                        device_id={"chan": to, "cyl": owner},
                        device_id_type=pl.DeviceIdType.MESH,
                    ).start()

                return inner

            lax.fori_loop(0, n_chan, send, 0)
        return carry

    lax.fori_loop(0, stages, one_stage, 0)

    depth = devices * stages

    def spread_stage(s, carry):
        pltpu.make_async_copy(recv_ref.at[s], recv_ref.at[s], recv_sem.at[s]).wait()

        def one(source, inner):
            row = (source * steps + s // FRAMES) * FRAMES + s % FRAMES
            for e in range(per):
                tile = recv_ref[s, source, e].astype(jnp.float32)
                for odd in range(2):
                    at = (e * near + odd) * depth + row
                    out_ref[pl.ds(at, near // 2, 2 * depth), :] = tile[odd * (near // 2) : (odd + 1) * (near // 2)]
            return inner

        lax.fori_loop(0, devices, one, 0)
        return carry

    lax.fori_loop(0, stages, spread_stage, 0)
    sent = recv_ref.at[:, : devices - 1]
    pltpu.make_async_copy(sent, sent, send_sem).wait()
    for d in range(1, n_cyl):
        pltpu.make_async_copy(held_ref.at[0], held_ref.at[0], volt_send_sem.at[d]).wait()


def fused(n_chan, n_cyl, volts, gain_exponents):
    chans, per, pols, times, inputs = volts.shape
    feeds = inputs // 2
    cyls = per * n_cyl
    own = chans // n_cyl
    group = 128 // UP
    steps = own // group
    stages = steps * FRAMES
    span = times // FRAMES
    blocks = span // UP
    near = feeds // n_chan
    devices = n_chan * n_cyl
    wide = group * UP
    pieces = 4
    fine = jnp.asarray(fine_rows(cyls, 1, UP)[0])
    ns = jnp.asarray(half_rows(feeds))
    operands = (volts, gain_exponents.T, fine, ns)
    dma = pltpu.SemaphoreType.DMA
    out = pl.pallas_call(
        functools.partial(fused_kernel, n_chan, n_cyl),
        out_shape=jax.ShapeDtypeStruct((per * near * devices * stages, wide), jnp.float32),
        in_specs=[pl.BlockSpec(memory_space=pltpu.HBM)] * 4,
        out_specs=pl.BlockSpec(memory_space=pltpu.VMEM),
        scratch_shapes=[
            pltpu.VMEM((n_cyl, stages, group, per, pols, span, inputs), jnp.bfloat16),
            pltpu.VMEM((pols * blocks, 2, cyls, group, UP, feeds), jnp.bfloat16),
            pltpu.VMEM((stages, n_cyl, n_chan, per, near, wide), jnp.bfloat16),
            pltpu.VMEM((stages, devices, per, near, wide), jnp.bfloat16),
            pltpu.VMEM((n_cyl, per, chans), jnp.int32),
            pltpu.VMEM((steps, cyls, wide), jnp.float32),
            pltpu.VMEM(fine.shape, jnp.bfloat16),
            pltpu.VMEM(ns.shape, jnp.bfloat16),
            dma((stages,)),
            dma((n_cyl,)),
            dma((n_cyl, stages, pieces)),
            dma,
            dma((n_cyl,)),
            dma((n_cyl,)),
            dma((2,)),
            dma,
            dma((stages,)),
            pltpu.SemaphoreType.REGULAR,
            pltpu.SemaphoreType.REGULAR,
        ],
        compiler_params=pltpu.CompilerParams(
            collective_id=0, has_side_effects=True, vmem_limit_bytes=48 * 1024 * 1024
        ),
        name="fused",
    )(*[pltpu.with_memory_space_constraint(x, pltpu.HBM) for x in operands])
    out = out.reshape(per, near, devices * steps, FRAMES, wide)
    return jnp.transpose(out, (0, 1, 3, 2, 4)).reshape(per, near, FRAMES, -1)


def fits(n_chan, n_cyl, volts):
    chans, per, pols, times, inputs = volts.shape
    own = chans // n_cyl
    feeds = inputs // 2
    return (
        n_cyl == 2
        and n_chan % 2 == 0
        and own % (128 // UP) == 0
        and feeds % (16 * n_chan) == 0
        and feeds % 256 == 0
        and times % (FRAMES * UP) == 0
    )


def local(n_chan, n_cyl, volts, gain_exponents):
    chans, per, pols, times, inputs = volts.shape
    feeds = inputs // 2
    cyls = per * n_cyl
    own = chans // n_cyl
    group = math.gcd(8, own)
    steps = own // group
    wide = group * UP
    blocks = times // UP
    rank = lax.axis_index("cyl")
    gains = [lax.dynamic_slice_in_dim(gain_exponents, rank * own, own, 0)]
    for d in range(1, n_cyl):
        ring = [(k, (k + d) % n_cyl) for k in range(n_cyl)]
        to = (rank + d) % n_cyl
        gains.append(
            lax.ppermute(lax.dynamic_slice_in_dim(gain_exponents, to * own, own, 0), "cyl", ring)
        )
    stacked = jnp.stack(gains)
    order = (rank - jnp.arange(n_cyl, dtype=jnp.int32)) % n_cyl
    exps = jnp.take(stacked, order, axis=0)
    exps = jnp.transpose(exps, (0, 2, 1)).reshape(cyls, steps, group)
    scale = jnp.exp2(2.0 * exps.astype(jnp.float32)) / (pols * (blocks // FRAMES))
    scale = jnp.transpose(jnp.repeat(scale, UP, axis=2), (1, 0, 2))

    fine = jnp.asarray(fine_rows(cyls, n_cyl, UP))
    ns = jnp.asarray(ns_rows(feeds))
    power = pl.pallas_call(
        functools.partial(beam_kernel, cyls, n_cyl),
        out_shape=jax.ShapeDtypeStruct((steps, cyls, FRAMES, feeds, wide), jnp.bfloat16),
        grid=(steps,),
        in_specs=[
            pl.BlockSpec(memory_space=pl.ANY),
            pl.BlockSpec(fine.shape, lambda g: (0, 0, 0)),
            pl.BlockSpec(ns.shape, lambda g: (0, 0)),
            pl.BlockSpec((1, cyls, wide), lambda g: (g, 0, 0)),
        ],
        out_specs=pl.BlockSpec((1, cyls, FRAMES, feeds, wide), lambda g: (g, 0, 0, 0, 0)),
        scratch_shapes=[
            pltpu.VMEM((pols * blocks, cyls, group, UP, inputs), jnp.bfloat16),
            pltpu.VMEM((n_cyl, steps, group, per, pols, times, inputs), jnp.bfloat16),
            pltpu.SemaphoreType.DMA((steps,)),
            pltpu.SemaphoreType.DMA((n_cyl, steps)),
            pltpu.SemaphoreType.DMA((n_cyl, steps)),
        ],
        compiler_params=pltpu.CompilerParams(
            dimension_semantics=("arbitrary",), collective_id=0, has_side_effects=True
        ),
        name="beams",
    )(volts, fine, ns, scale)

    near = feeds // n_chan
    power = power.reshape(steps, n_cyl, per, FRAMES, n_chan, near, wide)
    power = jnp.transpose(power, (4, 1, 2, 3, 0, 5, 6))
    power = power.reshape(n_chan * n_cyl, per, FRAMES, steps, near, wide)
    power = lax.all_to_all(power, ("chan", "cyl"), split_axis=0, concat_axis=0, tiled=True)
    if (steps * wide) % 128 == 0:
        return spread(power)
    power = jnp.transpose(power, (1, 4, 2, 0, 3, 5))
    return power.reshape(per, near, FRAMES, -1).astype(jnp.float32)


def either(n_chan, n_cyl, volts, gain_exponents):
    if fits(n_chan, n_cyl, volts):
        return fused(n_chan, n_cyl, volts, gain_exponents)
    return local(n_chan, n_cyl, volts, gain_exponents)


def solution(mesh):
    return jax.shard_map(
        functools.partial(either, mesh.shape["chan"], mesh.shape["cyl"]),
        mesh=mesh,
        in_specs=(P("chan", "cyl", None, None, None), P("chan", "cyl")),
        out_specs=P("cyl", "chan", None, None),
        check_vma=False,
    )
```

```python
import functools
import math

import jax
import jax.numpy as jnp
import ml_dtypes
import numpy as np
from jax import lax
from jax.experimental import pallas as pl
from jax.experimental.pallas import tpu as pltpu
from jax.sharding import PartitionSpec as P

UP = 16
FRAMES = 2


def ns_rows(feeds):
    index = np.arange(feeds)
    theta = (index[None, :] * (index[:, None] - feeds // 2) % feeds) * (2.0 * math.pi / feeds)
    cosine = np.cos(theta) / math.sqrt(feeds)
    sine = np.sin(theta) / math.sqrt(feeds)
    table = np.concatenate(
        [np.concatenate([cosine, sine], axis=1), np.concatenate([-sine, cosine], axis=1)], axis=0
    )
    return table.astype(ml_dtypes.bfloat16)


def fine_rows(cyls, n_cyl, up):
    index = np.arange(up)
    theta = (index[:, None] * index[None, :] % up) * (2.0 * math.pi / up)
    rounded = lambda x: (x / math.sqrt(up)).astype(ml_dtypes.bfloat16).astype(np.float64)
    fine = rounded(np.cos(theta)) - 1j * rounded(np.sin(theta))
    cyl = np.arange(cyls)
    phase = 2.0 * math.pi * cyl[None, :] * (cyl[:, None] - (cyls - 1) / 2.0) / cyls
    weight = np.exp(-1j * phase) / 2.0
    both = np.einsum("ec,km->emck", weight, fine)
    parts = np.stack(
        [np.stack([both.real, -both.imag], axis=3), np.stack([both.imag, both.real], axis=3)], axis=0
    )
    per = cyls // n_cyl
    tables = []
    for rank in range(n_cyl):
        order = [((rank - d) % n_cyl) * per + c for d in range(n_cyl) for c in range(per)]
        tables.append(parts[:, :, :, order].reshape(2 * cyls * up, cyls * 2 * up))
    return np.stack(tables).astype(ml_dtypes.bfloat16)


def beam_kernel(
    cyls, n_cyl, volts_ref, fine_ref, ns_ref, gain_ref, out_ref,
    mid_ref, held_ref, own_sem, send_sem, recv_sem,
):
    step = pl.program_id(0)
    steps = pl.num_programs(0)
    _, _, group, per, pols, times, inputs = held_ref.shape
    feeds = inputs // 2
    blocks = times // UP
    sums = blocks // FRAMES
    rank = lax.axis_index("cyl")

    def own_copy(g):
        rows = pl.ds((rank * steps + g) * group, group)
        return pltpu.make_async_copy(volts_ref.at[rows], held_ref.at[0, g], own_sem.at[g])

    def far_copy(d, g):
        to = lax.rem(rank + d, n_cyl)
        rows = pl.ds((to * steps + g) * group, group)
        return pltpu.make_async_remote_copy(
            src_ref=volts_ref.at[rows],
            dst_ref=held_ref.at[d, g],
            send_sem=send_sem.at[d, g],
            recv_sem=recv_sem.at[d, g],
            device_id={"cyl": to},
            device_id_type=pl.DeviceIdType.MESH,
        )

    @pl.when(step == 0)
    def _():
        own_copy(0).start()
        barrier = pltpu.get_barrier_semaphore()
        for d in range(1, n_cyl):
            pl.semaphore_signal(
                barrier, inc=1, device_id={"cyl": lax.rem(rank + d, n_cyl)},
                device_id_type=pl.DeviceIdType.MESH,
            )
        pl.semaphore_wait(barrier, n_cyl - 1)

        def start(g, carry):
            for d in range(1, n_cyl):
                far_copy(d, g).start()

            @pl.when(g > 0)
            def _():
                own_copy(g).start()

            return carry

        lax.fori_loop(0, steps, start, 0)

    own_copy(step).wait()
    for d in range(1, n_cyl):
        far_copy(d, step).wait()
    volt_refs = [held_ref.at[d, step] for d in range(n_cyl)]
    fine = fine_ref[rank]

    def one_chan(ch, carry):
        for p in range(pols):
            for j in range(blocks):
                rows = jnp.concatenate(
                    [
                        ref[ch, c, p, j * UP : (j + 1) * UP, r * feeds : (r + 1) * feeds]
                        for ref in volt_refs
                        for c in range(per)
                        for r in range(2)
                    ],
                    axis=0,
                )
                got = jnp.dot(fine, rows, preferred_element_type=jnp.float32).astype(jnp.bfloat16)
                for s in range(2):
                    for e in range(cyls):
                        at = (s * cyls + e) * UP
                        mid_ref[p * blocks + j, e, ch, :, s * feeds : (s + 1) * feeds] = got[at : at + UP]
        return carry

    lax.fori_loop(0, group, one_chan, 0)
    wide = group * UP
    pair = 2 if cyls % 2 == 0 else 1
    ns = ns_ref[...]
    for q in range(FRAMES):
        for e in range(0, cyls, pair):
            total = None
            for p in range(pols):
                for j in range(q * sums, (q + 1) * sums):
                    block = mid_ref[p * blocks + j, e : e + pair].reshape(pair * wide, inputs)
                    spectra = lax.dot_general(
                        ns, block, (((1,), (1,)), ((), ())), preferred_element_type=jnp.float32
                    )
                    squared = spectra * spectra
                    power = squared[:feeds] + squared[feeds:]
                    total = power if total is None else total + power
            for i in range(pair):
                scaled = total[:, i * wide : (i + 1) * wide] * gain_ref[0, e + i : e + i + 1, :]
                out_ref[0, e + i, q] = scaled.astype(jnp.bfloat16)


def spread_kernel(in_ref, out_ref):
    sources, _, frames, steps, near, wide = in_ref.shape

    def one(source, carry):
        at = pl.multiple_of(source * (steps * wide), 128)
        for g in range(steps):
            rows = [in_ref[source, 0, q, g].astype(jnp.float32) for q in range(frames)]
            out_ref[0, :, :, pl.ds(at + g * wide, wide)] = jnp.stack(rows, axis=1)
        return carry

    lax.fori_loop(0, sources, one, 0)


def spread(power):
    sources, per, frames, steps, near, wide = power.shape
    lanes = sources * steps * wide
    return pl.pallas_call(
        spread_kernel,
        out_shape=jax.ShapeDtypeStruct((per, near, frames, lanes), jnp.float32),
        grid=(per,),
        in_specs=[pl.BlockSpec((sources, 1, frames, steps, near, wide), lambda e: (0, e, 0, 0, 0, 0))],
        out_specs=pl.BlockSpec((1, near, frames, lanes), lambda e: (e, 0, 0, 0)),
        compiler_params=pltpu.CompilerParams(dimension_semantics=("arbitrary",)),
        name="spread",
    )(power)


def half_rows(feeds):
    half = feeds // 2
    table = np.asarray(ns_rows(feeds)).reshape(2, half, 2, 2, feeds)[..., :half]
    return np.transpose(table, (2, 0, 1, 3, 4)).reshape(2, feeds, feeds)


def fused_kernel(
    n_chan, n_cyl, volts_ref, gains_ref, fine_hbm, ns_hbm, out_ref,
    held_ref, mid_ref, head_out_ref, send_ref, head_in_ref, recv_ref,
    exps_ref, head_scale_ref, scale_ref, fine_ref, ns_ref,
    own_sem, volt_send_sem, volt_recv_sem, exp_sem, exp_send_sem, exp_recv_sem, table_sem,
    head_send_sem, head_recv_sem, send_sem, recv_sem, pair_sem, go_sem,
):
    chip = lax.axis_index("chan")
    rank = lax.axis_index("cyl")
    me = chip * n_cyl + rank
    devices = n_chan * n_cyl
    _, stages, group, per, pols, times, inputs = held_ref.shape
    pieces = volt_recv_sem.shape[2]
    piece = group // pieces
    blocks = times // UP
    feeds = inputs // 2
    half = feeds // 2
    cyls = per * n_cyl
    steps = stages // FRAMES
    own = steps * group
    wide = group * UP
    near = feeds // n_chan
    part = group // per
    slim = part * UP

    def volt_rows(to, s, first, count):
        at = to * own + (s // FRAMES) * group + first
        time = pl.multiple_of((s % FRAMES) * times, times)
        return volts_ref.at[pl.ds(at, count), :, :, pl.ds(time, times), :]

    def own_copy(s):
        return pltpu.make_async_copy(volt_rows(rank, s, 0, group), held_ref.at[rank, s], own_sem.at[s])

    def far_copy(d, s, i):
        to = lax.rem(rank + d, n_cyl)
        return pltpu.make_async_remote_copy(
            src_ref=volt_rows(to, s, i * piece, piece),
            dst_ref=held_ref.at[rank, s, pl.ds(i * piece, piece)],
            send_sem=volt_send_sem.at[d],
            recv_sem=volt_recv_sem.at[d, s, i],
            device_id={"cyl": to},
            device_id_type=pl.DeviceIdType.MESH,
        )

    def far_arrived(d, s, i):
        source = lax.rem(rank + n_cyl - d, n_cyl)
        there = held_ref.at[source, s, pl.ds(i * piece, piece)]
        return pltpu.make_async_copy(there, there, volt_recv_sem.at[d, s, i])

    def exp_copy(d):
        return pltpu.make_async_remote_copy(
            src_ref=gains_ref,
            dst_ref=exps_ref.at[rank],
            send_sem=exp_send_sem.at[d],
            recv_sem=exp_recv_sem.at[d],
            device_id={"cyl": lax.rem(rank + d, n_cyl)},
            device_id_type=pl.DeviceIdType.MESH,
        )

    fine_copy = pltpu.make_async_copy(fine_hbm, fine_ref, table_sem.at[0])
    ns_copy = pltpu.make_async_copy(ns_hbm, ns_ref, table_sem.at[1])
    own_exps = pltpu.make_async_copy(gains_ref, exps_ref.at[rank], exp_sem)

    barrier = pltpu.get_barrier_semaphore()
    mesh_id = pl.DeviceIdType.MESH

    @pl.when(rank == 0)
    def _():
        pl.semaphore_signal(barrier, inc=1, device_id={"cyl": 1}, device_id_type=mesh_id)

    @pl.when(rank == 1)
    def _():
        pl.semaphore_signal(barrier, inc=1, device_id={"cyl": 0}, device_id_type=mesh_id)

    def greet(i, carry):
        to = lax.rem(chip + i, n_chan)
        pl.semaphore_signal(barrier, inc=1, device_id={"chan": to, "cyl": 0}, device_id_type=mesh_id)
        return carry

    lax.fori_loop(1, n_chan, greet, 0)
    own_copy(0).start()
    fine_copy.start()
    own_exps.start()
    ns_copy.start()

    @pl.when(rank == 1)
    def _():
        pl.semaphore_wait(barrier, 1)
        pl.semaphore_signal(pair_sem, inc=1, device_id={"cyl": 0}, device_id_type=mesh_id)

    @pl.when(rank == 0)
    def _():
        pl.semaphore_wait(pair_sem, 1)

    def all_here():
        @pl.when(rank == 0)
        def _():
            pl.semaphore_wait(barrier, devices - 1)
            pl.semaphore_signal(go_sem, inc=1, device_id={"cyl": 1}, device_id_type=mesh_id)

        @pl.when(rank == 1)
        def _():
            pl.semaphore_wait(go_sem, 1)

    def start_own(s, carry):
        own_copy(s).start()
        return carry

    def start_far(n, carry):
        for d in range(1, n_cyl):
            far_copy(d, n // pieces, n % pieces).start()
        return carry

    for d in range(1, n_cyl):
        exp_copy(d).start()
    lax.fori_loop(0, pieces, start_far, 0)
    lax.fori_loop(1, stages, start_own, 0)
    lax.fori_loop(pieces, stages * pieces, start_far, 0)
    fine_copy.wait()

    own_exps.wait()
    for d in range(1, n_cyl):
        exp_copy(d).wait()
    chans = exps_ref.shape[2]
    lane = lax.broadcasted_iota(jnp.int32, (chans, own * UP), 1)
    chan = lax.broadcasted_iota(jnp.int32, (chans, own * UP), 0) - rank * own
    exps = jnp.concatenate([exps_ref[i] for i in range(n_cyl)], axis=0).astype(jnp.float32)

    def scale_of(pick):
        spread = jnp.dot(exps, pick.astype(jnp.float32), preferred_element_type=jnp.float32)
        return jnp.exp2(2.0 * spread) / (pols * blocks)

    scale = scale_of(chan == lane // UP)
    for g in range(steps):
        for o in range(n_cyl):
            scale_ref[g, o] = scale[o * per : (o + 1) * per, g * wide : (g + 1) * wide]
    lane, chan = lane[:, :wide], chan[:, :wide]
    for h in range(per):
        scale = scale_of(chan == h * part + lane % slim // UP)
        for o in range(n_cyl):
            row = scale[o * per : o * per + 1]
            for e in range(1, per):
                row = jnp.where(lane[:1] // slim == e, scale[o * per + e : o * per + e + 1], row)
            head_scale_ref[h, o] = row

    def fine_piece(s, i):
        fine = fine_ref[...]
        for d in range(1, n_cyl):
            far_arrived(d, s, i).wait()
        for c0 in range(piece):
            ch = i * piece + c0
            for p in range(pols):
                for j in range(blocks):
                    rows = jnp.concatenate(
                        [
                            held_ref[o, s, ch, c, p, j * UP : (j + 1) * UP, r * feeds : (r + 1) * feeds]
                            for o in range(n_cyl)
                            for c in range(per)
                            for r in range(2)
                        ],
                        axis=0,
                    )
                    got = jnp.dot(fine, rows, preferred_element_type=jnp.float32)
                    low, high = got[:, :half], got[:, half:]
                    both = ((low + high).astype(jnp.bfloat16), (low - high).astype(jnp.bfloat16))
                    for odd in range(2):
                        for r in range(2):
                            for e in range(cyls):
                                at = (r * cyls + e) * UP
                                mid_ref[p * blocks + j, odd, e, ch, :, r * half : (r + 1) * half] = (
                                    both[odd][at : at + UP]
                                )

    def fine_pieces(s, first, last):
        def one(i, carry):
            fine_piece(s, i)
            return carry

        lax.fori_loop(first, last, one, 0)

    def powers(owner, first, count):
        parts = []
        for odd in range(2):
            total = None
            for b in range(pols * blocks):
                block = mid_ref[b, odd, pl.ds(owner * per, per), first : first + count]
                spectra = lax.dot_general(
                    ns_ref[odd], block.reshape(per * count * UP, feeds), (((1,), (1,)), ((), ())),
                    preferred_element_type=jnp.float32,
                )
                squared = spectra * spectra
                power = squared[:half] + squared[half:]
                total = power if total is None else total + power
            parts.append(total)
        return parts

    def by_chip(parts, factor):
        scaled = [(part * factor).reshape(n_chan, near // 2, wide) for part in parts]
        return jnp.concatenate(scaled, axis=1).astype(jnp.bfloat16)

    def send_all(source_ref, target_ref, out_sem, in_sem):
        def send(i, carry):
            peer = lax.rem(me + 1 + i, devices)
            to = peer // n_cyl
            owner = lax.rem(peer, n_cyl)

            @pl.when(peer == me)
            def _():
                pltpu.make_async_copy(source_ref.at[owner, to], target_ref.at[me], in_sem).start()

            @pl.when(peer != me)
            def _():
                pltpu.make_async_remote_copy(
                    src_ref=source_ref.at[owner, to],
                    dst_ref=target_ref.at[me],
                    send_sem=out_sem,
                    recv_sem=in_sem,
                    device_id={"chan": to, "cyl": owner},
                    device_id_type=mesh_id,
                ).start()

            return carry

        lax.fori_loop(0, devices, send, 0)

    own_copy(0).wait()
    for h in range(per):
        fine_pieces(0, h * part // piece, (h + 1) * part // piece)
        if h == 0:
            ns_copy.wait()

        def head_owner(owner, carry):
            head_out_ref[h, owner] = by_chip(powers(owner, h * part, part), head_scale_ref[h, owner])
            return carry

        lax.fori_loop(0, n_cyl, head_owner, 0)
        if h == 0:
            all_here()
        send_all(head_out_ref.at[h], head_in_ref.at[h], head_send_sem, head_recv_sem.at[h])

    def one_stage(s, carry):
        own_copy(s).wait()
        fine_pieces(s, 0, pieces)

        def one_owner(owner, inner):
            parts = powers(owner, 0, group)
            for e in range(per):
                send_ref[s - 1, owner, :, e] = by_chip(
                    [part[:, e * wide : (e + 1) * wide] for part in parts],
                    scale_ref[s // FRAMES, owner, e : e + 1, :],
                )
            return inner

        lax.fori_loop(0, n_cyl, one_owner, 0)
        send_all(send_ref.at[s - 1], recv_ref.at[s - 1], send_sem, recv_sem.at[s - 1])
        return carry

    lax.fori_loop(1, stages, one_stage, 0)

    depth = devices * stages

    several = math.gcd(4, devices)

    def place(s, source, e, tile):
        row = (source * steps + s // FRAMES) * FRAMES + s % FRAMES
        for odd in range(2):
            at = (e * near + odd) * depth + row
            out_ref[pl.ds(at, near // 2, 2 * depth), :] = tile[odd * (near // 2) : (odd + 1) * (near // 2)]

    for h in range(per):
        pltpu.make_async_copy(head_in_ref.at[h], head_in_ref.at[h], head_recv_sem.at[h]).wait()
    slot = lax.broadcasted_iota(jnp.int32, (near, wide), 1) // slim

    def spread_head(source, carry):
        tiles = [head_in_ref[h, source].astype(jnp.float32) for h in range(per)]
        for e in range(per):
            tile = tiles[e]
            for h in range(per):
                if h != e:
                    moved = pltpu.roll(tiles[h], (h - e) * slim % wide, 1)
                    tile = jnp.where(slot == h, moved, tile)
            place(0, source, e, tile)
        return carry

    lax.fori_loop(0, devices, spread_head, 0)

    def spread_stage(s, carry):
        pltpu.make_async_copy(recv_ref.at[s - 1], recv_ref.at[s - 1], recv_sem.at[s - 1]).wait()

        def some(n, inner):
            for k in range(several):
                for e in range(per):
                    source = n * several + k
                    place(s, source, e, recv_ref[s - 1, source, e].astype(jnp.float32))
            return inner

        lax.fori_loop(0, devices // several, some, 0)
        return carry

    lax.fori_loop(1, stages, spread_stage, 0)
    for ref, sem in ((head_in_ref, head_send_sem), (recv_ref, send_sem)):
        sent = ref.at[:, : devices - 1]
        pltpu.make_async_copy(sent, sent, sem).wait()
    for d in range(1, n_cyl):
        pltpu.make_async_copy(held_ref.at[0], held_ref.at[0], volt_send_sem.at[d]).wait()


def fused(n_chan, n_cyl, volts, gain_exponents):
    chans, per, pols, times, inputs = volts.shape
    feeds = inputs // 2
    cyls = per * n_cyl
    own = chans // n_cyl
    group = 128 // UP
    steps = own // group
    stages = steps * FRAMES
    span = times // FRAMES
    blocks = span // UP
    near = feeds // n_chan
    devices = n_chan * n_cyl
    wide = group * UP
    pieces = 4
    fine = jnp.asarray(fine_rows(cyls, 1, UP)[0])
    ns = jnp.asarray(half_rows(feeds))
    operands = (volts, gain_exponents.T, fine, ns)
    dma = pltpu.SemaphoreType.DMA
    out = pl.pallas_call(
        functools.partial(fused_kernel, n_chan, n_cyl),
        out_shape=jax.ShapeDtypeStruct((per * near * devices * stages, wide), jnp.float32),
        in_specs=[pl.BlockSpec(memory_space=pltpu.HBM)] * 4,
        out_specs=pl.BlockSpec(memory_space=pltpu.VMEM),
        scratch_shapes=[
            pltpu.VMEM((n_cyl, stages, group, per, pols, span, inputs), jnp.bfloat16),
            pltpu.VMEM((pols * blocks, 2, cyls, group, UP, feeds), jnp.bfloat16),
            pltpu.VMEM((per, n_cyl, n_chan, near, wide), jnp.bfloat16),
            pltpu.VMEM((stages - 1, n_cyl, n_chan, per, near, wide), jnp.bfloat16),
            pltpu.VMEM((per, devices, near, wide), jnp.bfloat16),
            pltpu.VMEM((stages - 1, devices, per, near, wide), jnp.bfloat16),
            pltpu.VMEM((n_cyl, per, chans), jnp.int32),
            pltpu.VMEM((per, n_cyl, 1, wide), jnp.float32),
            pltpu.VMEM((steps, n_cyl, per, wide), jnp.float32),
            pltpu.VMEM(fine.shape, jnp.bfloat16),
            pltpu.VMEM(ns.shape, jnp.bfloat16),
            dma((stages,)),
            dma((n_cyl,)),
            dma((n_cyl, stages, pieces)),
            dma,
            dma((n_cyl,)),
            dma((n_cyl,)),
            dma((2,)),
            dma,
            dma((per,)),
            dma,
            dma((stages - 1,)),
            pltpu.SemaphoreType.REGULAR,
            pltpu.SemaphoreType.REGULAR,
        ],
        compiler_params=pltpu.CompilerParams(
            collective_id=0, has_side_effects=True, vmem_limit_bytes=48 * 1024 * 1024
        ),
        name="fused",
    )(*[pltpu.with_memory_space_constraint(x, pltpu.HBM) for x in operands])
    out = out.reshape(per, near, devices * steps, FRAMES, wide)
    return jnp.transpose(out, (0, 1, 3, 2, 4)).reshape(per, near, FRAMES, -1)


def fits(n_chan, n_cyl, volts):
    chans, per, pols, times, inputs = volts.shape
    own = chans // n_cyl
    feeds = inputs // 2
    return (
        n_cyl == 2
        and per in (1, 2)
        and own % (128 // UP) == 0
        and feeds % (16 * n_chan) == 0
        and feeds % 256 == 0
        and times % (FRAMES * UP) == 0
    )


def local(n_chan, n_cyl, volts, gain_exponents):
    chans, per, pols, times, inputs = volts.shape
    feeds = inputs // 2
    cyls = per * n_cyl
    own = chans // n_cyl
    group = math.gcd(8, own)
    steps = own // group
    wide = group * UP
    blocks = times // UP
    rank = lax.axis_index("cyl")
    gains = [lax.dynamic_slice_in_dim(gain_exponents, rank * own, own, 0)]
    for d in range(1, n_cyl):
        ring = [(k, (k + d) % n_cyl) for k in range(n_cyl)]
        to = (rank + d) % n_cyl
        gains.append(
            lax.ppermute(lax.dynamic_slice_in_dim(gain_exponents, to * own, own, 0), "cyl", ring)
        )
    stacked = jnp.stack(gains)
    order = (rank - jnp.arange(n_cyl, dtype=jnp.int32)) % n_cyl
    exps = jnp.take(stacked, order, axis=0)
    exps = jnp.transpose(exps, (0, 2, 1)).reshape(cyls, steps, group)
    scale = jnp.exp2(2.0 * exps.astype(jnp.float32)) / (pols * (blocks // FRAMES))
    scale = jnp.transpose(jnp.repeat(scale, UP, axis=2), (1, 0, 2))

    fine = jnp.asarray(fine_rows(cyls, n_cyl, UP))
    ns = jnp.asarray(ns_rows(feeds))
    power = pl.pallas_call(
        functools.partial(beam_kernel, cyls, n_cyl),
        out_shape=jax.ShapeDtypeStruct((steps, cyls, FRAMES, feeds, wide), jnp.bfloat16),
        grid=(steps,),
        in_specs=[
            pl.BlockSpec(memory_space=pl.ANY),
            pl.BlockSpec(fine.shape, lambda g: (0, 0, 0)),
            pl.BlockSpec(ns.shape, lambda g: (0, 0)),
            pl.BlockSpec((1, cyls, wide), lambda g: (g, 0, 0)),
        ],
        out_specs=pl.BlockSpec((1, cyls, FRAMES, feeds, wide), lambda g: (g, 0, 0, 0, 0)),
        scratch_shapes=[
            pltpu.VMEM((pols * blocks, cyls, group, UP, inputs), jnp.bfloat16),
            pltpu.VMEM((n_cyl, steps, group, per, pols, times, inputs), jnp.bfloat16),
            pltpu.SemaphoreType.DMA((steps,)),
            pltpu.SemaphoreType.DMA((n_cyl, steps)),
            pltpu.SemaphoreType.DMA((n_cyl, steps)),
        ],
        compiler_params=pltpu.CompilerParams(
            dimension_semantics=("arbitrary",), collective_id=0, has_side_effects=True
        ),
        name="beams",
    )(volts, fine, ns, scale)

    near = feeds // n_chan
    power = power.reshape(steps, n_cyl, per, FRAMES, n_chan, near, wide)
    power = jnp.transpose(power, (4, 1, 2, 3, 0, 5, 6))
    power = power.reshape(n_chan * n_cyl, per, FRAMES, steps, near, wide)
    power = lax.all_to_all(power, ("chan", "cyl"), split_axis=0, concat_axis=0, tiled=True)
    if (steps * wide) % 128 == 0:
        return spread(power)
    power = jnp.transpose(power, (1, 4, 2, 0, 3, 5))
    return power.reshape(per, near, FRAMES, -1).astype(jnp.float32)


def either(n_chan, n_cyl, volts, gain_exponents):
    if fits(n_chan, n_cyl, volts):
        return fused(n_chan, n_cyl, volts, gain_exponents)
    return local(n_chan, n_cyl, volts, gain_exponents)


def solution(mesh):
    return jax.shard_map(
        functools.partial(either, mesh.shape["chan"], mesh.shape["cyl"]),
        mesh=mesh,
        in_specs=(P("chan", "cyl", None, None, None), P("chan", "cyl")),
        out_specs=P("cyl", "chan", None, None),
        check_vma=False,
    )
```

```python
import functools
import math

import jax
import jax.numpy as jnp
import ml_dtypes
import numpy as np
from jax import lax
from jax.experimental import pallas as pl
from jax.experimental.pallas import tpu as pltpu
from jax.sharding import PartitionSpec as P

UP = 16
FRAMES = 2


def ns_rows(feeds):
    index = np.arange(feeds)
    theta = (index[None, :] * (index[:, None] - feeds // 2) % feeds) * (2.0 * math.pi / feeds)
    cosine = np.cos(theta) / math.sqrt(feeds)
    sine = np.sin(theta) / math.sqrt(feeds)
    table = np.concatenate(
        [np.concatenate([cosine, sine], axis=1), np.concatenate([-sine, cosine], axis=1)], axis=0
    )
    return table.astype(ml_dtypes.bfloat16)


def fine_rows(cyls, n_cyl, up):
    index = np.arange(up)
    theta = (index[:, None] * index[None, :] % up) * (2.0 * math.pi / up)
    rounded = lambda x: (x / math.sqrt(up)).astype(ml_dtypes.bfloat16).astype(np.float64)
    fine = rounded(np.cos(theta)) - 1j * rounded(np.sin(theta))
    cyl = np.arange(cyls)
    phase = 2.0 * math.pi * cyl[None, :] * (cyl[:, None] - (cyls - 1) / 2.0) / cyls
    weight = np.exp(-1j * phase) / 2.0
    both = np.einsum("ec,km->emck", weight, fine)
    parts = np.stack(
        [np.stack([both.real, -both.imag], axis=3), np.stack([both.imag, both.real], axis=3)], axis=0
    )
    per = cyls // n_cyl
    tables = []
    for rank in range(n_cyl):
        order = [((rank - d) % n_cyl) * per + c for d in range(n_cyl) for c in range(per)]
        tables.append(parts[:, :, :, order].reshape(2 * cyls * up, cyls * 2 * up))
    return np.stack(tables).astype(ml_dtypes.bfloat16)


def beam_kernel(
    cyls, n_cyl, volts_ref, fine_ref, ns_ref, gain_ref, out_ref,
    mid_ref, held_ref, own_sem, send_sem, recv_sem,
):
    step = pl.program_id(0)
    steps = pl.num_programs(0)
    _, _, group, per, pols, times, inputs = held_ref.shape
    feeds = inputs // 2
    blocks = times // UP
    sums = blocks // FRAMES
    rank = lax.axis_index("cyl")

    def own_copy(g):
        rows = pl.ds((rank * steps + g) * group, group)
        return pltpu.make_async_copy(volts_ref.at[rows], held_ref.at[0, g], own_sem.at[g])

    def far_copy(d, g):
        to = lax.rem(rank + d, n_cyl)
        rows = pl.ds((to * steps + g) * group, group)
        return pltpu.make_async_remote_copy(
            src_ref=volts_ref.at[rows],
            dst_ref=held_ref.at[d, g],
            send_sem=send_sem.at[d, g],
            recv_sem=recv_sem.at[d, g],
            device_id={"cyl": to},
            device_id_type=pl.DeviceIdType.MESH,
        )

    @pl.when(step == 0)
    def _():
        own_copy(0).start()
        barrier = pltpu.get_barrier_semaphore()
        for d in range(1, n_cyl):
            pl.semaphore_signal(
                barrier, inc=1, device_id={"cyl": lax.rem(rank + d, n_cyl)},
                device_id_type=pl.DeviceIdType.MESH,
            )
        pl.semaphore_wait(barrier, n_cyl - 1)

        def start(g, carry):
            for d in range(1, n_cyl):
                far_copy(d, g).start()

            @pl.when(g > 0)
            def _():
                own_copy(g).start()

            return carry

        lax.fori_loop(0, steps, start, 0)

    own_copy(step).wait()
    for d in range(1, n_cyl):
        far_copy(d, step).wait()
    volt_refs = [held_ref.at[d, step] for d in range(n_cyl)]
    fine = fine_ref[rank]

    def one_chan(ch, carry):
        for p in range(pols):
            for j in range(blocks):
                rows = jnp.concatenate(
                    [
                        ref[ch, c, p, j * UP : (j + 1) * UP, r * feeds : (r + 1) * feeds]
                        for ref in volt_refs
                        for c in range(per)
                        for r in range(2)
                    ],
                    axis=0,
                )
                got = jnp.dot(fine, rows, preferred_element_type=jnp.float32).astype(jnp.bfloat16)
                for s in range(2):
                    for e in range(cyls):
                        at = (s * cyls + e) * UP
                        mid_ref[p * blocks + j, e, ch, :, s * feeds : (s + 1) * feeds] = got[at : at + UP]
        return carry

    lax.fori_loop(0, group, one_chan, 0)
    wide = group * UP
    pair = 2 if cyls % 2 == 0 else 1
    ns = ns_ref[...]
    for q in range(FRAMES):
        for e in range(0, cyls, pair):
            total = None
            for p in range(pols):
                for j in range(q * sums, (q + 1) * sums):
                    block = mid_ref[p * blocks + j, e : e + pair].reshape(pair * wide, inputs)
                    spectra = lax.dot_general(
                        ns, block, (((1,), (1,)), ((), ())), preferred_element_type=jnp.float32
                    )
                    squared = spectra * spectra
                    power = squared[:feeds] + squared[feeds:]
                    total = power if total is None else total + power
            for i in range(pair):
                scaled = total[:, i * wide : (i + 1) * wide] * gain_ref[0, e + i : e + i + 1, :]
                out_ref[0, e + i, q] = scaled.astype(jnp.bfloat16)


def spread_kernel(in_ref, out_ref):
    sources, _, frames, steps, near, wide = in_ref.shape

    def one(source, carry):
        at = pl.multiple_of(source * (steps * wide), 128)
        for g in range(steps):
            rows = [in_ref[source, 0, q, g].astype(jnp.float32) for q in range(frames)]
            out_ref[0, :, :, pl.ds(at + g * wide, wide)] = jnp.stack(rows, axis=1)
        return carry

    lax.fori_loop(0, sources, one, 0)


def spread(power):
    sources, per, frames, steps, near, wide = power.shape
    lanes = sources * steps * wide
    return pl.pallas_call(
        spread_kernel,
        out_shape=jax.ShapeDtypeStruct((per, near, frames, lanes), jnp.float32),
        grid=(per,),
        in_specs=[pl.BlockSpec((sources, 1, frames, steps, near, wide), lambda e: (0, e, 0, 0, 0, 0))],
        out_specs=pl.BlockSpec((1, near, frames, lanes), lambda e: (e, 0, 0, 0)),
        compiler_params=pltpu.CompilerParams(dimension_semantics=("arbitrary",)),
        name="spread",
    )(power)


def half_rows(feeds):
    half = feeds // 2
    table = np.asarray(ns_rows(feeds)).reshape(2, half, 2, 2, feeds)[..., :half]
    return np.transpose(table, (2, 0, 1, 3, 4)).reshape(2, feeds, feeds)


def fused_kernel(
    n_chan, n_cyl, volts_ref, gains_ref, fine_hbm, ns_hbm, out_ref,
    held_ref, mid_ref, head_out_ref, send_ref, head_in_ref, recv_ref,
    exps_ref, head_scale_ref, scale_ref, fine_ref, ns_ref,
    own_sem, volt_send_sem, volt_recv_sem, exp_sem, exp_send_sem, exp_recv_sem, table_sem,
    head_send_sem, head_recv_sem, send_sem, recv_sem, pair_sem, go_sem,
):
    chip = lax.axis_index("chan")
    rank = lax.axis_index("cyl")
    me = chip * n_cyl + rank
    devices = n_chan * n_cyl
    _, stages, group, per, pols, times, inputs = held_ref.shape
    pieces = volt_recv_sem.shape[2]
    piece = group // pieces
    blocks = times // UP
    feeds = inputs // 2
    half = feeds // 2
    cyls = per * n_cyl
    steps = stages // FRAMES
    own = steps * group
    wide = group * UP
    near = feeds // n_chan
    share = group // per
    slim = share * UP

    def volt_rows(to, s, first, count):
        at = to * own + (s // FRAMES) * group + first
        time = pl.multiple_of((s % FRAMES) * times, times)
        return volts_ref.at[pl.ds(at, count), :, :, pl.ds(time, times), :]

    def own_copy(s):
        return pltpu.make_async_copy(volt_rows(rank, s, 0, group), held_ref.at[rank, s], own_sem.at[s])

    def far_copy(d, s, i):
        to = lax.rem(rank + d, n_cyl)
        return pltpu.make_async_remote_copy(
            src_ref=volt_rows(to, s, i * piece, piece),
            dst_ref=held_ref.at[rank, s, pl.ds(i * piece, piece)],
            send_sem=volt_send_sem.at[d],
            recv_sem=volt_recv_sem.at[d, s, i],
            device_id={"cyl": to},
            device_id_type=pl.DeviceIdType.MESH,
        )

    def far_arrived(d, s, i):
        source = lax.rem(rank + n_cyl - d, n_cyl)
        there = held_ref.at[source, s, pl.ds(i * piece, piece)]
        return pltpu.make_async_copy(there, there, volt_recv_sem.at[d, s, i])

    def exp_copy(d):
        return pltpu.make_async_remote_copy(
            src_ref=gains_ref,
            dst_ref=exps_ref.at[rank],
            send_sem=exp_send_sem.at[d],
            recv_sem=exp_recv_sem.at[d],
            device_id={"cyl": lax.rem(rank + d, n_cyl)},
            device_id_type=pl.DeviceIdType.MESH,
        )

    fine_copy = pltpu.make_async_copy(fine_hbm, fine_ref, table_sem.at[0])
    ns_copy = pltpu.make_async_copy(ns_hbm, ns_ref, table_sem.at[1])
    own_exps = pltpu.make_async_copy(gains_ref, exps_ref.at[rank], exp_sem)

    barrier = pltpu.get_barrier_semaphore()
    mesh_id = pl.DeviceIdType.MESH

    @pl.when(rank == 0)
    def _():
        pl.semaphore_signal(barrier, inc=1, device_id={"cyl": 1}, device_id_type=mesh_id)

    @pl.when(rank == 1)
    def _():
        pl.semaphore_signal(barrier, inc=1, device_id={"cyl": 0}, device_id_type=mesh_id)

    def greet(i, carry):
        to = lax.rem(chip + i, n_chan)
        pl.semaphore_signal(barrier, inc=1, device_id={"chan": to, "cyl": 0}, device_id_type=mesh_id)
        return carry

    lax.fori_loop(1, n_chan, greet, 0)
    own_copy(0).start()
    fine_copy.start()
    own_exps.start()
    ns_copy.start()

    @pl.when(rank == 1)
    def _():
        pl.semaphore_wait(barrier, 1)
        pl.semaphore_signal(pair_sem, inc=1, device_id={"cyl": 0}, device_id_type=mesh_id)

    @pl.when(rank == 0)
    def _():
        pl.semaphore_wait(pair_sem, 1)

    def all_here():
        @pl.when(rank == 0)
        def _():
            pl.semaphore_wait(barrier, devices - 1)
            pl.semaphore_signal(go_sem, inc=1, device_id={"cyl": 1}, device_id_type=mesh_id)

        @pl.when(rank == 1)
        def _():
            pl.semaphore_wait(go_sem, 1)

    def start_own(s, carry):
        own_copy(s).start()
        return carry

    def start_far(n, carry):
        for d in range(1, n_cyl):
            far_copy(d, n // pieces, n % pieces).start()
        return carry

    for d in range(1, n_cyl):
        exp_copy(d).start()
    lax.fori_loop(0, pieces, start_far, 0)
    lax.fori_loop(1, stages, start_own, 0)
    lax.fori_loop(pieces, stages * pieces, start_far, 0)
    fine_copy.wait()

    own_exps.wait()
    for d in range(1, n_cyl):
        exp_copy(d).wait()
    chans = exps_ref.shape[2]
    lane = lax.broadcasted_iota(jnp.int32, (chans, own * UP), 1)
    chan = lax.broadcasted_iota(jnp.int32, (chans, own * UP), 0) - rank * own
    exps = jnp.concatenate([exps_ref[i] for i in range(n_cyl)], axis=0).astype(jnp.float32)

    def scale_of(pick):
        spread = jnp.dot(exps, pick.astype(jnp.float32), preferred_element_type=jnp.float32)
        return jnp.exp2(2.0 * spread) / (pols * blocks)

    scale = scale_of(chan == lane // UP)
    for g in range(steps):
        for o in range(n_cyl):
            scale_ref[g, o] = scale[o * per : (o + 1) * per, g * wide : (g + 1) * wide]
    lane, chan = lane[:, :wide], chan[:, :wide]
    for h in range(per):
        scale = scale_of(chan == h * share + lane % slim // UP)
        for o in range(n_cyl):
            row = scale[o * per : o * per + 1]
            for e in range(1, per):
                row = jnp.where(lane[:1] // slim == e, scale[o * per + e : o * per + e + 1], row)
            head_scale_ref[h, o] = row

    def fine_piece(s, i):
        fine = fine_ref[...]
        for d in range(1, n_cyl):
            far_arrived(d, s, i).wait()
        for c0 in range(piece):
            ch = i * piece + c0
            for p in range(pols):
                for j in range(blocks):
                    rows = jnp.concatenate(
                        [
                            held_ref[o, s, ch, c, p, j * UP : (j + 1) * UP, r * feeds : (r + 1) * feeds]
                            for o in range(n_cyl)
                            for c in range(per)
                            for r in range(2)
                        ],
                        axis=0,
                    )
                    got = jnp.dot(fine, rows, preferred_element_type=jnp.float32)
                    low, high = got[:, :half], got[:, half:]
                    both = ((low + high).astype(jnp.bfloat16), (low - high).astype(jnp.bfloat16))
                    for odd in range(2):
                        for r in range(2):
                            for e in range(cyls):
                                at = (r * cyls + e) * UP
                                mid_ref[p * blocks + j, odd, e, ch, :, r * half : (r + 1) * half] = (
                                    both[odd][at : at + UP]
                                )

    def fine_pieces(s, first, last):
        def one(i, carry):
            fine_piece(s, i)
            return carry

        lax.fori_loop(first, last, one, 0)

    def powers(beams, first, count):
        parts = []
        for odd in range(2):
            total = None
            for b in range(pols * blocks):
                block = mid_ref[b, odd, beams, first : first + count]
                spectra = lax.dot_general(
                    ns_ref[odd], block.reshape(-1, feeds), (((1,), (1,)), ((), ())),
                    preferred_element_type=jnp.float32,
                )
                squared = spectra * spectra
                power = squared[:half] + squared[half:]
                total = power if total is None else total + power
            parts.append(total)
        return parts

    def by_chip(parts, factor):
        scaled = [(part * factor).reshape(n_chan, near // 2, wide) for part in parts]
        return jnp.concatenate(scaled, axis=1).astype(jnp.bfloat16)

    def send_all(source_ref, target_ref, out_sem, in_sem):
        def send(i, carry):
            peer = lax.rem(me + 1 + i, devices)
            to = peer // n_cyl
            owner = lax.rem(peer, n_cyl)

            @pl.when(peer == me)
            def _():
                pltpu.make_async_copy(source_ref.at[owner, to], target_ref.at[me], in_sem).start()

            @pl.when(peer != me)
            def _():
                pltpu.make_async_remote_copy(
                    src_ref=source_ref.at[owner, to],
                    dst_ref=target_ref.at[me],
                    send_sem=out_sem,
                    recv_sem=in_sem,
                    device_id={"chan": to, "cyl": owner},
                    device_id_type=mesh_id,
                ).start()

            return carry

        lax.fori_loop(0, devices, send, 0)

    own_copy(0).wait()
    for h in range(per):
        fine_pieces(0, h * share // piece, (h + 1) * share // piece)
        if h == 0:
            ns_copy.wait()

        parts = powers(pl.ds(0, cyls), h * share, share)
        for o in range(n_cyl):
            head_out_ref[h, o] = by_chip(
                [part[:, o * wide : (o + 1) * wide] for part in parts], head_scale_ref[h, o]
            )
        if h == 0:
            all_here()
        send_all(head_out_ref.at[h], head_in_ref.at[h], head_send_sem, head_recv_sem.at[h])

    def one_stage(s, carry):
        own_copy(s).wait()
        fine_pieces(s, 0, pieces)

        def one_owner(owner, inner):
            parts = powers(pl.ds(owner * per, per), 0, group)
            for e in range(per):
                send_ref[s - 1, owner, :, e] = by_chip(
                    [part[:, e * wide : (e + 1) * wide] for part in parts],
                    scale_ref[s // FRAMES, owner, e : e + 1, :],
                )
            return inner

        lax.fori_loop(0, n_cyl, one_owner, 0)
        send_all(send_ref.at[s - 1], recv_ref.at[s - 1], send_sem, recv_sem.at[s - 1])
        return carry

    lax.fori_loop(1, stages, one_stage, 0)

    depth = devices * stages

    several = math.gcd(4, devices)

    def place(s, source, e, tile):
        row = (source * steps + s // FRAMES) * FRAMES + s % FRAMES
        for odd in range(2):
            at = (e * near + odd) * depth + row
            out_ref[pl.ds(at, near // 2, 2 * depth), :] = tile[odd * (near // 2) : (odd + 1) * (near // 2)]

    for h in range(per):
        pltpu.make_async_copy(head_in_ref.at[h], head_in_ref.at[h], head_recv_sem.at[h]).wait()
    slot = lax.broadcasted_iota(jnp.int32, (near, wide), 1) // slim

    def spread_head(source, carry):
        tiles = [head_in_ref[h, source].astype(jnp.float32) for h in range(per)]
        for e in range(per):
            tile = tiles[e]
            for h in range(per):
                if h != e:
                    moved = pltpu.roll(tiles[h], (h - e) * slim % wide, 1)
                    tile = jnp.where(slot == h, moved, tile)
            place(0, source, e, tile)
        return carry

    lax.fori_loop(0, devices, spread_head, 0)

    def spread_stage(s, carry):
        pltpu.make_async_copy(recv_ref.at[s - 1], recv_ref.at[s - 1], recv_sem.at[s - 1]).wait()

        def some(n, inner):
            for k in range(several):
                for e in range(per):
                    source = n * several + k
                    place(s, source, e, recv_ref[s - 1, source, e].astype(jnp.float32))
            return inner

        lax.fori_loop(0, devices // several, some, 0)
        return carry

    lax.fori_loop(1, stages, spread_stage, 0)
    for ref, sem in ((head_in_ref, head_send_sem), (recv_ref, send_sem)):
        sent = ref.at[:, : devices - 1]
        pltpu.make_async_copy(sent, sent, sem).wait()
    for d in range(1, n_cyl):
        pltpu.make_async_copy(held_ref.at[0], held_ref.at[0], volt_send_sem.at[d]).wait()


def fused(n_chan, n_cyl, volts, gain_exponents):
    chans, per, pols, times, inputs = volts.shape
    feeds = inputs // 2
    cyls = per * n_cyl
    own = chans // n_cyl
    group = 128 // UP
    steps = own // group
    stages = steps * FRAMES
    span = times // FRAMES
    blocks = span // UP
    near = feeds // n_chan
    devices = n_chan * n_cyl
    wide = group * UP
    pieces = 4
    fine = jnp.asarray(fine_rows(cyls, 1, UP)[0])
    ns = jnp.asarray(half_rows(feeds))
    operands = (volts, gain_exponents.T, fine, ns)
    dma = pltpu.SemaphoreType.DMA
    out = pl.pallas_call(
        functools.partial(fused_kernel, n_chan, n_cyl),
        out_shape=jax.ShapeDtypeStruct((per * near * devices * stages, wide), jnp.float32),
        in_specs=[pl.BlockSpec(memory_space=pltpu.HBM)] * 4,
        out_specs=pl.BlockSpec(memory_space=pltpu.VMEM),
        scratch_shapes=[
            pltpu.VMEM((n_cyl, stages, group, per, pols, span, inputs), jnp.bfloat16),
            pltpu.VMEM((pols * blocks, 2, cyls, group, UP, feeds), jnp.bfloat16),
            pltpu.VMEM((per, n_cyl, n_chan, near, wide), jnp.bfloat16),
            pltpu.VMEM((stages - 1, n_cyl, n_chan, per, near, wide), jnp.bfloat16),
            pltpu.VMEM((per, devices, near, wide), jnp.bfloat16),
            pltpu.VMEM((stages - 1, devices, per, near, wide), jnp.bfloat16),
            pltpu.VMEM((n_cyl, per, chans), jnp.int32),
            pltpu.VMEM((per, n_cyl, 1, wide), jnp.float32),
            pltpu.VMEM((steps, n_cyl, per, wide), jnp.float32),
            pltpu.VMEM(fine.shape, jnp.bfloat16),
            pltpu.VMEM(ns.shape, jnp.bfloat16),
            dma((stages,)),
            dma((n_cyl,)),
            dma((n_cyl, stages, pieces)),
            dma,
            dma((n_cyl,)),
            dma((n_cyl,)),
            dma((2,)),
            dma,
            dma((per,)),
            dma,
            dma((stages - 1,)),
            pltpu.SemaphoreType.REGULAR,
            pltpu.SemaphoreType.REGULAR,
        ],
        compiler_params=pltpu.CompilerParams(
            collective_id=0, has_side_effects=True, vmem_limit_bytes=48 * 1024 * 1024
        ),
        name="fused",
    )(*[pltpu.with_memory_space_constraint(x, pltpu.HBM) for x in operands])
    out = out.reshape(per, near, devices * steps, FRAMES, wide)
    return jnp.transpose(out, (0, 1, 3, 2, 4)).reshape(per, near, FRAMES, -1)


def fits(n_chan, n_cyl, volts):
    chans, per, pols, times, inputs = volts.shape
    own = chans // n_cyl
    feeds = inputs // 2
    return (
        n_cyl == 2
        and per in (1, 2)
        and own % (128 // UP) == 0
        and feeds % (16 * n_chan) == 0
        and feeds % 256 == 0
        and times % (FRAMES * UP) == 0
    )


def local(n_chan, n_cyl, volts, gain_exponents):
    chans, per, pols, times, inputs = volts.shape
    feeds = inputs // 2
    cyls = per * n_cyl
    own = chans // n_cyl
    group = math.gcd(8, own)
    steps = own // group
    wide = group * UP
    blocks = times // UP
    rank = lax.axis_index("cyl")
    gains = [lax.dynamic_slice_in_dim(gain_exponents, rank * own, own, 0)]
    for d in range(1, n_cyl):
        ring = [(k, (k + d) % n_cyl) for k in range(n_cyl)]
        to = (rank + d) % n_cyl
        gains.append(
            lax.ppermute(lax.dynamic_slice_in_dim(gain_exponents, to * own, own, 0), "cyl", ring)
        )
    stacked = jnp.stack(gains)
    order = (rank - jnp.arange(n_cyl, dtype=jnp.int32)) % n_cyl
    exps = jnp.take(stacked, order, axis=0)
    exps = jnp.transpose(exps, (0, 2, 1)).reshape(cyls, steps, group)
    scale = jnp.exp2(2.0 * exps.astype(jnp.float32)) / (pols * (blocks // FRAMES))
    scale = jnp.transpose(jnp.repeat(scale, UP, axis=2), (1, 0, 2))

    fine = jnp.asarray(fine_rows(cyls, n_cyl, UP))
    ns = jnp.asarray(ns_rows(feeds))
    power = pl.pallas_call(
        functools.partial(beam_kernel, cyls, n_cyl),
        out_shape=jax.ShapeDtypeStruct((steps, cyls, FRAMES, feeds, wide), jnp.bfloat16),
        grid=(steps,),
        in_specs=[
            pl.BlockSpec(memory_space=pl.ANY),
            pl.BlockSpec(fine.shape, lambda g: (0, 0, 0)),
            pl.BlockSpec(ns.shape, lambda g: (0, 0)),
            pl.BlockSpec((1, cyls, wide), lambda g: (g, 0, 0)),
        ],
        out_specs=pl.BlockSpec((1, cyls, FRAMES, feeds, wide), lambda g: (g, 0, 0, 0, 0)),
        scratch_shapes=[
            pltpu.VMEM((pols * blocks, cyls, group, UP, inputs), jnp.bfloat16),
            pltpu.VMEM((n_cyl, steps, group, per, pols, times, inputs), jnp.bfloat16),
            pltpu.SemaphoreType.DMA((steps,)),
            pltpu.SemaphoreType.DMA((n_cyl, steps)),
            pltpu.SemaphoreType.DMA((n_cyl, steps)),
        ],
        compiler_params=pltpu.CompilerParams(
            dimension_semantics=("arbitrary",), collective_id=0, has_side_effects=True
        ),
        name="beams",
    )(volts, fine, ns, scale)

    near = feeds // n_chan
    power = power.reshape(steps, n_cyl, per, FRAMES, n_chan, near, wide)
    power = jnp.transpose(power, (4, 1, 2, 3, 0, 5, 6))
    power = power.reshape(n_chan * n_cyl, per, FRAMES, steps, near, wide)
    power = lax.all_to_all(power, ("chan", "cyl"), split_axis=0, concat_axis=0, tiled=True)
    if (steps * wide) % 128 == 0:
        return spread(power)
    power = jnp.transpose(power, (1, 4, 2, 0, 3, 5))
    return power.reshape(per, near, FRAMES, -1).astype(jnp.float32)


def either(n_chan, n_cyl, volts, gain_exponents):
    if fits(n_chan, n_cyl, volts):
        return fused(n_chan, n_cyl, volts, gain_exponents)
    return local(n_chan, n_cyl, volts, gain_exponents)


def solution(mesh):
    return jax.shard_map(
        functools.partial(either, mesh.shape["chan"], mesh.shape["cyl"]),
        mesh=mesh,
        in_specs=(P("chan", "cyl", None, None, None), P("chan", "cyl")),
        out_specs=P("cyl", "chan", None, None),
        check_vma=False,
    )
```

```python
import functools
import math

import jax
import jax.numpy as jnp
import ml_dtypes
import numpy as np
from jax import lax
from jax.experimental import pallas as pl
from jax.experimental.pallas import tpu as pltpu
from jax.sharding import PartitionSpec as P

UP = 16
FRAMES = 2


def ns_rows(feeds):
    index = np.arange(feeds)
    theta = (index[None, :] * (index[:, None] - feeds // 2) % feeds) * (2.0 * math.pi / feeds)
    cosine = np.cos(theta) / math.sqrt(feeds)
    sine = np.sin(theta) / math.sqrt(feeds)
    table = np.concatenate(
        [np.concatenate([cosine, sine], axis=1), np.concatenate([-sine, cosine], axis=1)], axis=0
    )
    return table.astype(ml_dtypes.bfloat16)


def fine_rows(cyls, n_cyl, up):
    index = np.arange(up)
    theta = (index[:, None] * index[None, :] % up) * (2.0 * math.pi / up)
    rounded = lambda x: (x / math.sqrt(up)).astype(ml_dtypes.bfloat16).astype(np.float64)
    fine = rounded(np.cos(theta)) - 1j * rounded(np.sin(theta))
    cyl = np.arange(cyls)
    phase = 2.0 * math.pi * cyl[None, :] * (cyl[:, None] - (cyls - 1) / 2.0) / cyls
    weight = np.exp(-1j * phase) / 2.0
    both = np.einsum("ec,km->emck", weight, fine)
    parts = np.stack(
        [np.stack([both.real, -both.imag], axis=3), np.stack([both.imag, both.real], axis=3)], axis=0
    )
    per = cyls // n_cyl
    tables = []
    for rank in range(n_cyl):
        order = [((rank - d) % n_cyl) * per + c for d in range(n_cyl) for c in range(per)]
        tables.append(parts[:, :, :, order].reshape(2 * cyls * up, cyls * 2 * up))
    return np.stack(tables).astype(ml_dtypes.bfloat16)


def beam_kernel(
    cyls, n_cyl, volts_ref, fine_ref, ns_ref, gain_ref, out_ref,
    mid_ref, held_ref, own_sem, send_sem, recv_sem,
):
    step = pl.program_id(0)
    steps = pl.num_programs(0)
    _, _, group, per, pols, times, inputs = held_ref.shape
    feeds = inputs // 2
    blocks = times // UP
    sums = blocks // FRAMES
    rank = lax.axis_index("cyl")

    def own_copy(g):
        rows = pl.ds((rank * steps + g) * group, group)
        return pltpu.make_async_copy(volts_ref.at[rows], held_ref.at[0, g], own_sem.at[g])

    def far_copy(d, g):
        to = lax.rem(rank + d, n_cyl)
        rows = pl.ds((to * steps + g) * group, group)
        return pltpu.make_async_remote_copy(
            src_ref=volts_ref.at[rows],
            dst_ref=held_ref.at[d, g],
            send_sem=send_sem.at[d, g],
            recv_sem=recv_sem.at[d, g],
            device_id={"cyl": to},
            device_id_type=pl.DeviceIdType.MESH,
        )

    @pl.when(step == 0)
    def _():
        own_copy(0).start()
        barrier = pltpu.get_barrier_semaphore()
        for d in range(1, n_cyl):
            pl.semaphore_signal(
                barrier, inc=1, device_id={"cyl": lax.rem(rank + d, n_cyl)},
                device_id_type=pl.DeviceIdType.MESH,
            )
        pl.semaphore_wait(barrier, n_cyl - 1)

        def start(g, carry):
            for d in range(1, n_cyl):
                far_copy(d, g).start()

            @pl.when(g > 0)
            def _():
                own_copy(g).start()

            return carry

        lax.fori_loop(0, steps, start, 0)

    own_copy(step).wait()
    for d in range(1, n_cyl):
        far_copy(d, step).wait()
    volt_refs = [held_ref.at[d, step] for d in range(n_cyl)]
    fine = fine_ref[rank]

    def one_chan(ch, carry):
        for p in range(pols):
            for j in range(blocks):
                rows = jnp.concatenate(
                    [
                        ref[ch, c, p, j * UP : (j + 1) * UP, r * feeds : (r + 1) * feeds]
                        for ref in volt_refs
                        for c in range(per)
                        for r in range(2)
                    ],
                    axis=0,
                )
                got = jnp.dot(fine, rows, preferred_element_type=jnp.float32).astype(jnp.bfloat16)
                for s in range(2):
                    for e in range(cyls):
                        at = (s * cyls + e) * UP
                        mid_ref[p * blocks + j, e, ch, :, s * feeds : (s + 1) * feeds] = got[at : at + UP]
        return carry

    lax.fori_loop(0, group, one_chan, 0)
    wide = group * UP
    pair = 2 if cyls % 2 == 0 else 1
    ns = ns_ref[...]
    for q in range(FRAMES):
        for e in range(0, cyls, pair):
            total = None
            for p in range(pols):
                for j in range(q * sums, (q + 1) * sums):
                    block = mid_ref[p * blocks + j, e : e + pair].reshape(pair * wide, inputs)
                    spectra = lax.dot_general(
                        ns, block, (((1,), (1,)), ((), ())), preferred_element_type=jnp.float32
                    )
                    squared = spectra * spectra
                    power = squared[:feeds] + squared[feeds:]
                    total = power if total is None else total + power
            for i in range(pair):
                scaled = total[:, i * wide : (i + 1) * wide] * gain_ref[0, e + i : e + i + 1, :]
                out_ref[0, e + i, q] = scaled.astype(jnp.bfloat16)


def spread_kernel(in_ref, out_ref):
    sources, _, frames, steps, near, wide = in_ref.shape

    def one(source, carry):
        at = pl.multiple_of(source * (steps * wide), 128)
        for g in range(steps):
            rows = [in_ref[source, 0, q, g].astype(jnp.float32) for q in range(frames)]
            out_ref[0, :, :, pl.ds(at + g * wide, wide)] = jnp.stack(rows, axis=1)
        return carry

    lax.fori_loop(0, sources, one, 0)


def spread(power):
    sources, per, frames, steps, near, wide = power.shape
    lanes = sources * steps * wide
    return pl.pallas_call(
        spread_kernel,
        out_shape=jax.ShapeDtypeStruct((per, near, frames, lanes), jnp.float32),
        grid=(per,),
        in_specs=[pl.BlockSpec((sources, 1, frames, steps, near, wide), lambda e: (0, e, 0, 0, 0, 0))],
        out_specs=pl.BlockSpec((1, near, frames, lanes), lambda e: (e, 0, 0, 0)),
        compiler_params=pltpu.CompilerParams(dimension_semantics=("arbitrary",)),
        name="spread",
    )(power)


def half_rows(feeds):
    half = feeds // 2
    table = np.asarray(ns_rows(feeds)).reshape(2, half, 2, 2, feeds)[..., :half]
    return np.transpose(table, (2, 0, 1, 3, 4)).reshape(2, feeds, feeds)


def fused_kernel(
    n_chan, n_cyl, volts_ref, gains_ref, fine_hbm, ns_hbm, out_ref,
    held_ref, mid_ref, head_out_ref, send_ref, head_in_ref, recv_ref,
    exps_ref, head_scale_ref, scale_ref, fine_ref, ns_ref,
    own_sem, volt_send_sem, volt_recv_sem, exp_sem, exp_send_sem, exp_recv_sem, table_sem,
    head_send_sem, head_recv_sem, send_sem, recv_sem, pair_sem, go_sem,
):
    chip = lax.axis_index("chan")
    rank = lax.axis_index("cyl")
    me = chip * n_cyl + rank
    devices = n_chan * n_cyl
    _, stages, group, per, pols, times, inputs = held_ref.shape
    pieces = volt_recv_sem.shape[2]
    piece = group // pieces
    blocks = times // UP
    feeds = inputs // 2
    half = feeds // 2
    cyls = per * n_cyl
    steps = stages // FRAMES
    own = steps * group
    wide = group * UP
    near = feeds // n_chan
    share = group // per
    slim = share * UP

    def volt_rows(to, s, first, count):
        at = to * own + (s // FRAMES) * group + first
        time = pl.multiple_of((s % FRAMES) * times, times)
        return volts_ref.at[pl.ds(at, count), :, :, pl.ds(time, times), :]

    def own_copy(s):
        return pltpu.make_async_copy(volt_rows(rank, s, 0, group), held_ref.at[rank, s], own_sem.at[s])

    def far_copy(d, s, i):
        to = lax.rem(rank + d, n_cyl)
        return pltpu.make_async_remote_copy(
            src_ref=volt_rows(to, s, i * piece, piece),
            dst_ref=held_ref.at[rank, s, pl.ds(i * piece, piece)],
            send_sem=volt_send_sem.at[d],
            recv_sem=volt_recv_sem.at[d, s, i],
            device_id={"cyl": to},
            device_id_type=pl.DeviceIdType.MESH,
        )

    def far_arrived(d, s, i):
        source = lax.rem(rank + n_cyl - d, n_cyl)
        there = held_ref.at[source, s, pl.ds(i * piece, piece)]
        return pltpu.make_async_copy(there, there, volt_recv_sem.at[d, s, i])

    def exp_copy(d):
        return pltpu.make_async_remote_copy(
            src_ref=gains_ref,
            dst_ref=exps_ref.at[rank],
            send_sem=exp_send_sem.at[d],
            recv_sem=exp_recv_sem.at[d],
            device_id={"cyl": lax.rem(rank + d, n_cyl)},
            device_id_type=pl.DeviceIdType.MESH,
        )

    fine_copy = pltpu.make_async_copy(fine_hbm, fine_ref, table_sem.at[0])
    ns_copy = pltpu.make_async_copy(ns_hbm, ns_ref, table_sem.at[1])
    own_exps = pltpu.make_async_copy(gains_ref, exps_ref.at[rank], exp_sem)

    barrier = pltpu.get_barrier_semaphore()
    mesh_id = pl.DeviceIdType.MESH

    @pl.when(rank == 0)
    def _():
        pl.semaphore_signal(barrier, inc=1, device_id={"cyl": 1}, device_id_type=mesh_id)

    @pl.when(rank == 1)
    def _():
        pl.semaphore_signal(barrier, inc=1, device_id={"cyl": 0}, device_id_type=mesh_id)

    def greet(i, carry):
        to = lax.rem(chip + i, n_chan)
        pl.semaphore_signal(barrier, inc=1, device_id={"chan": to, "cyl": 0}, device_id_type=mesh_id)
        return carry

    lax.fori_loop(1, n_chan, greet, 0)
    own_copy(0).start()
    fine_copy.start()
    own_exps.start()
    ns_copy.start()

    @pl.when(rank == 1)
    def _():
        pl.semaphore_wait(barrier, 1)
        pl.semaphore_signal(pair_sem, inc=1, device_id={"cyl": 0}, device_id_type=mesh_id)

    @pl.when(rank == 0)
    def _():
        pl.semaphore_wait(pair_sem, 1)

    def all_here():
        @pl.when(rank == 0)
        def _():
            pl.semaphore_wait(barrier, devices - 1)
            pl.semaphore_signal(go_sem, inc=1, device_id={"cyl": 1}, device_id_type=mesh_id)

        @pl.when(rank == 1)
        def _():
            pl.semaphore_wait(go_sem, 1)

    def start_own(s, carry):
        own_copy(s).start()
        return carry

    def start_far(n, carry):
        for d in range(1, n_cyl):
            far_copy(d, n // pieces, n % pieces).start()
        return carry

    for d in range(1, n_cyl):
        exp_copy(d).start()
    lax.fori_loop(0, pieces, start_far, 0)
    lax.fori_loop(1, stages, start_own, 0)
    lax.fori_loop(pieces, stages * pieces, start_far, 0)
    fine_copy.wait()

    own_exps.wait()
    for d in range(1, n_cyl):
        exp_copy(d).wait()
    chans = exps_ref.shape[2]
    lane = lax.broadcasted_iota(jnp.int32, (chans, own * UP), 1)
    chan = lax.broadcasted_iota(jnp.int32, (chans, own * UP), 0) - rank * own
    exps = jnp.concatenate([exps_ref[i] for i in range(n_cyl)], axis=0).astype(jnp.float32)

    def scale_of(pick):
        spread = jnp.dot(exps, pick.astype(jnp.float32), preferred_element_type=jnp.float32)
        return jnp.exp2(2.0 * spread) / (pols * blocks)

    scale = scale_of(chan == lane // UP)
    for g in range(steps):
        for o in range(n_cyl):
            scale_ref[g, o] = scale[o * per : (o + 1) * per, g * wide : (g + 1) * wide]
    lane, chan = lane[:, :wide], chan[:, :wide]
    for h in range(per):
        scale = scale_of(chan == h * share + lane % slim // UP)
        for o in range(n_cyl):
            row = scale[o * per : o * per + 1]
            for e in range(1, per):
                row = jnp.where(lane[:1] // slim == e, scale[o * per + e : o * per + e + 1], row)
            head_scale_ref[h, o] = row

    def fine_piece(s, i):
        fine = fine_ref[...]
        for d in range(1, n_cyl):
            far_arrived(d, s, i).wait()
        for c0 in range(piece):
            ch = i * piece + c0
            for p in range(pols):
                for j in range(blocks):
                    rows = jnp.concatenate(
                        [
                            held_ref[o, s, ch, c, p, j * UP : (j + 1) * UP, r * feeds : (r + 1) * feeds]
                            for o in range(n_cyl)
                            for c in range(per)
                            for r in range(2)
                        ],
                        axis=0,
                    )
                    got = jnp.dot(fine, rows, preferred_element_type=jnp.float32)
                    low, high = got[:, :half], got[:, half:]
                    both = ((low + high).astype(jnp.bfloat16), (low - high).astype(jnp.bfloat16))
                    for odd in range(2):
                        for r in range(2):
                            for e in range(cyls):
                                at = (r * cyls + e) * UP
                                mid_ref[p * blocks + j, odd, e, ch, :, r * half : (r + 1) * half] = (
                                    both[odd][at : at + UP]
                                )

    def fine_pieces(s, first, last):
        def one(i, carry):
            fine_piece(s, i)
            return carry

        lax.fori_loop(first, last, one, 0)

    def powers(beams, first, count):
        parts = []
        for odd in range(2):
            total = None
            for b in range(pols * blocks):
                block = mid_ref[b, odd, beams, first : first + count]
                spectra = lax.dot_general(
                    ns_ref[odd], block.reshape(-1, feeds), (((1,), (1,)), ((), ())),
                    preferred_element_type=jnp.float32,
                )
                squared = spectra * spectra
                power = squared[:half] + squared[half:]
                total = power if total is None else total + power
            parts.append(total)
        return parts

    def by_chip(parts, factor):
        scaled = [(part * factor).reshape(n_chan, near // 2, wide) for part in parts]
        return jnp.concatenate(scaled, axis=1).astype(jnp.bfloat16)

    def send_all(source_ref, target_ref, out_sem, in_sem):
        for i in range(1, devices):
            turned = rank + i % n_cyl
            over = turned >= n_cyl
            owner = jnp.where(over, turned - n_cyl, turned)
            ahead = chip + jnp.where(over, i // n_cyl + 1, i // n_cyl)
            to = jnp.where(ahead >= n_chan, ahead - n_chan, ahead)
            pltpu.make_async_remote_copy(
                src_ref=source_ref.at[owner, to],
                dst_ref=target_ref.at[me],
                send_sem=out_sem,
                recv_sem=in_sem,
                device_id={"chan": to, "cyl": owner},
                device_id_type=mesh_id,
            ).start()
        pltpu.make_async_copy(source_ref.at[rank, chip], target_ref.at[me], in_sem).start()

    own_copy(0).wait()
    for h in range(per):
        fine_pieces(0, h * share // piece, (h + 1) * share // piece)
        if h == 0:
            ns_copy.wait()

        parts = powers(pl.ds(0, cyls), h * share, share)
        for o in range(n_cyl):
            head_out_ref[h, o] = by_chip(
                [part[:, o * wide : (o + 1) * wide] for part in parts], head_scale_ref[h, o]
            )
        if h == 0:
            all_here()
        send_all(head_out_ref.at[h], head_in_ref.at[h], head_send_sem, head_recv_sem.at[h])

    def one_stage(s, carry):
        own_copy(s).wait()
        fine_pieces(s, 0, pieces)

        def one_owner(owner, inner):
            parts = powers(pl.ds(owner * per, per), 0, group)
            for e in range(per):
                send_ref[s - 1, owner, :, e] = by_chip(
                    [part[:, e * wide : (e + 1) * wide] for part in parts],
                    scale_ref[s // FRAMES, owner, e : e + 1, :],
                )
            return inner

        lax.fori_loop(0, n_cyl, one_owner, 0)
        send_all(send_ref.at[s - 1], recv_ref.at[s - 1], send_sem, recv_sem.at[s - 1])
        return carry

    lax.fori_loop(1, stages, one_stage, 0)

    depth = devices * stages

    several = math.gcd(4, devices)

    def place(s, source, e, tile):
        row = (source * steps + s // FRAMES) * FRAMES + s % FRAMES
        for odd in range(2):
            at = (e * near + odd) * depth + row
            out_ref[pl.ds(at, near // 2, 2 * depth), :] = tile[odd * (near // 2) : (odd + 1) * (near // 2)]

    for h in range(per):
        pltpu.make_async_copy(head_in_ref.at[h], head_in_ref.at[h], head_recv_sem.at[h]).wait()
    slot = lax.broadcasted_iota(jnp.int32, (near, wide), 1) // slim

    def spread_head(source, carry):
        tiles = [head_in_ref[h, source].astype(jnp.float32) for h in range(per)]
        for e in range(per):
            tile = tiles[e]
            for h in range(per):
                if h != e:
                    moved = pltpu.roll(tiles[h], (h - e) * slim % wide, 1)
                    tile = jnp.where(slot == h, moved, tile)
            place(0, source, e, tile)
        return carry

    lax.fori_loop(0, devices, spread_head, 0)

    def spread_stage(s, carry):
        pltpu.make_async_copy(recv_ref.at[s - 1], recv_ref.at[s - 1], recv_sem.at[s - 1]).wait()

        def some(n, inner):
            for k in range(several):
                for e in range(per):
                    source = n * several + k
                    place(s, source, e, recv_ref[s - 1, source, e].astype(jnp.float32))
            return inner

        lax.fori_loop(0, devices // several, some, 0)
        return carry

    lax.fori_loop(1, stages, spread_stage, 0)
    for ref, sem in ((head_in_ref, head_send_sem), (recv_ref, send_sem)):
        sent = ref.at[:, : devices - 1]
        pltpu.make_async_copy(sent, sent, sem).wait()
    for d in range(1, n_cyl):
        pltpu.make_async_copy(held_ref.at[0], held_ref.at[0], volt_send_sem.at[d]).wait()


def fused(n_chan, n_cyl, volts, gain_exponents):
    chans, per, pols, times, inputs = volts.shape
    feeds = inputs // 2
    cyls = per * n_cyl
    own = chans // n_cyl
    group = 128 // UP
    steps = own // group
    stages = steps * FRAMES
    span = times // FRAMES
    blocks = span // UP
    near = feeds // n_chan
    devices = n_chan * n_cyl
    wide = group * UP
    pieces = 4
    fine = jnp.asarray(fine_rows(cyls, 1, UP)[0])
    ns = jnp.asarray(half_rows(feeds))
    operands = (volts, gain_exponents.T, fine, ns)
    dma = pltpu.SemaphoreType.DMA
    out = pl.pallas_call(
        functools.partial(fused_kernel, n_chan, n_cyl),
        out_shape=jax.ShapeDtypeStruct((per * near * devices * stages, wide), jnp.float32),
        in_specs=[pl.BlockSpec(memory_space=pltpu.HBM)] * 4,
        out_specs=pl.BlockSpec(memory_space=pltpu.VMEM),
        scratch_shapes=[
            pltpu.VMEM((n_cyl, stages, group, per, pols, span, inputs), jnp.bfloat16),
            pltpu.VMEM((pols * blocks, 2, cyls, group, UP, feeds), jnp.bfloat16),
            pltpu.VMEM((per, n_cyl, n_chan, near, wide), jnp.bfloat16),
            pltpu.VMEM((stages - 1, n_cyl, n_chan, per, near, wide), jnp.bfloat16),
            pltpu.VMEM((per, devices, near, wide), jnp.bfloat16),
            pltpu.VMEM((stages - 1, devices, per, near, wide), jnp.bfloat16),
            pltpu.VMEM((n_cyl, per, chans), jnp.int32),
            pltpu.VMEM((per, n_cyl, 1, wide), jnp.float32),
            pltpu.VMEM((steps, n_cyl, per, wide), jnp.float32),
            pltpu.VMEM(fine.shape, jnp.bfloat16),
            pltpu.VMEM(ns.shape, jnp.bfloat16),
            dma((stages,)),
            dma((n_cyl,)),
            dma((n_cyl, stages, pieces)),
            dma,
            dma((n_cyl,)),
            dma((n_cyl,)),
            dma((2,)),
            dma,
            dma((per,)),
            dma,
            dma((stages - 1,)),
            pltpu.SemaphoreType.REGULAR,
            pltpu.SemaphoreType.REGULAR,
        ],
        compiler_params=pltpu.CompilerParams(
            collective_id=0, has_side_effects=True, vmem_limit_bytes=48 * 1024 * 1024
        ),
        name="fused",
    )(*[pltpu.with_memory_space_constraint(x, pltpu.HBM) for x in operands])
    out = out.reshape(per, near, devices * steps, FRAMES, wide)
    return jnp.transpose(out, (0, 1, 3, 2, 4)).reshape(per, near, FRAMES, -1)


def fits(n_chan, n_cyl, volts):
    chans, per, pols, times, inputs = volts.shape
    own = chans // n_cyl
    feeds = inputs // 2
    return (
        n_cyl == 2
        and per in (1, 2)
        and own % (128 // UP) == 0
        and feeds % (16 * n_chan) == 0
        and feeds % 256 == 0
        and times % (FRAMES * UP) == 0
    )


def local(n_chan, n_cyl, volts, gain_exponents):
    chans, per, pols, times, inputs = volts.shape
    feeds = inputs // 2
    cyls = per * n_cyl
    own = chans // n_cyl
    group = math.gcd(8, own)
    steps = own // group
    wide = group * UP
    blocks = times // UP
    rank = lax.axis_index("cyl")
    gains = [lax.dynamic_slice_in_dim(gain_exponents, rank * own, own, 0)]
    for d in range(1, n_cyl):
        ring = [(k, (k + d) % n_cyl) for k in range(n_cyl)]
        to = (rank + d) % n_cyl
        gains.append(
            lax.ppermute(lax.dynamic_slice_in_dim(gain_exponents, to * own, own, 0), "cyl", ring)
        )
    stacked = jnp.stack(gains)
    order = (rank - jnp.arange(n_cyl, dtype=jnp.int32)) % n_cyl
    exps = jnp.take(stacked, order, axis=0)
    exps = jnp.transpose(exps, (0, 2, 1)).reshape(cyls, steps, group)
    scale = jnp.exp2(2.0 * exps.astype(jnp.float32)) / (pols * (blocks // FRAMES))
    scale = jnp.transpose(jnp.repeat(scale, UP, axis=2), (1, 0, 2))

    fine = jnp.asarray(fine_rows(cyls, n_cyl, UP))
    ns = jnp.asarray(ns_rows(feeds))
    power = pl.pallas_call(
        functools.partial(beam_kernel, cyls, n_cyl),
        out_shape=jax.ShapeDtypeStruct((steps, cyls, FRAMES, feeds, wide), jnp.bfloat16),
        grid=(steps,),
        in_specs=[
            pl.BlockSpec(memory_space=pl.ANY),
            pl.BlockSpec(fine.shape, lambda g: (0, 0, 0)),
            pl.BlockSpec(ns.shape, lambda g: (0, 0)),
            pl.BlockSpec((1, cyls, wide), lambda g: (g, 0, 0)),
        ],
        out_specs=pl.BlockSpec((1, cyls, FRAMES, feeds, wide), lambda g: (g, 0, 0, 0, 0)),
        scratch_shapes=[
            pltpu.VMEM((pols * blocks, cyls, group, UP, inputs), jnp.bfloat16),
            pltpu.VMEM((n_cyl, steps, group, per, pols, times, inputs), jnp.bfloat16),
            pltpu.SemaphoreType.DMA((steps,)),
            pltpu.SemaphoreType.DMA((n_cyl, steps)),
            pltpu.SemaphoreType.DMA((n_cyl, steps)),
        ],
        compiler_params=pltpu.CompilerParams(
            dimension_semantics=("arbitrary",), collective_id=0, has_side_effects=True
        ),
        name="beams",
    )(volts, fine, ns, scale)

    near = feeds // n_chan
    power = power.reshape(steps, n_cyl, per, FRAMES, n_chan, near, wide)
    power = jnp.transpose(power, (4, 1, 2, 3, 0, 5, 6))
    power = power.reshape(n_chan * n_cyl, per, FRAMES, steps, near, wide)
    power = lax.all_to_all(power, ("chan", "cyl"), split_axis=0, concat_axis=0, tiled=True)
    if (steps * wide) % 128 == 0:
        return spread(power)
    power = jnp.transpose(power, (1, 4, 2, 0, 3, 5))
    return power.reshape(per, near, FRAMES, -1).astype(jnp.float32)


def either(n_chan, n_cyl, volts, gain_exponents):
    if fits(n_chan, n_cyl, volts):
        return fused(n_chan, n_cyl, volts, gain_exponents)
    return local(n_chan, n_cyl, volts, gain_exponents)


def solution(mesh):
    return jax.shard_map(
        functools.partial(either, mesh.shape["chan"], mesh.shape["cyl"]),
        mesh=mesh,
        in_specs=(P("chan", "cyl", None, None, None), P("chan", "cyl")),
        out_specs=P("cyl", "chan", None, None),
        check_vma=False,
    )
```

```python
import functools
import math

import jax
import jax.numpy as jnp
import ml_dtypes
import numpy as np
from jax import lax
from jax.experimental import pallas as pl
from jax.experimental.pallas import tpu as pltpu
from jax.sharding import PartitionSpec as P

UP = 16
FRAMES = 2


def ns_rows(feeds):
    index = np.arange(feeds)
    theta = (index[None, :] * (index[:, None] - feeds // 2) % feeds) * (2.0 * math.pi / feeds)
    cosine = np.cos(theta) / math.sqrt(feeds)
    sine = np.sin(theta) / math.sqrt(feeds)
    table = np.concatenate(
        [np.concatenate([cosine, sine], axis=1), np.concatenate([-sine, cosine], axis=1)], axis=0
    )
    return table.astype(ml_dtypes.bfloat16)


def fine_rows(cyls, n_cyl, up):
    index = np.arange(up)
    theta = (index[:, None] * index[None, :] % up) * (2.0 * math.pi / up)
    rounded = lambda x: (x / math.sqrt(up)).astype(ml_dtypes.bfloat16).astype(np.float64)
    fine = rounded(np.cos(theta)) - 1j * rounded(np.sin(theta))
    cyl = np.arange(cyls)
    phase = 2.0 * math.pi * cyl[None, :] * (cyl[:, None] - (cyls - 1) / 2.0) / cyls
    weight = np.exp(-1j * phase) / 2.0
    both = np.einsum("ec,km->emck", weight, fine)
    parts = np.stack(
        [np.stack([both.real, -both.imag], axis=3), np.stack([both.imag, both.real], axis=3)], axis=0
    )
    per = cyls // n_cyl
    tables = []
    for rank in range(n_cyl):
        order = [((rank - d) % n_cyl) * per + c for d in range(n_cyl) for c in range(per)]
        tables.append(parts[:, :, :, order].reshape(2 * cyls * up, cyls * 2 * up))
    return np.stack(tables).astype(ml_dtypes.bfloat16)


def beam_kernel(
    cyls, n_cyl, volts_ref, fine_ref, ns_ref, gain_ref, out_ref,
    mid_ref, held_ref, own_sem, send_sem, recv_sem,
):
    step = pl.program_id(0)
    steps = pl.num_programs(0)
    _, _, group, per, pols, times, inputs = held_ref.shape
    feeds = inputs // 2
    blocks = times // UP
    sums = blocks // FRAMES
    rank = lax.axis_index("cyl")

    def own_copy(g):
        rows = pl.ds((rank * steps + g) * group, group)
        return pltpu.make_async_copy(volts_ref.at[rows], held_ref.at[0, g], own_sem.at[g])

    def far_copy(d, g):
        to = lax.rem(rank + d, n_cyl)
        rows = pl.ds((to * steps + g) * group, group)
        return pltpu.make_async_remote_copy(
            src_ref=volts_ref.at[rows],
            dst_ref=held_ref.at[d, g],
            send_sem=send_sem.at[d, g],
            recv_sem=recv_sem.at[d, g],
            device_id={"cyl": to},
            device_id_type=pl.DeviceIdType.MESH,
        )

    @pl.when(step == 0)
    def _():
        own_copy(0).start()
        barrier = pltpu.get_barrier_semaphore()
        for d in range(1, n_cyl):
            pl.semaphore_signal(
                barrier, inc=1, device_id={"cyl": lax.rem(rank + d, n_cyl)},
                device_id_type=pl.DeviceIdType.MESH,
            )
        pl.semaphore_wait(barrier, n_cyl - 1)

        def start(g, carry):
            for d in range(1, n_cyl):
                far_copy(d, g).start()

            @pl.when(g > 0)
            def _():
                own_copy(g).start()

            return carry

        lax.fori_loop(0, steps, start, 0)

    own_copy(step).wait()
    for d in range(1, n_cyl):
        far_copy(d, step).wait()
    volt_refs = [held_ref.at[d, step] for d in range(n_cyl)]
    fine = fine_ref[rank]

    def one_chan(ch, carry):
        for p in range(pols):
            for j in range(blocks):
                rows = jnp.concatenate(
                    [
                        ref[ch, c, p, j * UP : (j + 1) * UP, r * feeds : (r + 1) * feeds]
                        for ref in volt_refs
                        for c in range(per)
                        for r in range(2)
                    ],
                    axis=0,
                )
                got = jnp.dot(fine, rows, preferred_element_type=jnp.float32).astype(jnp.bfloat16)
                for s in range(2):
                    for e in range(cyls):
                        at = (s * cyls + e) * UP
                        mid_ref[p * blocks + j, e, ch, :, s * feeds : (s + 1) * feeds] = got[at : at + UP]
        return carry

    lax.fori_loop(0, group, one_chan, 0)
    wide = group * UP
    pair = 2 if cyls % 2 == 0 else 1
    ns = ns_ref[...]
    for q in range(FRAMES):
        for e in range(0, cyls, pair):
            total = None
            for p in range(pols):
                for j in range(q * sums, (q + 1) * sums):
                    block = mid_ref[p * blocks + j, e : e + pair].reshape(pair * wide, inputs)
                    spectra = lax.dot_general(
                        ns, block, (((1,), (1,)), ((), ())), preferred_element_type=jnp.float32
                    )
                    squared = spectra * spectra
                    power = squared[:feeds] + squared[feeds:]
                    total = power if total is None else total + power
            for i in range(pair):
                scaled = total[:, i * wide : (i + 1) * wide] * gain_ref[0, e + i : e + i + 1, :]
                out_ref[0, e + i, q] = scaled.astype(jnp.bfloat16)


def spread_kernel(in_ref, out_ref):
    sources, _, frames, steps, near, wide = in_ref.shape

    def one(source, carry):
        at = pl.multiple_of(source * (steps * wide), 128)
        for g in range(steps):
            rows = [in_ref[source, 0, q, g].astype(jnp.float32) for q in range(frames)]
            out_ref[0, :, :, pl.ds(at + g * wide, wide)] = jnp.stack(rows, axis=1)
        return carry

    lax.fori_loop(0, sources, one, 0)


def spread(power):
    sources, per, frames, steps, near, wide = power.shape
    lanes = sources * steps * wide
    return pl.pallas_call(
        spread_kernel,
        out_shape=jax.ShapeDtypeStruct((per, near, frames, lanes), jnp.float32),
        grid=(per,),
        in_specs=[pl.BlockSpec((sources, 1, frames, steps, near, wide), lambda e: (0, e, 0, 0, 0, 0))],
        out_specs=pl.BlockSpec((1, near, frames, lanes), lambda e: (e, 0, 0, 0)),
        compiler_params=pltpu.CompilerParams(dimension_semantics=("arbitrary",)),
        name="spread",
    )(power)


def half_rows(feeds):
    half = feeds // 2
    table = np.asarray(ns_rows(feeds)).reshape(2, half, 2, 2, feeds)[..., :half]
    return np.transpose(table, (2, 0, 1, 3, 4)).reshape(2, feeds, feeds)


def fused_kernel(
    n_chan, n_cyl, volts_ref, gains_ref, fine_hbm, ns_hbm, out_ref,
    held_ref, mid_ref, head_out_ref, send_ref, head_in_ref, recv_ref,
    exps_ref, head_scale_ref, scale_ref, fine_ref, ns_ref,
    own_sem, volt_send_sem, volt_recv_sem, exp_sem, exp_send_sem, exp_recv_sem, table_sem,
    head_send_sem, head_recv_sem, send_sem, recv_sem, pair_sem, go_sem,
):
    chip = lax.axis_index("chan")
    rank = lax.axis_index("cyl")
    me = chip * n_cyl + rank
    devices = n_chan * n_cyl
    _, stages, group, per, pols, times, inputs = held_ref.shape
    pieces = volt_recv_sem.shape[2]
    piece = group // pieces
    blocks = times // UP
    feeds = inputs // 2
    half = feeds // 2
    cyls = per * n_cyl
    steps = stages // FRAMES
    own = steps * group
    wide = group * UP
    near = feeds // n_chan
    share = group // per
    slim = share * UP

    def volt_rows(to, s, first, count):
        at = to * own + (s // FRAMES) * group + first
        time = pl.multiple_of((s % FRAMES) * times, times)
        return volts_ref.at[pl.ds(at, count), :, :, pl.ds(time, times), :]

    def own_copy(s):
        return pltpu.make_async_copy(volt_rows(rank, s, 0, group), held_ref.at[rank, s], own_sem.at[s])

    def far_copy(d, s, i):
        to = lax.rem(rank + d, n_cyl)
        return pltpu.make_async_remote_copy(
            src_ref=volt_rows(to, s, i * piece, piece),
            dst_ref=held_ref.at[rank, s, pl.ds(i * piece, piece)],
            send_sem=volt_send_sem.at[d],
            recv_sem=volt_recv_sem.at[d, s, i],
            device_id={"cyl": to},
            device_id_type=pl.DeviceIdType.MESH,
        )

    def far_arrived(d, s, i):
        source = lax.rem(rank + n_cyl - d, n_cyl)
        there = held_ref.at[source, s, pl.ds(i * piece, piece)]
        return pltpu.make_async_copy(there, there, volt_recv_sem.at[d, s, i])

    def exp_copy(d):
        return pltpu.make_async_remote_copy(
            src_ref=gains_ref,
            dst_ref=exps_ref.at[rank],
            send_sem=exp_send_sem.at[d],
            recv_sem=exp_recv_sem.at[d],
            device_id={"cyl": lax.rem(rank + d, n_cyl)},
            device_id_type=pl.DeviceIdType.MESH,
        )

    fine_copy = pltpu.make_async_copy(fine_hbm, fine_ref, table_sem.at[0])
    ns_copy = pltpu.make_async_copy(ns_hbm, ns_ref, table_sem.at[1])
    own_exps = pltpu.make_async_copy(gains_ref, exps_ref.at[rank], exp_sem)

    barrier = pltpu.get_barrier_semaphore()
    mesh_id = pl.DeviceIdType.MESH

    lead = n_cyl - 1

    @pl.when(rank == lead)
    def _():
        pl.semaphore_signal(barrier, inc=1, device_id={"cyl": 0}, device_id_type=mesh_id)

    @pl.when(rank != lead)
    def _():
        pl.semaphore_signal(barrier, inc=1, device_id={"cyl": lead}, device_id_type=mesh_id)

    def greet(i, carry):
        to = lax.rem(chip + i, n_chan)
        pl.semaphore_signal(barrier, inc=1, device_id={"chan": to, "cyl": lead}, device_id_type=mesh_id)
        return carry

    lax.fori_loop(1, n_chan, greet, 0)
    own_copy(0).start()
    fine_copy.start()
    own_exps.start()
    ns_copy.start()

    @pl.when(rank != lead)
    def _():
        pl.semaphore_wait(barrier, 1)
        pl.semaphore_signal(pair_sem, inc=1, device_id={"cyl": lead}, device_id_type=mesh_id)

    @pl.when(rank == lead)
    def _():
        pl.semaphore_wait(pair_sem, 1)

    def all_here():
        @pl.when(rank == lead)
        def _():
            pl.semaphore_wait(barrier, devices - 1)
            pl.semaphore_signal(go_sem, inc=1, device_id={"cyl": 0}, device_id_type=mesh_id)

        @pl.when(rank != lead)
        def _():
            pl.semaphore_wait(go_sem, 1)

    def start_own(s, carry):
        own_copy(s).start()
        return carry

    def start_far(n, carry):
        for d in range(1, n_cyl):
            far_copy(d, n // pieces, n % pieces).start()
        return carry

    for d in range(1, n_cyl):
        exp_copy(d).start()
    lax.fori_loop(0, pieces, start_far, 0)
    lax.fori_loop(1, stages, start_own, 0)
    lax.fori_loop(pieces, stages * pieces, start_far, 0)
    fine_copy.wait()

    own_exps.wait()
    for d in range(1, n_cyl):
        exp_copy(d).wait()
    chans = exps_ref.shape[2]
    lane = lax.broadcasted_iota(jnp.int32, (chans, own * UP), 1)
    chan = lax.broadcasted_iota(jnp.int32, (chans, own * UP), 0) - rank * own
    exps = jnp.concatenate([exps_ref[i] for i in range(n_cyl)], axis=0).astype(jnp.float32)

    def scale_of(pick):
        spread = jnp.dot(exps, pick.astype(jnp.float32), preferred_element_type=jnp.float32)
        return jnp.exp2(2.0 * spread) / (pols * blocks)

    scale = scale_of(chan == lane // UP)
    for g in range(steps):
        for o in range(n_cyl):
            scale_ref[g, o] = scale[o * per : (o + 1) * per, g * wide : (g + 1) * wide]
    lane, chan = lane[:, :wide], chan[:, :wide]
    for h in range(per):
        scale = scale_of(chan == h * share + lane % slim // UP)
        for o in range(n_cyl):
            row = scale[o * per : o * per + 1]
            for e in range(1, per):
                row = jnp.where(lane[:1] // slim == e, scale[o * per + e : o * per + e + 1], row)
            head_scale_ref[h, o] = row

    def fine_piece(s, i):
        fine = fine_ref[...]
        for d in range(1, n_cyl):
            far_arrived(d, s, i).wait()
        for c0 in range(piece):
            ch = i * piece + c0
            for p in range(pols):
                for j in range(blocks):
                    rows = jnp.concatenate(
                        [
                            held_ref[o, s, ch, c, p, j * UP : (j + 1) * UP, r * feeds : (r + 1) * feeds]
                            for o in range(n_cyl)
                            for c in range(per)
                            for r in range(2)
                        ],
                        axis=0,
                    )
                    got = jnp.dot(fine, rows, preferred_element_type=jnp.float32)
                    low, high = got[:, :half], got[:, half:]
                    both = ((low + high).astype(jnp.bfloat16), (low - high).astype(jnp.bfloat16))
                    for odd in range(2):
                        for r in range(2):
                            for e in range(cyls):
                                at = (r * cyls + e) * UP
                                mid_ref[p * blocks + j, odd, e, ch, :, r * half : (r + 1) * half] = (
                                    both[odd][at : at + UP]
                                )

    def fine_pieces(s, first, last):
        def one(i, carry):
            fine_piece(s, i)
            return carry

        lax.fori_loop(first, last, one, 0)

    def powers(beams, first, count):
        parts = []
        for odd in range(2):
            total = None
            for b in range(pols * blocks):
                block = mid_ref[b, odd, beams, first : first + count]
                spectra = lax.dot_general(
                    ns_ref[odd], block.reshape(-1, feeds), (((1,), (1,)), ((), ())),
                    preferred_element_type=jnp.float32,
                )
                squared = spectra * spectra
                power = squared[:half] + squared[half:]
                total = power if total is None else total + power
            parts.append(total)
        return parts

    def by_chip(parts, factor):
        scaled = [(part * factor).reshape(n_chan, near // 2, wide) for part in parts]
        return jnp.concatenate(scaled, axis=1).astype(jnp.bfloat16)

    def send_all(source_ref, target_ref, out_sem, in_sem):
        for i in range(1, devices):
            turned = rank + i % n_cyl
            over = turned >= n_cyl
            owner = jnp.where(over, turned - n_cyl, turned)
            ahead = chip + jnp.where(over, i // n_cyl + 1, i // n_cyl)
            to = jnp.where(ahead >= n_chan, ahead - n_chan, ahead)
            pltpu.make_async_remote_copy(
                src_ref=source_ref.at[owner, to],
                dst_ref=target_ref.at[me],
                send_sem=out_sem,
                recv_sem=in_sem,
                device_id={"chan": to, "cyl": owner},
                device_id_type=mesh_id,
            ).start()
        pltpu.make_async_copy(source_ref.at[rank, chip], target_ref.at[me], in_sem).start()

    own_copy(0).wait()
    for h in range(per):
        fine_pieces(0, h * share // piece, (h + 1) * share // piece)
        if h == 0:
            ns_copy.wait()

        parts = powers(pl.ds(0, cyls), h * share, share)
        for o in range(n_cyl):
            head_out_ref[h, o] = by_chip(
                [part[:, o * wide : (o + 1) * wide] for part in parts], head_scale_ref[h, o]
            )
        if h == 0:
            all_here()
        send_all(head_out_ref.at[h], head_in_ref.at[h], head_send_sem, head_recv_sem.at[h])

    def one_stage(s, carry):
        own_copy(s).wait()
        fine_pieces(s, 0, pieces)

        def one_owner(owner, inner):
            parts = powers(pl.ds(owner * per, per), 0, group)
            for e in range(per):
                send_ref[s - 1, owner, :, e] = by_chip(
                    [part[:, e * wide : (e + 1) * wide] for part in parts],
                    scale_ref[s // FRAMES, owner, e : e + 1, :],
                )
            return inner

        lax.fori_loop(0, n_cyl, one_owner, 0)
        send_all(send_ref.at[s - 1], recv_ref.at[s - 1], send_sem, recv_sem.at[s - 1])
        return carry

    lax.fori_loop(1, stages, one_stage, 0)

    depth = devices * stages

    several = math.gcd(4, devices)

    def place(s, source, e, tile):
        row = (source * steps + s // FRAMES) * FRAMES + s % FRAMES
        for odd in range(2):
            at = (e * near + odd) * depth + row
            out_ref[pl.ds(at, near // 2, 2 * depth), :] = tile[odd * (near // 2) : (odd + 1) * (near // 2)]

    for h in range(per):
        pltpu.make_async_copy(head_in_ref.at[h], head_in_ref.at[h], head_recv_sem.at[h]).wait()
    slot = lax.broadcasted_iota(jnp.int32, (near, wide), 1) // slim

    def spread_head(source, carry):
        tiles = [head_in_ref[h, source].astype(jnp.float32) for h in range(per)]
        for e in range(per):
            tile = tiles[e]
            for h in range(per):
                if h != e:
                    moved = pltpu.roll(tiles[h], (h - e) * slim % wide, 1)
                    tile = jnp.where(slot == h, moved, tile)
            place(0, source, e, tile)
        return carry

    lax.fori_loop(0, devices, spread_head, 0)

    def spread_stage(s, carry):
        pltpu.make_async_copy(recv_ref.at[s - 1], recv_ref.at[s - 1], recv_sem.at[s - 1]).wait()

        def some(n, inner):
            for k in range(several):
                for e in range(per):
                    source = n * several + k
                    place(s, source, e, recv_ref[s - 1, source, e].astype(jnp.float32))
            return inner

        lax.fori_loop(0, devices // several, some, 0)
        return carry

    lax.fori_loop(1, stages, spread_stage, 0)
    for ref, sem in ((head_in_ref, head_send_sem), (recv_ref, send_sem)):
        sent = ref.at[:, : devices - 1]
        pltpu.make_async_copy(sent, sent, sem).wait()
    for d in range(1, n_cyl):
        pltpu.make_async_copy(held_ref.at[0], held_ref.at[0], volt_send_sem.at[d]).wait()


def fused(n_chan, n_cyl, volts, gain_exponents):
    chans, per, pols, times, inputs = volts.shape
    feeds = inputs // 2
    cyls = per * n_cyl
    own = chans // n_cyl
    group = 128 // UP
    steps = own // group
    stages = steps * FRAMES
    span = times // FRAMES
    blocks = span // UP
    near = feeds // n_chan
    devices = n_chan * n_cyl
    wide = group * UP
    pieces = 4
    fine = jnp.asarray(fine_rows(cyls, 1, UP)[0])
    ns = jnp.asarray(half_rows(feeds))
    operands = (volts, gain_exponents.T, fine, ns)
    dma = pltpu.SemaphoreType.DMA
    out = pl.pallas_call(
        functools.partial(fused_kernel, n_chan, n_cyl),
        out_shape=jax.ShapeDtypeStruct((per * near * devices * stages, wide), jnp.float32),
        in_specs=[pl.BlockSpec(memory_space=pltpu.HBM)] * 4,
        out_specs=pl.BlockSpec(memory_space=pltpu.VMEM),
        scratch_shapes=[
            pltpu.VMEM((n_cyl, stages, group, per, pols, span, inputs), jnp.bfloat16),
            pltpu.VMEM((pols * blocks, 2, cyls, group, UP, feeds), jnp.bfloat16),
            pltpu.VMEM((per, n_cyl, n_chan, near, wide), jnp.bfloat16),
            pltpu.VMEM((stages - 1, n_cyl, n_chan, per, near, wide), jnp.bfloat16),
            pltpu.VMEM((per, devices, near, wide), jnp.bfloat16),
            pltpu.VMEM((stages - 1, devices, per, near, wide), jnp.bfloat16),
            pltpu.VMEM((n_cyl, per, chans), jnp.int32),
            pltpu.VMEM((per, n_cyl, 1, wide), jnp.float32),
            pltpu.VMEM((steps, n_cyl, per, wide), jnp.float32),
            pltpu.VMEM(fine.shape, jnp.bfloat16),
            pltpu.VMEM(ns.shape, jnp.bfloat16),
            dma((stages,)),
            dma((n_cyl,)),
            dma((n_cyl, stages, pieces)),
            dma,
            dma((n_cyl,)),
            dma((n_cyl,)),
            dma((2,)),
            dma,
            dma((per,)),
            dma,
            dma((stages - 1,)),
            pltpu.SemaphoreType.REGULAR,
            pltpu.SemaphoreType.REGULAR,
        ],
        compiler_params=pltpu.CompilerParams(
            collective_id=0, has_side_effects=True, vmem_limit_bytes=48 * 1024 * 1024
        ),
        name="fused",
    )(*[pltpu.with_memory_space_constraint(x, pltpu.HBM) for x in operands])
    out = out.reshape(per, near, devices * steps, FRAMES, wide)
    return jnp.transpose(out, (0, 1, 3, 2, 4)).reshape(per, near, FRAMES, -1)


def fits(n_chan, n_cyl, volts):
    chans, per, pols, times, inputs = volts.shape
    own = chans // n_cyl
    feeds = inputs // 2
    return (
        n_cyl == 2
        and per in (1, 2)
        and own % (128 // UP) == 0
        and feeds % (16 * n_chan) == 0
        and feeds % 256 == 0
        and times % (FRAMES * UP) == 0
    )


def local(n_chan, n_cyl, volts, gain_exponents):
    chans, per, pols, times, inputs = volts.shape
    feeds = inputs // 2
    cyls = per * n_cyl
    own = chans // n_cyl
    group = math.gcd(8, own)
    steps = own // group
    wide = group * UP
    blocks = times // UP
    rank = lax.axis_index("cyl")
    gains = [lax.dynamic_slice_in_dim(gain_exponents, rank * own, own, 0)]
    for d in range(1, n_cyl):
        ring = [(k, (k + d) % n_cyl) for k in range(n_cyl)]
        to = (rank + d) % n_cyl
        gains.append(
            lax.ppermute(lax.dynamic_slice_in_dim(gain_exponents, to * own, own, 0), "cyl", ring)
        )
    stacked = jnp.stack(gains)
    order = (rank - jnp.arange(n_cyl, dtype=jnp.int32)) % n_cyl
    exps = jnp.take(stacked, order, axis=0)
    exps = jnp.transpose(exps, (0, 2, 1)).reshape(cyls, steps, group)
    scale = jnp.exp2(2.0 * exps.astype(jnp.float32)) / (pols * (blocks // FRAMES))
    scale = jnp.transpose(jnp.repeat(scale, UP, axis=2), (1, 0, 2))

    fine = jnp.asarray(fine_rows(cyls, n_cyl, UP))
    ns = jnp.asarray(ns_rows(feeds))
    power = pl.pallas_call(
        functools.partial(beam_kernel, cyls, n_cyl),
        out_shape=jax.ShapeDtypeStruct((steps, cyls, FRAMES, feeds, wide), jnp.bfloat16),
        grid=(steps,),
        in_specs=[
            pl.BlockSpec(memory_space=pl.ANY),
            pl.BlockSpec(fine.shape, lambda g: (0, 0, 0)),
            pl.BlockSpec(ns.shape, lambda g: (0, 0)),
            pl.BlockSpec((1, cyls, wide), lambda g: (g, 0, 0)),
        ],
        out_specs=pl.BlockSpec((1, cyls, FRAMES, feeds, wide), lambda g: (g, 0, 0, 0, 0)),
        scratch_shapes=[
            pltpu.VMEM((pols * blocks, cyls, group, UP, inputs), jnp.bfloat16),
            pltpu.VMEM((n_cyl, steps, group, per, pols, times, inputs), jnp.bfloat16),
            pltpu.SemaphoreType.DMA((steps,)),
            pltpu.SemaphoreType.DMA((n_cyl, steps)),
            pltpu.SemaphoreType.DMA((n_cyl, steps)),
        ],
        compiler_params=pltpu.CompilerParams(
            dimension_semantics=("arbitrary",), collective_id=0, has_side_effects=True
        ),
        name="beams",
    )(volts, fine, ns, scale)

    near = feeds // n_chan
    power = power.reshape(steps, n_cyl, per, FRAMES, n_chan, near, wide)
    power = jnp.transpose(power, (4, 1, 2, 3, 0, 5, 6))
    power = power.reshape(n_chan * n_cyl, per, FRAMES, steps, near, wide)
    power = lax.all_to_all(power, ("chan", "cyl"), split_axis=0, concat_axis=0, tiled=True)
    if (steps * wide) % 128 == 0:
        return spread(power)
    power = jnp.transpose(power, (1, 4, 2, 0, 3, 5))
    return power.reshape(per, near, FRAMES, -1).astype(jnp.float32)


def either(n_chan, n_cyl, volts, gain_exponents):
    if fits(n_chan, n_cyl, volts):
        return fused(n_chan, n_cyl, volts, gain_exponents)
    return local(n_chan, n_cyl, volts, gain_exponents)


def solution(mesh):
    return jax.shard_map(
        functools.partial(either, mesh.shape["chan"], mesh.shape["cyl"]),
        mesh=mesh,
        in_specs=(P("chan", "cyl", None, None, None), P("chan", "cyl")),
        out_specs=P("cyl", "chan", None, None),
        check_vma=False,
    )
```

```python
import functools
import math

import jax
import jax.numpy as jnp
import ml_dtypes
import numpy as np
from jax import lax
from jax.experimental import pallas as pl
from jax.experimental.pallas import tpu as pltpu
from jax.sharding import PartitionSpec as P

UP = 16
FRAMES = 2


def ns_rows(feeds):
    index = np.arange(feeds)
    theta = (index[None, :] * (index[:, None] - feeds // 2) % feeds) * (2.0 * math.pi / feeds)
    cosine = np.cos(theta) / math.sqrt(feeds)
    sine = np.sin(theta) / math.sqrt(feeds)
    table = np.concatenate(
        [np.concatenate([cosine, sine], axis=1), np.concatenate([-sine, cosine], axis=1)], axis=0
    )
    return table.astype(ml_dtypes.bfloat16)


def fine_rows(cyls, n_cyl, up):
    index = np.arange(up)
    theta = (index[:, None] * index[None, :] % up) * (2.0 * math.pi / up)
    rounded = lambda x: (x / math.sqrt(up)).astype(ml_dtypes.bfloat16).astype(np.float64)
    fine = rounded(np.cos(theta)) - 1j * rounded(np.sin(theta))
    cyl = np.arange(cyls)
    phase = 2.0 * math.pi * cyl[None, :] * (cyl[:, None] - (cyls - 1) / 2.0) / cyls
    weight = np.exp(-1j * phase) / 2.0
    both = np.einsum("ec,km->emck", weight, fine)
    parts = np.stack(
        [np.stack([both.real, -both.imag], axis=3), np.stack([both.imag, both.real], axis=3)], axis=0
    )
    per = cyls // n_cyl
    tables = []
    for rank in range(n_cyl):
        order = [((rank - d) % n_cyl) * per + c for d in range(n_cyl) for c in range(per)]
        tables.append(parts[:, :, :, order].reshape(2 * cyls * up, cyls * 2 * up))
    return np.stack(tables).astype(ml_dtypes.bfloat16)


def beam_kernel(
    cyls, n_cyl, volts_ref, fine_ref, ns_ref, gain_ref, out_ref,
    mid_ref, held_ref, own_sem, send_sem, recv_sem,
):
    step = pl.program_id(0)
    steps = pl.num_programs(0)
    _, _, group, per, pols, times, inputs = held_ref.shape
    feeds = inputs // 2
    blocks = times // UP
    sums = blocks // FRAMES
    rank = lax.axis_index("cyl")

    def own_copy(g):
        rows = pl.ds((rank * steps + g) * group, group)
        return pltpu.make_async_copy(volts_ref.at[rows], held_ref.at[0, g], own_sem.at[g])

    def far_copy(d, g):
        to = lax.rem(rank + d, n_cyl)
        rows = pl.ds((to * steps + g) * group, group)
        return pltpu.make_async_remote_copy(
            src_ref=volts_ref.at[rows],
            dst_ref=held_ref.at[d, g],
            send_sem=send_sem.at[d, g],
            recv_sem=recv_sem.at[d, g],
            device_id={"cyl": to},
            device_id_type=pl.DeviceIdType.MESH,
        )

    @pl.when(step == 0)
    def _():
        own_copy(0).start()
        barrier = pltpu.get_barrier_semaphore()
        for d in range(1, n_cyl):
            pl.semaphore_signal(
                barrier, inc=1, device_id={"cyl": lax.rem(rank + d, n_cyl)},
                device_id_type=pl.DeviceIdType.MESH,
            )
        pl.semaphore_wait(barrier, n_cyl - 1)

        def start(g, carry):
            for d in range(1, n_cyl):
                far_copy(d, g).start()

            @pl.when(g > 0)
            def _():
                own_copy(g).start()

            return carry

        lax.fori_loop(0, steps, start, 0)

    own_copy(step).wait()
    for d in range(1, n_cyl):
        far_copy(d, step).wait()
    volt_refs = [held_ref.at[d, step] for d in range(n_cyl)]
    fine = fine_ref[rank]

    def one_chan(ch, carry):
        for p in range(pols):
            for j in range(blocks):
                rows = jnp.concatenate(
                    [
                        ref[ch, c, p, j * UP : (j + 1) * UP, r * feeds : (r + 1) * feeds]
                        for ref in volt_refs
                        for c in range(per)
                        for r in range(2)
                    ],
                    axis=0,
                )
                got = jnp.dot(fine, rows, preferred_element_type=jnp.float32).astype(jnp.bfloat16)
                for s in range(2):
                    for e in range(cyls):
                        at = (s * cyls + e) * UP
                        mid_ref[p * blocks + j, e, ch, :, s * feeds : (s + 1) * feeds] = got[at : at + UP]
        return carry

    lax.fori_loop(0, group, one_chan, 0)
    wide = group * UP
    pair = 2 if cyls % 2 == 0 else 1
    ns = ns_ref[...]
    for q in range(FRAMES):
        for e in range(0, cyls, pair):
            total = None
            for p in range(pols):
                for j in range(q * sums, (q + 1) * sums):
                    block = mid_ref[p * blocks + j, e : e + pair].reshape(pair * wide, inputs)
                    spectra = lax.dot_general(
                        ns, block, (((1,), (1,)), ((), ())), preferred_element_type=jnp.float32
                    )
                    squared = spectra * spectra
                    power = squared[:feeds] + squared[feeds:]
                    total = power if total is None else total + power
            for i in range(pair):
                scaled = total[:, i * wide : (i + 1) * wide] * gain_ref[0, e + i : e + i + 1, :]
                out_ref[0, e + i, q] = scaled.astype(jnp.bfloat16)


def spread_kernel(in_ref, out_ref):
    sources, _, frames, steps, near, wide = in_ref.shape

    def one(source, carry):
        at = pl.multiple_of(source * (steps * wide), 128)
        for g in range(steps):
            rows = [in_ref[source, 0, q, g].astype(jnp.float32) for q in range(frames)]
            out_ref[0, :, :, pl.ds(at + g * wide, wide)] = jnp.stack(rows, axis=1)
        return carry

    lax.fori_loop(0, sources, one, 0)


def spread(power):
    sources, per, frames, steps, near, wide = power.shape
    lanes = sources * steps * wide
    return pl.pallas_call(
        spread_kernel,
        out_shape=jax.ShapeDtypeStruct((per, near, frames, lanes), jnp.float32),
        grid=(per,),
        in_specs=[pl.BlockSpec((sources, 1, frames, steps, near, wide), lambda e: (0, e, 0, 0, 0, 0))],
        out_specs=pl.BlockSpec((1, near, frames, lanes), lambda e: (e, 0, 0, 0)),
        compiler_params=pltpu.CompilerParams(dimension_semantics=("arbitrary",)),
        name="spread",
    )(power)


def half_rows(feeds):
    half = feeds // 2
    table = np.asarray(ns_rows(feeds)).reshape(2, half, 2, 2, feeds)[..., :half]
    return np.transpose(table, (2, 0, 1, 3, 4)).reshape(2, feeds, feeds)


def fused_kernel(
    n_chan, n_cyl, volts_ref, gains_ref, fine_hbm, ns_hbm, out_ref,
    held_ref, mid_ref, head_out_ref, send_ref, head_in_ref, recv_ref,
    exps_ref, head_scale_ref, scale_ref, fine_ref, ns_ref,
    own_sem, volt_send_sem, volt_recv_sem, exp_sem, exp_send_sem, exp_recv_sem, table_sem,
    head_send_sem, head_recv_sem, send_sem, recv_sem, pair_sem, go_sem,
):
    chip = lax.axis_index("chan")
    rank = lax.axis_index("cyl")
    me = chip * n_cyl + rank
    devices = n_chan * n_cyl
    _, stages, group, per, pols, times, inputs = held_ref.shape
    pieces = volt_recv_sem.shape[2]
    piece = group // pieces
    blocks = times // UP
    feeds = inputs // 2
    half = feeds // 2
    cyls = per * n_cyl
    steps = stages // FRAMES
    own = steps * group
    wide = group * UP
    near = feeds // n_chan
    share = group // per
    slim = share * UP

    def volt_rows(to, s, first, count):
        at = to * own + (s // FRAMES) * group + first
        time = pl.multiple_of((s % FRAMES) * times, times)
        return volts_ref.at[pl.ds(at, count), :, :, pl.ds(time, times), :]

    def own_copy(s):
        return pltpu.make_async_copy(volt_rows(rank, s, 0, group), held_ref.at[rank, s], own_sem.at[s])

    def far_copy(d, s, i):
        to = lax.rem(rank + d, n_cyl)
        return pltpu.make_async_remote_copy(
            src_ref=volt_rows(to, s, i * piece, piece),
            dst_ref=held_ref.at[rank, s, pl.ds(i * piece, piece)],
            send_sem=volt_send_sem.at[d],
            recv_sem=volt_recv_sem.at[d, s, i],
            device_id={"cyl": to},
            device_id_type=pl.DeviceIdType.MESH,
        )

    def far_arrived(d, s, i):
        source = lax.rem(rank + n_cyl - d, n_cyl)
        there = held_ref.at[source, s, pl.ds(i * piece, piece)]
        return pltpu.make_async_copy(there, there, volt_recv_sem.at[d, s, i])

    def exp_copy(d):
        return pltpu.make_async_remote_copy(
            src_ref=gains_ref,
            dst_ref=exps_ref.at[rank],
            send_sem=exp_send_sem.at[d],
            recv_sem=exp_recv_sem.at[d],
            device_id={"cyl": lax.rem(rank + d, n_cyl)},
            device_id_type=pl.DeviceIdType.MESH,
        )

    fine_copy = pltpu.make_async_copy(fine_hbm, fine_ref, table_sem.at[0])
    ns_copy = pltpu.make_async_copy(ns_hbm, ns_ref, table_sem.at[1])
    own_exps = pltpu.make_async_copy(gains_ref, exps_ref.at[rank], exp_sem)

    barrier = pltpu.get_barrier_semaphore()
    mesh_id = pl.DeviceIdType.MESH

    lead = n_cyl - 1

    @pl.when(rank == lead)
    def _():
        pl.semaphore_signal(barrier, inc=1, device_id={"cyl": 0}, device_id_type=mesh_id)

    @pl.when(rank != lead)
    def _():
        pl.semaphore_signal(barrier, inc=1, device_id={"cyl": lead}, device_id_type=mesh_id)

    def greet(i, carry):
        to = lax.rem(chip + i, n_chan)
        pl.semaphore_signal(barrier, inc=1, device_id={"chan": to, "cyl": lead}, device_id_type=mesh_id)
        return carry

    lax.fori_loop(1, n_chan, greet, 0)
    own_copy(0).start()
    fine_copy.start()
    own_exps.start()
    ns_copy.start()

    @pl.when(rank != lead)
    def _():
        pl.semaphore_wait(barrier, 1)
        pl.semaphore_signal(pair_sem, inc=1, device_id={"cyl": lead}, device_id_type=mesh_id)

    @pl.when(rank == lead)
    def _():
        pl.semaphore_wait(pair_sem, 1)

    def all_here():
        @pl.when(rank == lead)
        def _():
            pl.semaphore_wait(barrier, devices - 1)
            pl.semaphore_signal(go_sem, inc=1, device_id={"cyl": 0}, device_id_type=mesh_id)

        @pl.when(rank != lead)
        def _():
            pl.semaphore_wait(go_sem, 1)

    def start_own(s, carry):
        own_copy(s).start()
        return carry

    def start_far(n, carry):
        for d in range(1, n_cyl):
            far_copy(d, n // pieces, n % pieces).start()
        return carry

    for d in range(1, n_cyl):
        exp_copy(d).start()
    lax.fori_loop(0, pieces, start_far, 0)
    lax.fori_loop(1, stages, start_own, 0)
    lax.fori_loop(pieces, stages * pieces, start_far, 0)
    fine_copy.wait()

    own_exps.wait()
    for d in range(1, n_cyl):
        exp_copy(d).wait()
    chans = exps_ref.shape[2]
    lane = lax.broadcasted_iota(jnp.int32, (chans, own * UP), 1)
    chan = lax.broadcasted_iota(jnp.int32, (chans, own * UP), 0) - rank * own
    exps = jnp.concatenate([exps_ref[i] for i in range(n_cyl)], axis=0).astype(jnp.float32)

    def scale_of(pick):
        spread = jnp.dot(exps, pick.astype(jnp.float32), preferred_element_type=jnp.float32)
        return jnp.exp2(2.0 * spread) / (pols * blocks)

    scale = scale_of(chan == lane // UP)
    for g in range(steps):
        for o in range(n_cyl):
            scale_ref[g, o] = scale[o * per : (o + 1) * per, g * wide : (g + 1) * wide]
    lane, chan = lane[:, :wide], chan[:, :wide]
    for h in range(per):
        scale = scale_of(chan == h * share + lane % slim // UP)
        for o in range(n_cyl):
            row = scale[o * per : o * per + 1]
            for e in range(1, per):
                row = jnp.where(lane[:1] // slim == e, scale[o * per + e : o * per + e + 1], row)
            head_scale_ref[h, o] = row

    def fine_piece(s, i):
        fine = fine_ref[...]
        for d in range(1, n_cyl):
            far_arrived(d, s, i).wait()
        for c0 in range(piece):
            ch = i * piece + c0
            for p in range(pols):
                for j in range(blocks):
                    rows = jnp.concatenate(
                        [
                            held_ref[o, s, ch, c, p, j * UP : (j + 1) * UP, r * feeds : (r + 1) * feeds]
                            for o in range(n_cyl)
                            for c in range(per)
                            for r in range(2)
                        ],
                        axis=0,
                    )
                    got = jnp.dot(fine, rows, preferred_element_type=jnp.float32)
                    low, high = got[:, :half], got[:, half:]
                    both = ((low + high).astype(jnp.bfloat16), (low - high).astype(jnp.bfloat16))
                    for odd in range(2):
                        for r in range(2):
                            for e in range(cyls):
                                at = (r * cyls + e) * UP
                                mid_ref[p * blocks + j, odd, e, ch, :, r * half : (r + 1) * half] = (
                                    both[odd][at : at + UP]
                                )

    def fine_pieces(s, first, last):
        def one(i, carry):
            fine_piece(s, i)
            return carry

        lax.fori_loop(first, last, one, 0)

    def powers(beams, first, count, rows=None):
        parts = []
        for odd in range(2):
            total = None
            if rows is None:
                ns = ns_ref[odd]
            else:
                ns = jnp.concatenate([ns_ref[odd, pl.ds(r * half + rows, half // 2)] for r in range(2)], axis=0)
            kept = ns.shape[0] // 2
            for b in range(pols * blocks):
                block = mid_ref[b, odd, beams, first : first + count]
                spectra = lax.dot_general(
                    ns, block.reshape(-1, feeds), (((1,), (1,)), ((), ())),
                    preferred_element_type=jnp.float32,
                )
                squared = spectra * spectra
                power = squared[:kept] + squared[kept:]
                total = power if total is None else total + power
            parts.append(total)
        return parts

    def by_chip(parts, factor):
        scaled = [(part * factor).reshape(-1, near // 2, wide) for part in parts]
        return jnp.concatenate(scaled, axis=1).astype(jnp.bfloat16)

    def send_to(source_ref, target_ref, out_sem, in_sem, peer):
        owner = lax.rem(peer, n_cyl)
        to = lax.div(peer, n_cyl)
        pltpu.make_async_remote_copy(
            src_ref=source_ref.at[owner, to],
            dst_ref=target_ref.at[me],
            send_sem=out_sem,
            recv_sem=in_sem,
            device_id={"chan": to, "cyl": owner},
            device_id_type=mesh_id,
        ).start()

    def send_ring(base, count, source_ref, target_ref, out_sem, in_sem):
        at = me - base
        for i in range(1, count):
            peer = base + jnp.where(at + i >= count, at + i - count, at + i)
            send_to(source_ref, target_ref, out_sem, in_sem, peer)
        pltpu.make_async_copy(source_ref.at[rank, chip], target_ref.at[me], in_sem).start()

    side = lax.div(chip, n_chan // 2)
    many = devices // 2

    def send_other_side(*refs):
        at = me - side * many
        base = (1 - side) * many
        for i in range(many):
            send_to(*refs, base + jnp.where(at + i >= many, at + i - many, at + i))

    own_copy(0).wait()
    for h in range(per):
        fine_pieces(0, h * share // piece, (h + 1) * share // piece)
        if h == 0:
            ns_copy.wait()
        refs = (head_out_ref.at[h], head_in_ref.at[h], head_send_sem, head_recv_sem.at[h])
        for turn in range(2):
            which = jnp.where(side == turn, 1, 0)
            rows = pl.multiple_of(which * (half // 2), half // 2)
            parts = powers(pl.ds(0, cyls), h * share, share, rows)
            for o in range(n_cyl):
                head_out_ref[h, o, pl.ds(which * (n_chan // 2), n_chan // 2)] = by_chip(
                    [part[:, o * wide : (o + 1) * wide] for part in parts], head_scale_ref[h, o]
                )
            if turn == 0:
                if h == 0:
                    all_here()
                send_other_side(*refs)
            else:
                send_ring(side * many, many, *refs)

    def one_stage(s, carry):
        own_copy(s).wait()
        fine_pieces(s, 0, pieces)

        def one_owner(owner, inner):
            parts = powers(pl.ds(owner * per, per), 0, group)
            for e in range(per):
                send_ref[s - 1, owner, :, e] = by_chip(
                    [part[:, e * wide : (e + 1) * wide] for part in parts],
                    scale_ref[s // FRAMES, owner, e : e + 1, :],
                )
            return inner

        lax.fori_loop(0, n_cyl, one_owner, 0)
        send_ring(0, devices, send_ref.at[s - 1], recv_ref.at[s - 1], send_sem, recv_sem.at[s - 1])
        return carry

    lax.fori_loop(1, stages, one_stage, 0)

    depth = devices * stages

    several = math.gcd(4, devices)

    def place(s, source, e, tile):
        row = (source * steps + s // FRAMES) * FRAMES + s % FRAMES
        for odd in range(2):
            at = (e * near + odd) * depth + row
            out_ref[pl.ds(at, near // 2, 2 * depth), :] = tile[odd * (near // 2) : (odd + 1) * (near // 2)]

    for h in range(per):
        pltpu.make_async_copy(head_in_ref.at[h], head_in_ref.at[h], head_recv_sem.at[h]).wait()
    slot = lax.broadcasted_iota(jnp.int32, (near, wide), 1) // slim

    def spread_head(source, carry):
        tiles = [head_in_ref[h, source].astype(jnp.float32) for h in range(per)]
        for e in range(per):
            tile = tiles[e]
            for h in range(per):
                if h != e:
                    moved = pltpu.roll(tiles[h], (h - e) * slim % wide, 1)
                    tile = jnp.where(slot == h, moved, tile)
            place(0, source, e, tile)
        return carry

    lax.fori_loop(0, devices, spread_head, 0)

    def spread_stage(s, carry):
        pltpu.make_async_copy(recv_ref.at[s - 1], recv_ref.at[s - 1], recv_sem.at[s - 1]).wait()

        def some(n, inner):
            for k in range(several):
                for e in range(per):
                    source = n * several + k
                    place(s, source, e, recv_ref[s - 1, source, e].astype(jnp.float32))
            return inner

        lax.fori_loop(0, devices // several, some, 0)
        return carry

    lax.fori_loop(1, stages, spread_stage, 0)
    for ref, sem in ((head_in_ref, head_send_sem), (recv_ref, send_sem)):
        sent = ref.at[:, : devices - 1]
        pltpu.make_async_copy(sent, sent, sem).wait()
    for d in range(1, n_cyl):
        pltpu.make_async_copy(held_ref.at[0], held_ref.at[0], volt_send_sem.at[d]).wait()


def fused(n_chan, n_cyl, volts, gain_exponents):
    chans, per, pols, times, inputs = volts.shape
    feeds = inputs // 2
    cyls = per * n_cyl
    own = chans // n_cyl
    group = 128 // UP
    steps = own // group
    stages = steps * FRAMES
    span = times // FRAMES
    blocks = span // UP
    near = feeds // n_chan
    devices = n_chan * n_cyl
    wide = group * UP
    pieces = 4
    fine = jnp.asarray(fine_rows(cyls, 1, UP)[0])
    ns = jnp.asarray(half_rows(feeds))
    operands = (volts, gain_exponents.T, fine, ns)
    dma = pltpu.SemaphoreType.DMA
    out = pl.pallas_call(
        functools.partial(fused_kernel, n_chan, n_cyl),
        out_shape=jax.ShapeDtypeStruct((per * near * devices * stages, wide), jnp.float32),
        in_specs=[pl.BlockSpec(memory_space=pltpu.HBM)] * 4,
        out_specs=pl.BlockSpec(memory_space=pltpu.VMEM),
        scratch_shapes=[
            pltpu.VMEM((n_cyl, stages, group, per, pols, span, inputs), jnp.bfloat16),
            pltpu.VMEM((pols * blocks, 2, cyls, group, UP, feeds), jnp.bfloat16),
            pltpu.VMEM((per, n_cyl, n_chan, near, wide), jnp.bfloat16),
            pltpu.VMEM((stages - 1, n_cyl, n_chan, per, near, wide), jnp.bfloat16),
            pltpu.VMEM((per, devices, near, wide), jnp.bfloat16),
            pltpu.VMEM((stages - 1, devices, per, near, wide), jnp.bfloat16),
            pltpu.VMEM((n_cyl, per, chans), jnp.int32),
            pltpu.VMEM((per, n_cyl, 1, wide), jnp.float32),
            pltpu.VMEM((steps, n_cyl, per, wide), jnp.float32),
            pltpu.VMEM(fine.shape, jnp.bfloat16),
            pltpu.VMEM(ns.shape, jnp.bfloat16),
            dma((stages,)),
            dma((n_cyl,)),
            dma((n_cyl, stages, pieces)),
            dma,
            dma((n_cyl,)),
            dma((n_cyl,)),
            dma((2,)),
            dma,
            dma((per,)),
            dma,
            dma((stages - 1,)),
            pltpu.SemaphoreType.REGULAR,
            pltpu.SemaphoreType.REGULAR,
        ],
        compiler_params=pltpu.CompilerParams(
            collective_id=0, has_side_effects=True, vmem_limit_bytes=48 * 1024 * 1024
        ),
        name="fused",
    )(*[pltpu.with_memory_space_constraint(x, pltpu.HBM) for x in operands])
    out = out.reshape(per, near, devices * steps, FRAMES, wide)
    return jnp.transpose(out, (0, 1, 3, 2, 4)).reshape(per, near, FRAMES, -1)


def fits(n_chan, n_cyl, volts):
    chans, per, pols, times, inputs = volts.shape
    own = chans // n_cyl
    feeds = inputs // 2
    return (
        n_cyl == 2
        and n_chan % 2 == 0
        and per in (1, 2)
        and own % (128 // UP) == 0
        and feeds % (16 * n_chan) == 0
        and feeds % 256 == 0
        and times % (FRAMES * UP) == 0
    )


def local(n_chan, n_cyl, volts, gain_exponents):
    chans, per, pols, times, inputs = volts.shape
    feeds = inputs // 2
    cyls = per * n_cyl
    own = chans // n_cyl
    group = math.gcd(8, own)
    steps = own // group
    wide = group * UP
    blocks = times // UP
    rank = lax.axis_index("cyl")
    gains = [lax.dynamic_slice_in_dim(gain_exponents, rank * own, own, 0)]
    for d in range(1, n_cyl):
        ring = [(k, (k + d) % n_cyl) for k in range(n_cyl)]
        to = (rank + d) % n_cyl
        gains.append(
            lax.ppermute(lax.dynamic_slice_in_dim(gain_exponents, to * own, own, 0), "cyl", ring)
        )
    stacked = jnp.stack(gains)
    order = (rank - jnp.arange(n_cyl, dtype=jnp.int32)) % n_cyl
    exps = jnp.take(stacked, order, axis=0)
    exps = jnp.transpose(exps, (0, 2, 1)).reshape(cyls, steps, group)
    scale = jnp.exp2(2.0 * exps.astype(jnp.float32)) / (pols * (blocks // FRAMES))
    scale = jnp.transpose(jnp.repeat(scale, UP, axis=2), (1, 0, 2))

    fine = jnp.asarray(fine_rows(cyls, n_cyl, UP))
    ns = jnp.asarray(ns_rows(feeds))
    power = pl.pallas_call(
        functools.partial(beam_kernel, cyls, n_cyl),
        out_shape=jax.ShapeDtypeStruct((steps, cyls, FRAMES, feeds, wide), jnp.bfloat16),
        grid=(steps,),
        in_specs=[
            pl.BlockSpec(memory_space=pl.ANY),
            pl.BlockSpec(fine.shape, lambda g: (0, 0, 0)),
            pl.BlockSpec(ns.shape, lambda g: (0, 0)),
            pl.BlockSpec((1, cyls, wide), lambda g: (g, 0, 0)),
        ],
        out_specs=pl.BlockSpec((1, cyls, FRAMES, feeds, wide), lambda g: (g, 0, 0, 0, 0)),
        scratch_shapes=[
            pltpu.VMEM((pols * blocks, cyls, group, UP, inputs), jnp.bfloat16),
            pltpu.VMEM((n_cyl, steps, group, per, pols, times, inputs), jnp.bfloat16),
            pltpu.SemaphoreType.DMA((steps,)),
            pltpu.SemaphoreType.DMA((n_cyl, steps)),
            pltpu.SemaphoreType.DMA((n_cyl, steps)),
        ],
        compiler_params=pltpu.CompilerParams(
            dimension_semantics=("arbitrary",), collective_id=0, has_side_effects=True
        ),
        name="beams",
    )(volts, fine, ns, scale)

    near = feeds // n_chan
    power = power.reshape(steps, n_cyl, per, FRAMES, n_chan, near, wide)
    power = jnp.transpose(power, (4, 1, 2, 3, 0, 5, 6))
    power = power.reshape(n_chan * n_cyl, per, FRAMES, steps, near, wide)
    power = lax.all_to_all(power, ("chan", "cyl"), split_axis=0, concat_axis=0, tiled=True)
    if (steps * wide) % 128 == 0:
        return spread(power)
    power = jnp.transpose(power, (1, 4, 2, 0, 3, 5))
    return power.reshape(per, near, FRAMES, -1).astype(jnp.float32)


def either(n_chan, n_cyl, volts, gain_exponents):
    if fits(n_chan, n_cyl, volts):
        return fused(n_chan, n_cyl, volts, gain_exponents)
    return local(n_chan, n_cyl, volts, gain_exponents)


def solution(mesh):
    return jax.shard_map(
        functools.partial(either, mesh.shape["chan"], mesh.shape["cyl"]),
        mesh=mesh,
        in_specs=(P("chan", "cyl", None, None, None), P("chan", "cyl")),
        out_specs=P("cyl", "chan", None, None),
        check_vma=False,
    )
```

```python
import functools
import math

import jax
import jax.numpy as jnp
import ml_dtypes
import numpy as np
from jax import lax
from jax.experimental import pallas as pl
from jax.experimental.pallas import tpu as pltpu
from jax.sharding import PartitionSpec as P

UP = 16
FRAMES = 2


def ns_rows(feeds):
    index = np.arange(feeds)
    theta = (index[None, :] * (index[:, None] - feeds // 2) % feeds) * (2.0 * math.pi / feeds)
    cosine = np.cos(theta) / math.sqrt(feeds)
    sine = np.sin(theta) / math.sqrt(feeds)
    table = np.concatenate(
        [np.concatenate([cosine, sine], axis=1), np.concatenate([-sine, cosine], axis=1)], axis=0
    )
    return table.astype(ml_dtypes.bfloat16)


def fine_rows(cyls, n_cyl, up):
    index = np.arange(up)
    theta = (index[:, None] * index[None, :] % up) * (2.0 * math.pi / up)
    rounded = lambda x: (x / math.sqrt(up)).astype(ml_dtypes.bfloat16).astype(np.float64)
    fine = rounded(np.cos(theta)) - 1j * rounded(np.sin(theta))
    cyl = np.arange(cyls)
    phase = 2.0 * math.pi * cyl[None, :] * (cyl[:, None] - (cyls - 1) / 2.0) / cyls
    weight = np.exp(-1j * phase) / 2.0
    both = np.einsum("ec,km->emck", weight, fine)
    parts = np.stack(
        [np.stack([both.real, -both.imag], axis=3), np.stack([both.imag, both.real], axis=3)], axis=0
    )
    per = cyls // n_cyl
    tables = []
    for rank in range(n_cyl):
        order = [((rank - d) % n_cyl) * per + c for d in range(n_cyl) for c in range(per)]
        tables.append(parts[:, :, :, order].reshape(2 * cyls * up, cyls * 2 * up))
    return np.stack(tables).astype(ml_dtypes.bfloat16)


def beam_kernel(
    cyls, n_cyl, volts_ref, fine_ref, ns_ref, gain_ref, out_ref,
    mid_ref, held_ref, own_sem, send_sem, recv_sem,
):
    step = pl.program_id(0)
    steps = pl.num_programs(0)
    _, _, group, per, pols, times, inputs = held_ref.shape
    feeds = inputs // 2
    blocks = times // UP
    sums = blocks // FRAMES
    rank = lax.axis_index("cyl")

    def own_copy(g):
        rows = pl.ds((rank * steps + g) * group, group)
        return pltpu.make_async_copy(volts_ref.at[rows], held_ref.at[0, g], own_sem.at[g])

    def far_copy(d, g):
        to = lax.rem(rank + d, n_cyl)
        rows = pl.ds((to * steps + g) * group, group)
        return pltpu.make_async_remote_copy(
            src_ref=volts_ref.at[rows],
            dst_ref=held_ref.at[d, g],
            send_sem=send_sem.at[d, g],
            recv_sem=recv_sem.at[d, g],
            device_id={"cyl": to},
            device_id_type=pl.DeviceIdType.MESH,
        )

    @pl.when(step == 0)
    def _():
        own_copy(0).start()
        barrier = pltpu.get_barrier_semaphore()
        for d in range(1, n_cyl):
            pl.semaphore_signal(
                barrier, inc=1, device_id={"cyl": lax.rem(rank + d, n_cyl)},
                device_id_type=pl.DeviceIdType.MESH,
            )
        pl.semaphore_wait(barrier, n_cyl - 1)

        def start(g, carry):
            for d in range(1, n_cyl):
                far_copy(d, g).start()

            @pl.when(g > 0)
            def _():
                own_copy(g).start()

            return carry

        lax.fori_loop(0, steps, start, 0)

    own_copy(step).wait()
    for d in range(1, n_cyl):
        far_copy(d, step).wait()
    volt_refs = [held_ref.at[d, step] for d in range(n_cyl)]
    fine = fine_ref[rank]

    def one_chan(ch, carry):
        for p in range(pols):
            for j in range(blocks):
                rows = jnp.concatenate(
                    [
                        ref[ch, c, p, j * UP : (j + 1) * UP, r * feeds : (r + 1) * feeds]
                        for ref in volt_refs
                        for c in range(per)
                        for r in range(2)
                    ],
                    axis=0,
                )
                got = jnp.dot(fine, rows, preferred_element_type=jnp.float32).astype(jnp.bfloat16)
                for s in range(2):
                    for e in range(cyls):
                        at = (s * cyls + e) * UP
                        mid_ref[p * blocks + j, e, ch, :, s * feeds : (s + 1) * feeds] = got[at : at + UP]
        return carry

    lax.fori_loop(0, group, one_chan, 0)
    wide = group * UP
    pair = 2 if cyls % 2 == 0 else 1
    ns = ns_ref[...]
    for q in range(FRAMES):
        for e in range(0, cyls, pair):
            total = None
            for p in range(pols):
                for j in range(q * sums, (q + 1) * sums):
                    block = mid_ref[p * blocks + j, e : e + pair].reshape(pair * wide, inputs)
                    spectra = lax.dot_general(
                        ns, block, (((1,), (1,)), ((), ())), preferred_element_type=jnp.float32
                    )
                    squared = spectra * spectra
                    power = squared[:feeds] + squared[feeds:]
                    total = power if total is None else total + power
            for i in range(pair):
                scaled = total[:, i * wide : (i + 1) * wide] * gain_ref[0, e + i : e + i + 1, :]
                out_ref[0, e + i, q] = scaled.astype(jnp.bfloat16)


def spread_kernel(in_ref, out_ref):
    sources, _, frames, steps, near, wide = in_ref.shape

    def one(source, carry):
        at = pl.multiple_of(source * (steps * wide), 128)
        for g in range(steps):
            rows = [in_ref[source, 0, q, g].astype(jnp.float32) for q in range(frames)]
            out_ref[0, :, :, pl.ds(at + g * wide, wide)] = jnp.stack(rows, axis=1)
        return carry

    lax.fori_loop(0, sources, one, 0)


def spread(power):
    sources, per, frames, steps, near, wide = power.shape
    lanes = sources * steps * wide
    return pl.pallas_call(
        spread_kernel,
        out_shape=jax.ShapeDtypeStruct((per, near, frames, lanes), jnp.float32),
        grid=(per,),
        in_specs=[pl.BlockSpec((sources, 1, frames, steps, near, wide), lambda e: (0, e, 0, 0, 0, 0))],
        out_specs=pl.BlockSpec((1, near, frames, lanes), lambda e: (e, 0, 0, 0)),
        compiler_params=pltpu.CompilerParams(dimension_semantics=("arbitrary",)),
        name="spread",
    )(power)


def half_rows(feeds):
    half = feeds // 2
    table = np.asarray(ns_rows(feeds)).reshape(2, half, 2, 2, feeds)[..., :half]
    return np.transpose(table, (2, 0, 1, 3, 4)).reshape(2, feeds, feeds)


def fused_kernel(
    n_chan, n_cyl, volts_ref, gains_ref, fine_hbm, ns_hbm, out_ref,
    held_ref, mid_ref, head_out_ref, send_ref, head_in_ref, recv_ref,
    exps_ref, head_scale_ref, scale_ref, fine_ref, ns_ref,
    own_sem, volt_send_sem, volt_recv_sem, exp_sem, exp_send_sem, exp_recv_sem, table_sem,
    head_send_sem, head_recv_sem, send_sem, recv_sem, pair_sem, go_sem,
):
    chip = lax.axis_index("chan")
    rank = lax.axis_index("cyl")
    me = chip * n_cyl + rank
    devices = n_chan * n_cyl
    _, stages, group, per, pols, times, inputs = held_ref.shape
    pieces = volt_recv_sem.shape[2]
    piece = group // pieces
    blocks = times // UP
    feeds = inputs // 2
    half = feeds // 2
    cyls = per * n_cyl
    steps = stages // FRAMES
    own = steps * group
    wide = group * UP
    near = feeds // n_chan
    share = group // per
    slim = share * UP

    def volt_rows(to, s, first, count):
        at = to * own + (s // FRAMES) * group + first
        time = pl.multiple_of((s % FRAMES) * times, times)
        return volts_ref.at[pl.ds(at, count), :, :, pl.ds(time, times), :]

    def own_copy(s):
        return pltpu.make_async_copy(volt_rows(rank, s, 0, group), held_ref.at[rank, s], own_sem.at[s])

    def far_copy(d, s, i):
        to = lax.rem(rank + d, n_cyl)
        return pltpu.make_async_remote_copy(
            src_ref=volt_rows(to, s, i * piece, piece),
            dst_ref=held_ref.at[rank, s, pl.ds(i * piece, piece)],
            send_sem=volt_send_sem.at[d],
            recv_sem=volt_recv_sem.at[d, s, i],
            device_id={"cyl": to},
            device_id_type=pl.DeviceIdType.MESH,
        )

    def far_arrived(d, s, i):
        source = lax.rem(rank + n_cyl - d, n_cyl)
        there = held_ref.at[source, s, pl.ds(i * piece, piece)]
        return pltpu.make_async_copy(there, there, volt_recv_sem.at[d, s, i])

    def exp_copy(d):
        return pltpu.make_async_remote_copy(
            src_ref=gains_ref,
            dst_ref=exps_ref.at[rank],
            send_sem=exp_send_sem.at[d],
            recv_sem=exp_recv_sem.at[d],
            device_id={"cyl": lax.rem(rank + d, n_cyl)},
            device_id_type=pl.DeviceIdType.MESH,
        )

    fine_copy = pltpu.make_async_copy(fine_hbm, fine_ref, table_sem.at[0])
    ns_copy = pltpu.make_async_copy(ns_hbm, ns_ref, table_sem.at[1])
    own_exps = pltpu.make_async_copy(gains_ref, exps_ref.at[rank], exp_sem)

    barrier = pltpu.get_barrier_semaphore()
    mesh_id = pl.DeviceIdType.MESH

    lead = n_cyl - 1

    @pl.when(rank == lead)
    def _():
        pl.semaphore_signal(barrier, inc=1, device_id={"cyl": 0}, device_id_type=mesh_id)

    @pl.when(rank != lead)
    def _():
        pl.semaphore_signal(barrier, inc=1, device_id={"cyl": lead}, device_id_type=mesh_id)

    def greet(i, carry):
        to = lax.rem(chip + i, n_chan)
        pl.semaphore_signal(barrier, inc=1, device_id={"chan": to, "cyl": lead}, device_id_type=mesh_id)
        return carry

    own_copy(0).start()
    fine_copy.start()
    own_exps.start()
    ns_copy.start()

    @pl.when(rank != lead)
    def _():
        pl.semaphore_wait(barrier, 1)
        pl.semaphore_signal(pair_sem, inc=1, device_id={"cyl": lead}, device_id_type=mesh_id)

    @pl.when(rank == lead)
    def _():
        pl.semaphore_wait(pair_sem, 1)

    def all_here():
        @pl.when(rank == lead)
        def _():
            pl.semaphore_wait(barrier, devices - 1)
            pl.semaphore_signal(go_sem, inc=1, device_id={"cyl": 0}, device_id_type=mesh_id)

        @pl.when(rank != lead)
        def _():
            pl.semaphore_wait(go_sem, 1)

    def start_own(s, carry):
        own_copy(s).start()
        return carry

    def start_far(n, carry):
        for d in range(1, n_cyl):
            far_copy(d, n // pieces, n % pieces).start()
        return carry

    for d in range(1, n_cyl):
        exp_copy(d).start()
    lax.fori_loop(0, pieces // 2, start_far, 0)
    lax.fori_loop(1, n_chan, greet, 0)
    lax.fori_loop(pieces // 2, pieces, start_far, 0)
    lax.fori_loop(1, stages, start_own, 0)
    lax.fori_loop(pieces, stages * pieces, start_far, 0)
    fine_copy.wait()

    own_exps.wait()
    for d in range(1, n_cyl):
        exp_copy(d).wait()
    chans = exps_ref.shape[2]
    lane = lax.broadcasted_iota(jnp.int32, (chans, own * UP), 1)
    chan = lax.broadcasted_iota(jnp.int32, (chans, own * UP), 0) - rank * own
    exps = jnp.concatenate([exps_ref[i] for i in range(n_cyl)], axis=0).astype(jnp.float32)

    def scale_of(pick):
        spread = jnp.dot(exps, pick.astype(jnp.float32), preferred_element_type=jnp.float32)
        return jnp.exp2(2.0 * spread) / (pols * blocks)

    scale = scale_of(chan == lane // UP)
    for g in range(steps):
        for o in range(n_cyl):
            scale_ref[g, o] = scale[o * per : (o + 1) * per, g * wide : (g + 1) * wide]
    lane, chan = lane[:, :wide], chan[:, :wide]
    for h in range(per):
        scale = scale_of(chan == h * share + lane % slim // UP)
        for o in range(n_cyl):
            row = scale[o * per : o * per + 1]
            for e in range(1, per):
                row = jnp.where(lane[:1] // slim == e, scale[o * per + e : o * per + e + 1], row)
            head_scale_ref[h, o] = row

    def fine_piece(s, i):
        fine = fine_ref[...]
        for d in range(1, n_cyl):
            far_arrived(d, s, i).wait()
        for c0 in range(piece):
            ch = i * piece + c0
            for p in range(pols):
                for j in range(blocks):
                    rows = jnp.concatenate(
                        [
                            held_ref[o, s, ch, c, p, j * UP : (j + 1) * UP, r * feeds : (r + 1) * feeds]
                            for o in range(n_cyl)
                            for c in range(per)
                            for r in range(2)
                        ],
                        axis=0,
                    )
                    got = jnp.dot(fine, rows, preferred_element_type=jnp.float32)
                    low, high = got[:, :half], got[:, half:]
                    both = ((low + high).astype(jnp.bfloat16), (low - high).astype(jnp.bfloat16))
                    for odd in range(2):
                        for r in range(2):
                            for e in range(cyls):
                                at = (r * cyls + e) * UP
                                mid_ref[p * blocks + j, odd, e, ch, :, r * half : (r + 1) * half] = (
                                    both[odd][at : at + UP]
                                )

    def fine_pieces(s, first, last):
        def one(i, carry):
            fine_piece(s, i)
            return carry

        lax.fori_loop(first, last, one, 0)

    def powers(beams, first, count, rows=None):
        parts = []
        for odd in range(2):
            total = None
            if rows is None:
                ns = ns_ref[odd]
            else:
                ns = jnp.concatenate([ns_ref[odd, pl.ds(r * half + rows, half // 2)] for r in range(2)], axis=0)
            kept = ns.shape[0] // 2
            for b in range(pols * blocks):
                block = mid_ref[b, odd, beams, first : first + count]
                spectra = lax.dot_general(
                    ns, block.reshape(-1, feeds), (((1,), (1,)), ((), ())),
                    preferred_element_type=jnp.float32,
                )
                squared = spectra * spectra
                power = squared[:kept] + squared[kept:]
                total = power if total is None else total + power
            parts.append(total)
        return parts

    def by_chip(parts, factor):
        scaled = [(part * factor).reshape(-1, near // 2, wide) for part in parts]
        return jnp.concatenate(scaled, axis=1).astype(jnp.bfloat16)

    def send_to(source_ref, target_ref, out_sem, in_sem, peer):
        owner = lax.rem(peer, n_cyl)
        to = lax.div(peer, n_cyl)
        pltpu.make_async_remote_copy(
            src_ref=source_ref.at[owner, to],
            dst_ref=target_ref.at[me],
            send_sem=out_sem,
            recv_sem=in_sem,
            device_id={"chan": to, "cyl": owner},
            device_id_type=mesh_id,
        ).start()

    def send_ring(base, count, source_ref, target_ref, out_sem, in_sem):
        at = me - base
        for i in range(1, count):
            peer = base + jnp.where(at + i >= count, at + i - count, at + i)
            send_to(source_ref, target_ref, out_sem, in_sem, peer)
        pltpu.make_async_copy(source_ref.at[rank, chip], target_ref.at[me], in_sem).start()

    side = lax.div(chip, n_chan // 2)
    many = devices // 2

    def send_other_side(*refs):
        at = me - side * many
        base = (1 - side) * many
        for i in range(many):
            send_to(*refs, base + jnp.where(at + i >= many, at + i - many, at + i))

    own_copy(0).wait()
    for h in range(per):
        fine_pieces(0, h * share // piece, (h + 1) * share // piece)
        if h == 0:
            ns_copy.wait()
        refs = (head_out_ref.at[h], head_in_ref.at[h], head_send_sem, head_recv_sem.at[h])
        for turn in range(2):
            which = jnp.where(side == turn, 1, 0)
            rows = pl.multiple_of(which * (half // 2), half // 2)
            parts = powers(pl.ds(0, cyls), h * share, share, rows)
            for o in range(n_cyl):
                head_out_ref[h, o, pl.ds(which * (n_chan // 2), n_chan // 2)] = by_chip(
                    [part[:, o * wide : (o + 1) * wide] for part in parts], head_scale_ref[h, o]
                )
            if turn == 0:
                if h == 0:
                    all_here()
                send_other_side(*refs)
            else:
                send_ring(side * many, many, *refs)

    def one_stage(s, carry):
        own_copy(s).wait()
        fine_pieces(s, 0, pieces)

        def one_owner(owner, inner):
            parts = powers(pl.ds(owner * per, per), 0, group)
            for e in range(per):
                send_ref[s - 1, owner, :, e] = by_chip(
                    [part[:, e * wide : (e + 1) * wide] for part in parts],
                    scale_ref[s // FRAMES, owner, e : e + 1, :],
                )
            return inner

        lax.fori_loop(0, n_cyl, one_owner, 0)
        send_ring(0, devices, send_ref.at[s - 1], recv_ref.at[s - 1], send_sem, recv_sem.at[s - 1])
        return carry

    lax.fori_loop(1, stages, one_stage, 0)

    depth = devices * stages

    several = math.gcd(8, devices)

    def place(s, source, e, tile):
        row = (source * steps + s // FRAMES) * FRAMES + s % FRAMES
        for odd in range(2):
            at = (e * near + odd) * depth + row
            out_ref[pl.ds(at, near // 2, 2 * depth), :] = tile[odd * (near // 2) : (odd + 1) * (near // 2)]

    for h in range(per):
        pltpu.make_async_copy(head_in_ref.at[h], head_in_ref.at[h], head_recv_sem.at[h]).wait()
    slot = lax.broadcasted_iota(jnp.int32, (near, wide), 1) // slim

    def spread_head(source, carry):
        tiles = [head_in_ref[h, source].astype(jnp.float32) for h in range(per)]
        for e in range(per):
            tile = tiles[e]
            for h in range(per):
                if h != e:
                    moved = pltpu.roll(tiles[h], (h - e) * slim % wide, 1)
                    tile = jnp.where(slot == h, moved, tile)
            place(0, source, e, tile)
        return carry

    lax.fori_loop(0, devices, spread_head, 0)

    def spread_stage(s, carry):
        pltpu.make_async_copy(recv_ref.at[s - 1], recv_ref.at[s - 1], recv_sem.at[s - 1]).wait()

        def some(n, inner):
            for k in range(several):
                for e in range(per):
                    source = n * several + k
                    place(s, source, e, recv_ref[s - 1, source, e].astype(jnp.float32))
            return inner

        lax.fori_loop(0, devices // several, some, 0)
        return carry

    lax.fori_loop(1, stages, spread_stage, 0)
    for ref, sem in ((head_in_ref, head_send_sem), (recv_ref, send_sem)):
        sent = ref.at[:, : devices - 1]
        pltpu.make_async_copy(sent, sent, sem).wait()
    for d in range(1, n_cyl):
        pltpu.make_async_copy(held_ref.at[0], held_ref.at[0], volt_send_sem.at[d]).wait()


def fused(n_chan, n_cyl, volts, gain_exponents):
    chans, per, pols, times, inputs = volts.shape
    feeds = inputs // 2
    cyls = per * n_cyl
    own = chans // n_cyl
    group = 128 // UP
    steps = own // group
    stages = steps * FRAMES
    span = times // FRAMES
    blocks = span // UP
    near = feeds // n_chan
    devices = n_chan * n_cyl
    wide = group * UP
    pieces = 4
    fine = jnp.asarray(fine_rows(cyls, 1, UP)[0])
    ns = jnp.asarray(half_rows(feeds))
    operands = (volts, gain_exponents.T, fine, ns)
    dma = pltpu.SemaphoreType.DMA
    out = pl.pallas_call(
        functools.partial(fused_kernel, n_chan, n_cyl),
        out_shape=jax.ShapeDtypeStruct((per * near * devices * stages, wide), jnp.float32),
        in_specs=[pl.BlockSpec(memory_space=pltpu.HBM)] * 4,
        out_specs=pl.BlockSpec(memory_space=pltpu.VMEM),
        scratch_shapes=[
            pltpu.VMEM((n_cyl, stages, group, per, pols, span, inputs), jnp.bfloat16),
            pltpu.VMEM((pols * blocks, 2, cyls, group, UP, feeds), jnp.bfloat16),
            pltpu.VMEM((per, n_cyl, n_chan, near, wide), jnp.bfloat16),
            pltpu.VMEM((stages - 1, n_cyl, n_chan, per, near, wide), jnp.bfloat16),
            pltpu.VMEM((per, devices, near, wide), jnp.bfloat16),
            pltpu.VMEM((stages - 1, devices, per, near, wide), jnp.bfloat16),
            pltpu.VMEM((n_cyl, per, chans), jnp.int32),
            pltpu.VMEM((per, n_cyl, 1, wide), jnp.float32),
            pltpu.VMEM((steps, n_cyl, per, wide), jnp.float32),
            pltpu.VMEM(fine.shape, jnp.bfloat16),
            pltpu.VMEM(ns.shape, jnp.bfloat16),
            dma((stages,)),
            dma((n_cyl,)),
            dma((n_cyl, stages, pieces)),
            dma,
            dma((n_cyl,)),
            dma((n_cyl,)),
            dma((2,)),
            dma,
            dma((per,)),
            dma,
            dma((stages - 1,)),
            pltpu.SemaphoreType.REGULAR,
            pltpu.SemaphoreType.REGULAR,
        ],
        compiler_params=pltpu.CompilerParams(
            collective_id=0, has_side_effects=True, vmem_limit_bytes=48 * 1024 * 1024
        ),
        name="fused",
    )(*[pltpu.with_memory_space_constraint(x, pltpu.HBM) for x in operands])
    out = out.reshape(per, near, devices * steps, FRAMES, wide)
    return jnp.transpose(out, (0, 1, 3, 2, 4)).reshape(per, near, FRAMES, -1)


def fits(n_chan, n_cyl, volts):
    chans, per, pols, times, inputs = volts.shape
    own = chans // n_cyl
    feeds = inputs // 2
    return (
        n_cyl == 2
        and n_chan % 2 == 0
        and per in (1, 2)
        and own % (128 // UP) == 0
        and feeds % (16 * n_chan) == 0
        and feeds % 256 == 0
        and times % (FRAMES * UP) == 0
    )


def local(n_chan, n_cyl, volts, gain_exponents):
    chans, per, pols, times, inputs = volts.shape
    feeds = inputs // 2
    cyls = per * n_cyl
    own = chans // n_cyl
    group = math.gcd(8, own)
    steps = own // group
    wide = group * UP
    blocks = times // UP
    rank = lax.axis_index("cyl")
    gains = [lax.dynamic_slice_in_dim(gain_exponents, rank * own, own, 0)]
    for d in range(1, n_cyl):
        ring = [(k, (k + d) % n_cyl) for k in range(n_cyl)]
        to = (rank + d) % n_cyl
        gains.append(
            lax.ppermute(lax.dynamic_slice_in_dim(gain_exponents, to * own, own, 0), "cyl", ring)
        )
    stacked = jnp.stack(gains)
    order = (rank - jnp.arange(n_cyl, dtype=jnp.int32)) % n_cyl
    exps = jnp.take(stacked, order, axis=0)
    exps = jnp.transpose(exps, (0, 2, 1)).reshape(cyls, steps, group)
    scale = jnp.exp2(2.0 * exps.astype(jnp.float32)) / (pols * (blocks // FRAMES))
    scale = jnp.transpose(jnp.repeat(scale, UP, axis=2), (1, 0, 2))

    fine = jnp.asarray(fine_rows(cyls, n_cyl, UP))
    ns = jnp.asarray(ns_rows(feeds))
    power = pl.pallas_call(
        functools.partial(beam_kernel, cyls, n_cyl),
        out_shape=jax.ShapeDtypeStruct((steps, cyls, FRAMES, feeds, wide), jnp.bfloat16),
        grid=(steps,),
        in_specs=[
            pl.BlockSpec(memory_space=pl.ANY),
            pl.BlockSpec(fine.shape, lambda g: (0, 0, 0)),
            pl.BlockSpec(ns.shape, lambda g: (0, 0)),
            pl.BlockSpec((1, cyls, wide), lambda g: (g, 0, 0)),
        ],
        out_specs=pl.BlockSpec((1, cyls, FRAMES, feeds, wide), lambda g: (g, 0, 0, 0, 0)),
        scratch_shapes=[
            pltpu.VMEM((pols * blocks, cyls, group, UP, inputs), jnp.bfloat16),
            pltpu.VMEM((n_cyl, steps, group, per, pols, times, inputs), jnp.bfloat16),
            pltpu.SemaphoreType.DMA((steps,)),
            pltpu.SemaphoreType.DMA((n_cyl, steps)),
            pltpu.SemaphoreType.DMA((n_cyl, steps)),
        ],
        compiler_params=pltpu.CompilerParams(
            dimension_semantics=("arbitrary",), collective_id=0, has_side_effects=True
        ),
        name="beams",
    )(volts, fine, ns, scale)

    near = feeds // n_chan
    power = power.reshape(steps, n_cyl, per, FRAMES, n_chan, near, wide)
    power = jnp.transpose(power, (4, 1, 2, 3, 0, 5, 6))
    power = power.reshape(n_chan * n_cyl, per, FRAMES, steps, near, wide)
    power = lax.all_to_all(power, ("chan", "cyl"), split_axis=0, concat_axis=0, tiled=True)
    if (steps * wide) % 128 == 0:
        return spread(power)
    power = jnp.transpose(power, (1, 4, 2, 0, 3, 5))
    return power.reshape(per, near, FRAMES, -1).astype(jnp.float32)


def either(n_chan, n_cyl, volts, gain_exponents):
    if fits(n_chan, n_cyl, volts):
        return fused(n_chan, n_cyl, volts, gain_exponents)
    return local(n_chan, n_cyl, volts, gain_exponents)


def solution(mesh):
    return jax.shard_map(
        functools.partial(either, mesh.shape["chan"], mesh.shape["cyl"]),
        mesh=mesh,
        in_specs=(P("chan", "cyl", None, None, None), P("chan", "cyl")),
        out_specs=P("cyl", "chan", None, None),
        check_vma=False,
    )
```

```python
import functools
import math

import jax
import jax.numpy as jnp
import ml_dtypes
import numpy as np
from jax import lax
from jax.experimental import pallas as pl
from jax.experimental.pallas import tpu as pltpu
from jax.sharding import PartitionSpec as P

UP = 16
FRAMES = 2


def ns_rows(feeds):
    index = np.arange(feeds)
    theta = (index[None, :] * (index[:, None] - feeds // 2) % feeds) * (2.0 * math.pi / feeds)
    cosine = np.cos(theta) / math.sqrt(feeds)
    sine = np.sin(theta) / math.sqrt(feeds)
    table = np.concatenate(
        [np.concatenate([cosine, sine], axis=1), np.concatenate([-sine, cosine], axis=1)], axis=0
    )
    return table.astype(ml_dtypes.bfloat16)


def fine_rows(cyls, n_cyl, up):
    index = np.arange(up)
    theta = (index[:, None] * index[None, :] % up) * (2.0 * math.pi / up)
    rounded = lambda x: (x / math.sqrt(up)).astype(ml_dtypes.bfloat16).astype(np.float64)
    fine = rounded(np.cos(theta)) - 1j * rounded(np.sin(theta))
    cyl = np.arange(cyls)
    phase = 2.0 * math.pi * cyl[None, :] * (cyl[:, None] - (cyls - 1) / 2.0) / cyls
    weight = np.exp(-1j * phase) / 2.0
    both = np.einsum("ec,km->emck", weight, fine)
    parts = np.stack(
        [np.stack([both.real, -both.imag], axis=3), np.stack([both.imag, both.real], axis=3)], axis=0
    )
    per = cyls // n_cyl
    tables = []
    for rank in range(n_cyl):
        order = [((rank - d) % n_cyl) * per + c for d in range(n_cyl) for c in range(per)]
        tables.append(parts[:, :, :, order].reshape(2 * cyls * up, cyls * 2 * up))
    return np.stack(tables).astype(ml_dtypes.bfloat16)


def beam_kernel(
    cyls, n_cyl, volts_ref, fine_ref, ns_ref, gain_ref, out_ref,
    mid_ref, held_ref, own_sem, send_sem, recv_sem,
):
    step = pl.program_id(0)
    steps = pl.num_programs(0)
    _, _, group, per, pols, times, inputs = held_ref.shape
    feeds = inputs // 2
    blocks = times // UP
    sums = blocks // FRAMES
    rank = lax.axis_index("cyl")

    def own_copy(g):
        rows = pl.ds((rank * steps + g) * group, group)
        return pltpu.make_async_copy(volts_ref.at[rows], held_ref.at[0, g], own_sem.at[g])

    def far_copy(d, g):
        to = lax.rem(rank + d, n_cyl)
        rows = pl.ds((to * steps + g) * group, group)
        return pltpu.make_async_remote_copy(
            src_ref=volts_ref.at[rows],
            dst_ref=held_ref.at[d, g],
            send_sem=send_sem.at[d, g],
            recv_sem=recv_sem.at[d, g],
            device_id={"cyl": to},
            device_id_type=pl.DeviceIdType.MESH,
        )

    @pl.when(step == 0)
    def _():
        own_copy(0).start()
        barrier = pltpu.get_barrier_semaphore()
        for d in range(1, n_cyl):
            pl.semaphore_signal(
                barrier, inc=1, device_id={"cyl": lax.rem(rank + d, n_cyl)},
                device_id_type=pl.DeviceIdType.MESH,
            )
        pl.semaphore_wait(barrier, n_cyl - 1)

        def start(g, carry):
            for d in range(1, n_cyl):
                far_copy(d, g).start()

            @pl.when(g > 0)
            def _():
                own_copy(g).start()

            return carry

        lax.fori_loop(0, steps, start, 0)

    own_copy(step).wait()
    for d in range(1, n_cyl):
        far_copy(d, step).wait()
    volt_refs = [held_ref.at[d, step] for d in range(n_cyl)]
    fine = fine_ref[rank]

    def one_chan(ch, carry):
        for p in range(pols):
            for j in range(blocks):
                rows = jnp.concatenate(
                    [
                        ref[ch, c, p, j * UP : (j + 1) * UP, r * feeds : (r + 1) * feeds]
                        for ref in volt_refs
                        for c in range(per)
                        for r in range(2)
                    ],
                    axis=0,
                )
                got = jnp.dot(fine, rows, preferred_element_type=jnp.float32).astype(jnp.bfloat16)
                for s in range(2):
                    for e in range(cyls):
                        at = (s * cyls + e) * UP
                        mid_ref[p * blocks + j, e, ch, :, s * feeds : (s + 1) * feeds] = got[at : at + UP]
        return carry

    lax.fori_loop(0, group, one_chan, 0)
    wide = group * UP
    pair = 2 if cyls % 2 == 0 else 1
    ns = ns_ref[...]
    for q in range(FRAMES):
        for e in range(0, cyls, pair):
            total = None
            for p in range(pols):
                for j in range(q * sums, (q + 1) * sums):
                    block = mid_ref[p * blocks + j, e : e + pair].reshape(pair * wide, inputs)
                    spectra = lax.dot_general(
                        ns, block, (((1,), (1,)), ((), ())), preferred_element_type=jnp.float32
                    )
                    squared = spectra * spectra
                    power = squared[:feeds] + squared[feeds:]
                    total = power if total is None else total + power
            for i in range(pair):
                scaled = total[:, i * wide : (i + 1) * wide] * gain_ref[0, e + i : e + i + 1, :]
                out_ref[0, e + i, q] = scaled.astype(jnp.bfloat16)


def spread_kernel(in_ref, out_ref):
    sources, _, frames, steps, near, wide = in_ref.shape

    def one(source, carry):
        at = pl.multiple_of(source * (steps * wide), 128)
        for g in range(steps):
            rows = [in_ref[source, 0, q, g].astype(jnp.float32) for q in range(frames)]
            out_ref[0, :, :, pl.ds(at + g * wide, wide)] = jnp.stack(rows, axis=1)
        return carry

    lax.fori_loop(0, sources, one, 0)


def spread(power):
    sources, per, frames, steps, near, wide = power.shape
    lanes = sources * steps * wide
    return pl.pallas_call(
        spread_kernel,
        out_shape=jax.ShapeDtypeStruct((per, near, frames, lanes), jnp.float32),
        grid=(per,),
        in_specs=[pl.BlockSpec((sources, 1, frames, steps, near, wide), lambda e: (0, e, 0, 0, 0, 0))],
        out_specs=pl.BlockSpec((1, near, frames, lanes), lambda e: (e, 0, 0, 0)),
        compiler_params=pltpu.CompilerParams(dimension_semantics=("arbitrary",)),
        name="spread",
    )(power)


def half_rows(feeds):
    half = feeds // 2
    table = np.asarray(ns_rows(feeds)).reshape(2, half, 2, 2, feeds)[..., :half]
    return np.transpose(table, (2, 0, 1, 3, 4)).reshape(2, feeds, feeds)


def fused_kernel(
    n_chan, n_cyl, volts_ref, gains_ref, fine_hbm, ns_hbm, out_ref,
    held_ref, mid_ref, head_out_ref, send_ref, head_in_ref, recv_ref,
    exps_ref, head_scale_ref, scale_ref, fine_ref, ns_ref,
    own_sem, volt_send_sem, volt_recv_sem, exp_sem, exp_send_sem, exp_recv_sem, table_sem,
    head_send_sem, head_recv_sem, send_sem, recv_sem, pair_sem, go_sem,
):
    chip = lax.axis_index("chan")
    rank = lax.axis_index("cyl")
    me = chip * n_cyl + rank
    devices = n_chan * n_cyl
    _, stages, group, per, pols, times, inputs = held_ref.shape
    pieces = volt_recv_sem.shape[2]
    piece = group // pieces
    blocks = times // UP
    feeds = inputs // 2
    half = feeds // 2
    cyls = per * n_cyl
    steps = stages // FRAMES
    own = steps * group
    wide = group * UP
    near = feeds // n_chan
    share = group // per
    slim = share * UP

    def volt_rows(to, s, first, count):
        at = to * own + (s // FRAMES) * group + first
        time = pl.multiple_of((s % FRAMES) * times, times)
        return volts_ref.at[pl.ds(at, count), :, :, pl.ds(time, times), :]

    def own_copy(s):
        return pltpu.make_async_copy(volt_rows(rank, s, 0, group), held_ref.at[rank, s], own_sem.at[s])

    def far_copy(d, s, i):
        to = lax.rem(rank + d, n_cyl)
        return pltpu.make_async_remote_copy(
            src_ref=volt_rows(to, s, i * piece, piece),
            dst_ref=held_ref.at[rank, s, pl.ds(i * piece, piece)],
            send_sem=volt_send_sem.at[d],
            recv_sem=volt_recv_sem.at[d, s, i],
            device_id={"cyl": to},
            device_id_type=pl.DeviceIdType.MESH,
        )

    def far_arrived(d, s, i):
        source = lax.rem(rank + n_cyl - d, n_cyl)
        there = held_ref.at[source, s, pl.ds(i * piece, piece)]
        return pltpu.make_async_copy(there, there, volt_recv_sem.at[d, s, i])

    def exp_copy(d):
        return pltpu.make_async_remote_copy(
            src_ref=gains_ref,
            dst_ref=exps_ref.at[rank],
            send_sem=exp_send_sem.at[d],
            recv_sem=exp_recv_sem.at[d],
            device_id={"cyl": lax.rem(rank + d, n_cyl)},
            device_id_type=pl.DeviceIdType.MESH,
        )

    fine_copy = pltpu.make_async_copy(fine_hbm, fine_ref, table_sem.at[0])
    ns_copy = pltpu.make_async_copy(ns_hbm, ns_ref, table_sem.at[1])
    own_exps = pltpu.make_async_copy(gains_ref, exps_ref.at[rank], exp_sem)

    barrier = pltpu.get_barrier_semaphore()
    mesh_id = pl.DeviceIdType.MESH

    lead = n_cyl - 1

    @pl.when(rank == lead)
    def _():
        pl.semaphore_signal(barrier, inc=1, device_id={"cyl": 0}, device_id_type=mesh_id)

    @pl.when(rank != lead)
    def _():
        pl.semaphore_signal(barrier, inc=1, device_id={"cyl": lead}, device_id_type=mesh_id)

    def greet(i, carry):
        to = lax.rem(chip + i, n_chan)
        pl.semaphore_signal(barrier, inc=1, device_id={"chan": to, "cyl": lead}, device_id_type=mesh_id)
        return carry

    lax.fori_loop(1, n_chan, greet, 0)
    own_copy(0).start()
    fine_copy.start()
    own_exps.start()
    ns_copy.start()

    @pl.when(rank != lead)
    def _():
        pl.semaphore_wait(barrier, 1)
        pl.semaphore_signal(pair_sem, inc=1, device_id={"cyl": lead}, device_id_type=mesh_id)

    @pl.when(rank == lead)
    def _():
        pl.semaphore_wait(pair_sem, 1)

    def all_here():
        @pl.when(rank == lead)
        def _():
            pl.semaphore_wait(barrier, devices - 1)
            pl.semaphore_signal(go_sem, inc=1, device_id={"cyl": 0}, device_id_type=mesh_id)

        @pl.when(rank != lead)
        def _():
            pl.semaphore_wait(go_sem, 1)

    def start_own(s, carry):
        own_copy(s).start()
        return carry

    def start_far(n, carry):
        for d in range(1, n_cyl):
            far_copy(d, n // pieces, n % pieces).start()
        return carry

    for d in range(1, n_cyl):
        exp_copy(d).start()
    lax.fori_loop(0, pieces, start_far, 0)
    lax.fori_loop(1, stages, start_own, 0)
    lax.fori_loop(pieces, stages * pieces, start_far, 0)
    fine_copy.wait()

    own_exps.wait()
    for d in range(1, n_cyl):
        exp_copy(d).wait()
    chans = exps_ref.shape[2]
    lane = lax.broadcasted_iota(jnp.int32, (chans, own * UP), 1)
    chan = lax.broadcasted_iota(jnp.int32, (chans, own * UP), 0) - rank * own
    exps = jnp.concatenate([exps_ref[i] for i in range(n_cyl)], axis=0).astype(jnp.float32)

    def scale_of(pick):
        spread = jnp.dot(exps, pick.astype(jnp.float32), preferred_element_type=jnp.float32)
        return jnp.exp2(2.0 * spread) / (pols * blocks)

    scale = scale_of(chan == lane // UP)
    for g in range(steps):
        for o in range(n_cyl):
            scale_ref[g, o] = scale[o * per : (o + 1) * per, g * wide : (g + 1) * wide]
    lane, chan = lane[:, :wide], chan[:, :wide]
    for h in range(per):
        scale = scale_of(chan == h * share + lane % slim // UP)
        for o in range(n_cyl):
            row = scale[o * per : o * per + 1]
            for e in range(1, per):
                row = jnp.where(lane[:1] // slim == e, scale[o * per + e : o * per + e + 1], row)
            head_scale_ref[h, o] = row

    def fine_piece(s, i):
        fine = fine_ref[...]
        for d in range(1, n_cyl):
            far_arrived(d, s, i).wait()
        for c0 in range(piece):
            ch = i * piece + c0
            for p in range(pols):
                for j in range(blocks):
                    rows = jnp.concatenate(
                        [
                            held_ref[o, s, ch, c, p, j * UP : (j + 1) * UP, r * feeds : (r + 1) * feeds]
                            for o in range(n_cyl)
                            for c in range(per)
                            for r in range(2)
                        ],
                        axis=0,
                    )
                    got = jnp.dot(fine, rows, preferred_element_type=jnp.float32)
                    low, high = got[:, :half], got[:, half:]
                    both = ((low + high).astype(jnp.bfloat16), (low - high).astype(jnp.bfloat16))
                    for odd in range(2):
                        for r in range(2):
                            for e in range(cyls):
                                at = (r * cyls + e) * UP
                                mid_ref[p * blocks + j, odd, e, ch, :, r * half : (r + 1) * half] = (
                                    both[odd][at : at + UP]
                                )

    def fine_pieces(s, first, last):
        def one(i, carry):
            fine_piece(s, i)
            return carry

        lax.fori_loop(first, last, one, 0)

    def powers(beams, first, count, rows=None):
        parts = []
        for odd in range(2):
            total = None
            if rows is None:
                ns = ns_ref[odd]
            else:
                ns = jnp.concatenate([ns_ref[odd, pl.ds(r * half + rows, half // 2)] for r in range(2)], axis=0)
            kept = ns.shape[0] // 2
            for b in range(pols * blocks):
                block = mid_ref[b, odd, beams, first : first + count]
                spectra = lax.dot_general(
                    ns, block.reshape(-1, feeds), (((1,), (1,)), ((), ())),
                    preferred_element_type=jnp.float32,
                )
                squared = spectra * spectra
                power = squared[:kept] + squared[kept:]
                total = power if total is None else total + power
            parts.append(total)
        return parts

    def by_chip(parts, factor):
        scaled = [(part * factor).reshape(-1, near // 2, wide) for part in parts]
        return jnp.concatenate(scaled, axis=1).astype(jnp.bfloat16)

    def send_to(source_ref, target_ref, out_sem, in_sem, peer):
        owner = lax.rem(peer, n_cyl)
        to = lax.div(peer, n_cyl)
        pltpu.make_async_remote_copy(
            src_ref=source_ref.at[owner, to],
            dst_ref=target_ref.at[me],
            send_sem=out_sem,
            recv_sem=in_sem,
            device_id={"chan": to, "cyl": owner},
            device_id_type=mesh_id,
        ).start()

    def send_ring(base, count, source_ref, target_ref, out_sem, in_sem):
        at = me - base
        for i in range(1, count):
            peer = base + jnp.where(at + i >= count, at + i - count, at + i)
            send_to(source_ref, target_ref, out_sem, in_sem, peer)
        pltpu.make_async_copy(source_ref.at[rank, chip], target_ref.at[me], in_sem).start()

    side = lax.div(chip, n_chan // 2)
    many = devices // 2

    def send_other_side(*refs):
        at = me - side * many
        base = (1 - side) * many
        for i in range(many):
            send_to(*refs, base + jnp.where(at + i >= many, at + i - many, at + i))

    own_copy(0).wait()
    for h in range(per):
        fine_pieces(0, h * share // piece, (h + 1) * share // piece)
        if h == 0:
            ns_copy.wait()
        refs = (head_out_ref.at[h], head_in_ref.at[h], head_send_sem, head_recv_sem.at[h])
        for turn in range(2):
            which = jnp.where(side == turn, 1, 0)
            rows = pl.multiple_of(which * (half // 2), half // 2)
            parts = powers(pl.ds(0, cyls), h * share, share, rows)
            for o in range(n_cyl):
                head_out_ref[h, o, pl.ds(which * (n_chan // 2), n_chan // 2)] = by_chip(
                    [part[:, o * wide : (o + 1) * wide] for part in parts], head_scale_ref[h, o]
                )
            if turn == 0:
                if h == 0:
                    all_here()
                send_other_side(*refs)
            else:
                send_ring(side * many, many, *refs)

    def one_stage(s, carry):
        own_copy(s).wait()
        fine_pieces(s, 0, pieces)

        def one_owner(owner, inner):
            parts = powers(pl.ds(owner * per, per), 0, group)
            for e in range(per):
                send_ref[s - 1, owner, :, e] = by_chip(
                    [part[:, e * wide : (e + 1) * wide] for part in parts],
                    scale_ref[s // FRAMES, owner, e : e + 1, :],
                )
            return inner

        lax.fori_loop(0, n_cyl, one_owner, 0)
        send_ring(0, devices, send_ref.at[s - 1], recv_ref.at[s - 1], send_sem, recv_sem.at[s - 1, side])
        return carry

    lax.fori_loop(1, stages, one_stage, 0)

    depth = devices * stages

    several = math.gcd(4, many)

    def place(s, source, e, tile):
        row = (source * steps + s // FRAMES) * FRAMES + s % FRAMES
        for odd in range(2):
            at = (e * near + odd) * depth + row
            out_ref[pl.ds(at, near // 2, 2 * depth), :] = tile[odd * (near // 2) : (odd + 1) * (near // 2)]

    for h in range(per):
        pltpu.make_async_copy(head_in_ref.at[h], head_in_ref.at[h], head_recv_sem.at[h]).wait()
    slot = lax.broadcasted_iota(jnp.int32, (near, wide), 1) // slim

    def spread_head(source, carry):
        tiles = [head_in_ref[h, source].astype(jnp.float32) for h in range(per)]
        for e in range(per):
            tile = tiles[e]
            for h in range(per):
                if h != e:
                    moved = pltpu.roll(tiles[h], (h - e) * slim % wide, 1)
                    tile = jnp.where(slot == h, moved, tile)
            place(0, source, e, tile)
        return carry

    lax.fori_loop(0, devices, spread_head, 0)

    def spread_side(turn, carry):
        s = 1 + turn // 2
        which = lax.rem(side + turn, 2)
        arrived = recv_ref.at[s - 1, pl.ds(which * many, many)]
        pltpu.make_async_copy(arrived, arrived, recv_sem.at[s - 1, which]).wait()

        def some(n, inner):
            for k in range(several):
                for e in range(per):
                    source = which * many + n * several + k
                    place(s, source, e, recv_ref[s - 1, source, e].astype(jnp.float32))
            return inner

        lax.fori_loop(0, many // several, some, 0)
        return carry

    lax.fori_loop(0, 2 * (stages - 1), spread_side, 0)
    for ref, sem in ((head_in_ref, head_send_sem), (recv_ref, send_sem)):
        sent = ref.at[:, : devices - 1]
        pltpu.make_async_copy(sent, sent, sem).wait()
    for d in range(1, n_cyl):
        pltpu.make_async_copy(held_ref.at[0], held_ref.at[0], volt_send_sem.at[d]).wait()


def fused(n_chan, n_cyl, volts, gain_exponents):
    chans, per, pols, times, inputs = volts.shape
    feeds = inputs // 2
    cyls = per * n_cyl
    own = chans // n_cyl
    group = 128 // UP
    steps = own // group
    stages = steps * FRAMES
    span = times // FRAMES
    blocks = span // UP
    near = feeds // n_chan
    devices = n_chan * n_cyl
    wide = group * UP
    pieces = 4
    fine = jnp.asarray(fine_rows(cyls, 1, UP)[0])
    ns = jnp.asarray(half_rows(feeds))
    operands = (volts, gain_exponents.T, fine, ns)
    dma = pltpu.SemaphoreType.DMA
    out = pl.pallas_call(
        functools.partial(fused_kernel, n_chan, n_cyl),
        out_shape=jax.ShapeDtypeStruct((per * near * devices * stages, wide), jnp.float32),
        in_specs=[pl.BlockSpec(memory_space=pltpu.HBM)] * 4,
        out_specs=pl.BlockSpec(memory_space=pltpu.VMEM),
        scratch_shapes=[
            pltpu.VMEM((n_cyl, stages, group, per, pols, span, inputs), jnp.bfloat16),
            pltpu.VMEM((pols * blocks, 2, cyls, group, UP, feeds), jnp.bfloat16),
            pltpu.VMEM((per, n_cyl, n_chan, near, wide), jnp.bfloat16),
            pltpu.VMEM((stages - 1, n_cyl, n_chan, per, near, wide), jnp.bfloat16),
            pltpu.VMEM((per, devices, near, wide), jnp.bfloat16),
            pltpu.VMEM((stages - 1, devices, per, near, wide), jnp.bfloat16),
            pltpu.VMEM((n_cyl, per, chans), jnp.int32),
            pltpu.VMEM((per, n_cyl, 1, wide), jnp.float32),
            pltpu.VMEM((steps, n_cyl, per, wide), jnp.float32),
            pltpu.VMEM(fine.shape, jnp.bfloat16),
            pltpu.VMEM(ns.shape, jnp.bfloat16),
            dma((stages,)),
            dma((n_cyl,)),
            dma((n_cyl, stages, pieces)),
            dma,
            dma((n_cyl,)),
            dma((n_cyl,)),
            dma((2,)),
            dma,
            dma((per,)),
            dma,
            dma((stages - 1, 2)),
            pltpu.SemaphoreType.REGULAR,
            pltpu.SemaphoreType.REGULAR,
        ],
        compiler_params=pltpu.CompilerParams(
            collective_id=0, has_side_effects=True, vmem_limit_bytes=48 * 1024 * 1024
        ),
        name="fused",
    )(*[pltpu.with_memory_space_constraint(x, pltpu.HBM) for x in operands])
    out = out.reshape(per, near, devices * steps, FRAMES, wide)
    return jnp.transpose(out, (0, 1, 3, 2, 4)).reshape(per, near, FRAMES, -1)


def fits(n_chan, n_cyl, volts):
    chans, per, pols, times, inputs = volts.shape
    own = chans // n_cyl
    feeds = inputs // 2
    return (
        n_cyl == 2
        and n_chan % 2 == 0
        and per in (1, 2)
        and own % (128 // UP) == 0
        and feeds % (16 * n_chan) == 0
        and feeds % 256 == 0
        and times % (FRAMES * UP) == 0
    )


def local(n_chan, n_cyl, volts, gain_exponents):
    chans, per, pols, times, inputs = volts.shape
    feeds = inputs // 2
    cyls = per * n_cyl
    own = chans // n_cyl
    group = math.gcd(8, own)
    steps = own // group
    wide = group * UP
    blocks = times // UP
    rank = lax.axis_index("cyl")
    gains = [lax.dynamic_slice_in_dim(gain_exponents, rank * own, own, 0)]
    for d in range(1, n_cyl):
        ring = [(k, (k + d) % n_cyl) for k in range(n_cyl)]
        to = (rank + d) % n_cyl
        gains.append(
            lax.ppermute(lax.dynamic_slice_in_dim(gain_exponents, to * own, own, 0), "cyl", ring)
        )
    stacked = jnp.stack(gains)
    order = (rank - jnp.arange(n_cyl, dtype=jnp.int32)) % n_cyl
    exps = jnp.take(stacked, order, axis=0)
    exps = jnp.transpose(exps, (0, 2, 1)).reshape(cyls, steps, group)
    scale = jnp.exp2(2.0 * exps.astype(jnp.float32)) / (pols * (blocks // FRAMES))
    scale = jnp.transpose(jnp.repeat(scale, UP, axis=2), (1, 0, 2))

    fine = jnp.asarray(fine_rows(cyls, n_cyl, UP))
    ns = jnp.asarray(ns_rows(feeds))
    power = pl.pallas_call(
        functools.partial(beam_kernel, cyls, n_cyl),
        out_shape=jax.ShapeDtypeStruct((steps, cyls, FRAMES, feeds, wide), jnp.bfloat16),
        grid=(steps,),
        in_specs=[
            pl.BlockSpec(memory_space=pl.ANY),
            pl.BlockSpec(fine.shape, lambda g: (0, 0, 0)),
            pl.BlockSpec(ns.shape, lambda g: (0, 0)),
            pl.BlockSpec((1, cyls, wide), lambda g: (g, 0, 0)),
        ],
        out_specs=pl.BlockSpec((1, cyls, FRAMES, feeds, wide), lambda g: (g, 0, 0, 0, 0)),
        scratch_shapes=[
            pltpu.VMEM((pols * blocks, cyls, group, UP, inputs), jnp.bfloat16),
            pltpu.VMEM((n_cyl, steps, group, per, pols, times, inputs), jnp.bfloat16),
            pltpu.SemaphoreType.DMA((steps,)),
            pltpu.SemaphoreType.DMA((n_cyl, steps)),
            pltpu.SemaphoreType.DMA((n_cyl, steps)),
        ],
        compiler_params=pltpu.CompilerParams(
            dimension_semantics=("arbitrary",), collective_id=0, has_side_effects=True
        ),
        name="beams",
    )(volts, fine, ns, scale)

    near = feeds // n_chan
    power = power.reshape(steps, n_cyl, per, FRAMES, n_chan, near, wide)
    power = jnp.transpose(power, (4, 1, 2, 3, 0, 5, 6))
    power = power.reshape(n_chan * n_cyl, per, FRAMES, steps, near, wide)
    power = lax.all_to_all(power, ("chan", "cyl"), split_axis=0, concat_axis=0, tiled=True)
    if (steps * wide) % 128 == 0:
        return spread(power)
    power = jnp.transpose(power, (1, 4, 2, 0, 3, 5))
    return power.reshape(per, near, FRAMES, -1).astype(jnp.float32)


def either(n_chan, n_cyl, volts, gain_exponents):
    if fits(n_chan, n_cyl, volts):
        return fused(n_chan, n_cyl, volts, gain_exponents)
    return local(n_chan, n_cyl, volts, gain_exponents)


def solution(mesh):
    return jax.shard_map(
        functools.partial(either, mesh.shape["chan"], mesh.shape["cyl"]),
        mesh=mesh,
        in_specs=(P("chan", "cyl", None, None, None), P("chan", "cyl")),
        out_specs=P("cyl", "chan", None, None),
        check_vma=False,
    )
```
